32 devices in a mesh: section: 2 (over x), dp: 16 (over z, y, core).
Axes of the slice: x: 2, y: 2, z: 4, core: 2. Of those that a mesh axis runs over, the one named last changes fastest.
Arguments:
- edge_data: bfloat16 [2, 2, 1024, 960], P('section', None, 'dp'), may hold values from -6 to 6
- segment_ids: int32 [2, 1024], P(None, 'dp'), may hold values from 0 to 63, as said below
- attn_weight: bfloat16 [2, 960, 2560], P('section', None, 'dp'), may hold values from -0.1875 to 0.1875
- ffn_weight: bfloat16 [2, 3, 960, 2560], P('section', None, None, 'dp'), may hold values from -0.1875 to 0.1875
- gains: bfloat16 [2, 1920], P('section', 'dp'), may hold values from 0.5 to 1.5
Outputs:
- edge_out: bfloat16 [2, 2, 1024, 960], P('section', None, 'dp')
- attention_grad: float32 [2, 960, 2560], P('section', None, 'dp')
- ffn_grad: float32 [2, 3, 960, 2560], P('section', None, None, 'dp')
- gain_grad: float32 [2, 1920], P('section', 'dp')
The draws below stay inside these ranges and needn't reach their ends.
Inputs may be any that keep to these rules, and one draw needn't show every extreme that they name: `segment_ids`: inside each aligned block of 64 tokens (one index of dp in one micro-batch) the ids start at 0 at the block's first token and rise by 0 or 1 from token to token; tokens of a block with equal ids form one sequence; no sequence crosses a block; some sequence fills a whole block, and some block holds only sequences of one token.
All inputs are finite; a program needn't handle non-finite values.
Results may differ from the reference program's by a relative error of at most 0.02.
Values may be sent and summed in bfloat16 or wider, within the bound.
No kernel may reach another device: no remote copies, remote signals or barrier semaphores. Data moves between devices by JAX's collectives and lax.ppermute only.
A program may use at most 256 MiB of HBM per device.

```python
import jax
import jax.numpy as jnp
from jax import lax

D = 960
QUERY_HEADS = 15
KEY_VALUE_HEADS = 5
HEAD_SIZE = 64
FF = 2560
ATTN_COLS = 2560
MB = 2
TOK_DEV = 64
TOKENS = 1024
N_DP = 16


def draw_segment_ids(key, part):
    block_count = TOKENS // TOK_DEV
    rate_key, flag_key = jax.random.split(key)
    span_table = jnp.array([1, 2, 4, 8, 16, 32], dtype=jnp.int32)
    rate_pick = jax.random.randint(rate_key, (MB, block_count, 1), 0, 6)
    start_odds = span_table[rate_pick]
    draw_values = jax.random.randint(flag_key, (MB, block_count, TOK_DEV), 0, 64)
    position = jnp.arange(TOK_DEV, dtype=jnp.int32)
    start_flags = (draw_values < start_odds) | (position == 0)
    block_number = jnp.arange(MB * block_count, dtype=jnp.int32).reshape(MB, block_count, 1)
    start_flags = start_flags & ((block_number > 0) | (position == 0))
    start_flags = start_flags | (block_number == MB * block_count - 1)
    segment_out = jnp.cumsum(start_flags.astype(jnp.int32), axis=-1) - 1
    return segment_out.reshape(MB, TOKENS)


def steps_of(rng, shape, cuts, smallest, high):
    level = 1.0
    for dim, parts in cuts:
        heights = jax.random.uniform(jax.random.fold_in(jax.random.fold_in(rng, 6), dim), (parts,), jnp.float32, smallest / len(cuts), high / len(cuts))
        level = level * jnp.repeat(jnp.exp(heights), shape[dim] // parts).reshape((-1,) + (1,) * (len(shape) - 1 - dim))
    return level


def centred(key, shape, scale, reach, cuts=(), kind=jnp.bfloat16):
    values = scale * jax.random.normal(key, shape, jnp.float32)
    if cuts:
        values = values * steps_of(key, shape, cuts, -0.22, 0.18)
    return jnp.clip(values, -reach, reach).astype(kind)


def setup_inputs(seed: int = 0) -> dict:
    streams_of = jax.random.split(jax.random.key(seed), 6)
    return {
        "edge_data": centred(streams_of[0], (2, MB, TOKENS, D), 1.0, 6.0, ((0, 2), (2, 16))),
        "segment_ids": draw_segment_ids(jax.random.fold_in(streams_of[5], 71), 0),
        "attn_weight": centred(streams_of[2], (2, D, ATTN_COLS), D ** -0.5, 0.1875, ((0, 2), (2, 16))),
        "ffn_weight": centred(streams_of[3], (2, 3, D, FF), D ** -0.5, 0.1875, ((0, 2), (3, 16))),
        "gains": jnp.clip(1.0 + 0.1 * jax.random.normal(streams_of[4], (2, 2 * D), jnp.float32), 0.5, 1.5).astype(jnp.bfloat16),
    }


@jax.custom_vjp
def lower_half(v):
    return lax.optimization_barrier(v.astype(jnp.bfloat16)).astype(jnp.float32)

@jax.custom_vjp
def low_back(v):
    return v

def low_keep(v):
    return (lower_half(v), None)

def low_pass(kept, grad):
    return (grad,)

def back_keep(v):
    return (v, None)

def back_low(kept, grad):
    return (lower_half(grad),)
lower_half.defvjp(low_keep, low_pass)
low_back.defvjp(back_keep, back_low)
highest = lax.Precision.HIGHEST
epsilon = 1e-05
theta_base = 100000.0

def norm_rows(rows, gain):
    return rows * lax.rsqrt(lax.optimization_barrier(jnp.mean(rows * rows, axis=-1, keepdims=True)) + epsilon) * gain

def rotary_apply(rows, cosine_table, sine_values):
    half_size = rows.shape[-1] // 2
    front_part = rows[..., :half_size]
    back_part = rows[..., half_size:]
    return jnp.concatenate([front_part * cosine_table - back_part * sine_values, back_part * cosine_table + front_part * sine_values], axis=-1)

def block_tables(segments):
    block_len = segments.shape[-1]
    offsets = jnp.arange(block_len, dtype=jnp.int32)
    same_segment = segments[..., :, None] == segments[..., None, :]
    segment_start = lax.optimization_barrier(jnp.min(jnp.where(same_segment, offsets, block_len), axis=-1))
    positions = (offsets - segment_start).astype(jnp.float32)
    half_size = HEAD_SIZE // 2
    frequency = theta_base ** (-(2.0 * jnp.arange(half_size, dtype=jnp.float32)) / HEAD_SIZE)
    angles = positions[..., None] * frequency
    allowed = same_segment & (offsets[:, None] >= offsets[None, :])
    return (jnp.cos(angles), jnp.sin(angles), allowed)

def layer(inputs, attn_w, ffn_w, gain_row, cosine_table, sine_values, allowed):
    batch_rows_count, sequence_length, model_width = inputs.shape
    head_column_width = QUERY_HEADS * HEAD_SIZE
    key_value_width = KEY_VALUE_HEADS * HEAD_SIZE
    query_group_count = QUERY_HEADS // KEY_VALUE_HEADS
    score_scale = HEAD_SIZE ** (-0.5)
    split_at = head_column_width + 2 * key_value_width
    normed = lower_half(norm_rows(inputs, gain_row[:model_width]))
    projected_rows = low_back(jnp.einsum('btd,dc->btc', normed, attn_w[:, :split_at], precision=highest))
    query_matrix = lower_half(rotary_apply(projected_rows[..., :head_column_width].reshape(batch_rows_count, sequence_length, KEY_VALUE_HEADS, query_group_count, HEAD_SIZE), cosine_table[:, :, None, None, :], sine_values[:, :, None, None, :]))
    key_matrix_rows = lower_half(rotary_apply(projected_rows[..., head_column_width:head_column_width + key_value_width].reshape(batch_rows_count, sequence_length, KEY_VALUE_HEADS, HEAD_SIZE), cosine_table[:, :, None, :], sine_values[:, :, None, :]))
    value_matrix_rows = lower_half(projected_rows[..., head_column_width + key_value_width:].reshape(batch_rows_count, sequence_length, KEY_VALUE_HEADS, HEAD_SIZE))
    scores = low_back(score_scale * jnp.einsum('btgrd,bugd->bgrtu', query_matrix, key_matrix_rows, precision=highest))
    masked = jnp.where(allowed[:, None, None], scores, -1000000000.0)
    prob_low = lower_half(jax.nn.softmax(masked, axis=-1))
    attended = jnp.einsum('bgrtu,bugd->btgrd', prob_low, value_matrix_rows, precision=highest).reshape(batch_rows_count, sequence_length, head_column_width)
    attended = low_back(lower_half(attended))
    branch_out = low_back(jnp.einsum('bti,di->btd', attended, attn_w[:, split_at:], precision=highest))
    hidden = inputs + branch_out
    normed_two = lower_half(norm_rows(hidden, gain_row[model_width:]))
    gate_proj = low_back(jnp.einsum('btd,df->btf', normed_two, ffn_w[0], precision=highest))
    upward = low_back(jnp.einsum('btd,df->btf', normed_two, ffn_w[1], precision=highest))
    active = lower_half(jax.nn.silu(gate_proj) * upward)
    return hidden + low_back(jnp.einsum('btf,df->btd', active, ffn_w[2], precision=highest))

def reference(edge_data, segment_ids, attn_weight, ffn_weight, gains):
    block_count = MB * N_DP
    inputs = edge_data[0].astype(jnp.float32).reshape(block_count, TOK_DEV, D)
    cotangent = edge_data[1].astype(jnp.float32).reshape(block_count, TOK_DEV, D)
    cosine_table, sine_values, allowed = block_tables(segment_ids.reshape(block_count, TOK_DEV))

    def forward(first_in, attn_all, ffn_all, gain_all):
        middle = low_back(lower_half(layer(first_in, attn_all[0], ffn_all[0], gain_all[0], cosine_table, sine_values, allowed)))
        return layer(middle, attn_all[1], ffn_all[1], gain_all[1], cosine_table, sine_values, allowed)
    result, pullback = jax.vjp(forward, inputs, attn_weight.astype(jnp.float32), ffn_weight.astype(jnp.float32), gains.astype(jnp.float32))
    input_grad, attention_grad, ffn_grad, gain_grad = pullback(cotangent)
    edge_out = jnp.stack([input_grad.reshape(MB, TOKENS, D), result.reshape(MB, TOKENS, D)]).astype(jnp.bfloat16)
    return (edge_out, attention_grad, ffn_grad, gain_grad)
```

```python
import jax
import jax.numpy as jnp
from jax import lax
from jax.sharding import PartitionSpec as P

QUERY_HEADS = 15
KEY_VALUE_HEADS = 5
HEAD_SIZE = 64
GROUP = QUERY_HEADS // KEY_VALUE_HEADS
Q_COLS = QUERY_HEADS * HEAD_SIZE
KV_COLS = KEY_VALUE_HEADS * HEAD_SIZE
QKV_COLS = Q_COLS + 2 * KV_COLS

epsilon = 1e-05
theta_base = 100000.0
bf16 = jnp.bfloat16
f32 = jnp.float32


def dot_nn(a, b):
    return lax.dot_general(a, b, (((1,), (0,)), ((), ())), preferred_element_type=f32)


def dot_nt(a, b):
    return lax.dot_general(a, b, (((1,), (1,)), ((), ())), preferred_element_type=f32)


def rope(rows, cosine, sine):
    half = rows.shape[-1] // 2
    a, b = rows[..., :half], rows[..., half:]
    return jnp.concatenate([a * cosine - b * sine, b * cosine + a * sine], axis=-1)


def block_tables(segments):
    micro, block_len = segments.shape
    offsets = jnp.arange(block_len, dtype=jnp.int32)
    same = segments[:, :, None] == segments[:, None, :]
    start = jnp.min(jnp.where(same, offsets, block_len), axis=-1)
    positions = (offsets - start).astype(f32).reshape(-1)
    half = HEAD_SIZE // 2
    frequency = theta_base ** (-(2.0 * jnp.arange(half, dtype=f32)) / HEAD_SIZE)
    angles = positions[:, None] * frequency
    allowed = same & (offsets[:, None] >= offsets[None, :])
    eye = jnp.eye(micro, dtype=bool)
    full = allowed[:, :, None, :] & eye[:, None, :, None]
    total = micro * block_len
    return jnp.cos(angles), jnp.sin(angles), full.reshape(total, total)


def scores_of(q, k, allowed):
    s = jnp.einsum("tgrd,ugd->grtu", q, k, preferred_element_type=f32) * HEAD_SIZE**-0.5
    return jnp.where(allowed, s, -1000000000.0)


def forward(u, weights, tables):
    qkv_w, out_w, gate_w, up_w, down_w, gain_one, gain_two = weights
    cosine, sine, allowed = tables
    tokens = u.shape[0]
    u = u.astype(f32)
    r1 = lax.rsqrt(jnp.mean(u * u, axis=-1, keepdims=True) + epsilon)
    n = (u * r1 * gain_one).astype(bf16)
    proj = dot_nt(n, qkv_w)
    q = rope(
        proj[:, :Q_COLS].reshape(tokens, KEY_VALUE_HEADS, GROUP, HEAD_SIZE),
        cosine[:, None, None, :],
        sine[:, None, None, :],
    ).astype(bf16)
    k = rope(
        proj[:, Q_COLS : Q_COLS + KV_COLS].reshape(tokens, KEY_VALUE_HEADS, HEAD_SIZE),
        cosine[:, None, :],
        sine[:, None, :],
    ).astype(bf16)
    v = proj[:, Q_COLS + KV_COLS :].reshape(tokens, KEY_VALUE_HEADS, HEAD_SIZE).astype(bf16)
    masked = scores_of(q, k, allowed)
    peak = jnp.max(masked, axis=-1, keepdims=True)
    lse = peak + jnp.log(jnp.sum(jnp.exp(masked - peak), axis=-1, keepdims=True))
    prob = jnp.exp(masked - lse).astype(bf16)
    o = jnp.einsum("grtu,ugd->tgrd", prob, v, preferred_element_type=f32)
    o = o.reshape(tokens, Q_COLS).astype(bf16)
    h1 = u + dot_nn(o, out_w)
    r2 = lax.rsqrt(jnp.mean(h1 * h1, axis=-1, keepdims=True) + epsilon)
    m = (h1 * r2 * gain_two).astype(bf16)
    gate = dot_nt(m, gate_w)
    up = dot_nt(m, up_w)
    act = (jax.nn.silu(gate) * up).astype(bf16)
    out = h1 + dot_nn(act, down_w)
    return out, (u, r1, n, q, k, v, lse, o, h1, r2, m, gate, up, act)


def norm_back(grad, rows, r, gain):
    scaled = grad * gain
    part = r * scaled - rows * (r * r * r) * jnp.mean(scaled * rows, axis=-1, keepdims=True)
    return part, jnp.sum(grad * rows * r, axis=0)


def backward(e, state, weights, tables):
    qkv_w, out_w, gate_w, up_w, down_w, gain_one, gain_two = weights
    cosine, sine, allowed = tables
    u, r1, n, q, k, v, lse, o, h1, r2, m, gate, up, act = state
    tokens = u.shape[0]
    eb = e.astype(bf16)
    e = e.astype(f32)
    da = dot_nt(eb, down_w)
    sig = jax.nn.sigmoid(gate)
    dgate = (da * up * sig * (1.0 + gate * (1.0 - sig))).astype(bf16)
    dup = (da * gate * sig).astype(bf16)
    dm = dot_nn(dgate, gate_w) + dot_nn(dup, up_w)
    part, gain_two_grad = norm_back(dm, h1, r2, gain_two)
    dh1 = e + part
    dz = dh1.astype(bf16)
    do = dot_nt(dz, out_w).reshape(tokens, KEY_VALUE_HEADS, GROUP, HEAD_SIZE).astype(bf16)
    prob = jnp.exp(scores_of(q, k, allowed) - lse)
    dv = jnp.einsum("grtu,tgrd->ugd", prob.astype(bf16), do, preferred_element_type=f32)
    dp = jnp.einsum("tgrd,ugd->grtu", do, v, preferred_element_type=f32)
    ds = (prob * (dp - jnp.sum(dp * prob, axis=-1, keepdims=True))).astype(bf16)
    dq = jnp.einsum("grtu,ugd->tgrd", ds, k, preferred_element_type=f32) * HEAD_SIZE**-0.5
    dk = jnp.einsum("grtu,tgrd->ugd", ds, q, preferred_element_type=f32) * HEAD_SIZE**-0.5
    dq = rope(dq, cosine[:, None, None, :], -sine[:, None, None, :])
    dk = rope(dk, cosine[:, None, :], -sine[:, None, :])
    dproj = jnp.concatenate(
        [dq.reshape(tokens, Q_COLS), dk.reshape(tokens, KV_COLS), dv.reshape(tokens, KV_COLS)],
        axis=1,
    ).astype(bf16)
    dn = dot_nn(dproj, qkv_w)
    part, gain_one_grad = norm_back(dn, u, r1, gain_one)
    du = dh1 + part
    gain_grad = jnp.concatenate([gain_one_grad, gain_two_grad])
    return du, (n, dproj, o, dz, m, dgate, dup, eb, act), gain_grad


def flip(x, bit):
    size = lax.axis_size("dp")
    return lax.ppermute(x, "dp", [(i, i ^ bit) for i in range(size)])


def gather_small(row):
    size = lax.axis_size("dp")
    me = lax.axis_index("dp")
    bit = 1
    while bit < size:
        other = flip(row, bit)
        high = (me & bit) != 0
        row = jnp.concatenate([jnp.where(high, other, row), jnp.where(high, row, other)])
        bit *= 2
    return row


def scatter_small(row):
    size = lax.axis_size("dp")
    me = lax.axis_index("dp")
    bit = size // 2
    while bit >= 1:
        half = row.shape[0] // 2
        low, top = row[:half], row[half:]
        high = (me & bit) != 0
        row = jnp.where(high, top, low) + flip(jnp.where(high, low, top), bit)
        bit //= 2
    return row


def grads_generic(pieces):
    n, dproj, o, dz, m, dgate, dup, eb, act = pieces
    attn = jnp.concatenate([dot_nn(dproj.T, n), dot_nn(o.T, dz)], axis=0)
    both = [
        lax.psum_scatter(g, "dp", scatter_dimension=0, tiled=True)
        for g in (attn, dot_nn(dgate.T, m), dot_nn(dup.T, m), dot_nn(act.T, eb))
    ]
    return both[0], jnp.stack(both[1:])


def plane_rows(x, y_bit, core_bit):
    x = jnp.concatenate([x, flip(x, y_bit)], axis=0)
    return jnp.concatenate([x, flip(x, core_bit)], axis=0)


def plane_cols(cols, y, core, y_bit, core_bit):
    keep = lax.dynamic_index_in_dim(cols, y, 2, keepdims=False)
    send = lax.dynamic_index_in_dim(cols, 1 - y, 2, keepdims=False)
    cols = jnp.concatenate([keep, flip(send, y_bit)], axis=-1)
    keep = lax.dynamic_index_in_dim(cols, core, 2, keepdims=False)
    send = lax.dynamic_index_in_dim(cols, 1 - core, 2, keepdims=False)
    return jnp.concatenate([keep, flip(send, core_bit)], axis=-1)


def line_sum(parts, z):
    def shift(x, pairs):
        return lax.ppermute(x, "dp", [(4 * a + i, 4 * b + i) for a, b in pairs for i in range(4)])

    def pick(indices):
        return lax.dynamic_index_in_dim(parts, jnp.array(indices, jnp.int32)[z], 0, keepdims=False)

    def plus(x, recv):
        return (x.astype(f32) + recv.astype(f32)).astype(bf16)

    first = pick([3, 3, 0, 0])
    right = shift(first, [(0, 1)])
    left = shift(first, [(3, 2)])
    send_right = plus(pick([2, 3, 3, 3]), right)
    send_left = plus(pick([0, 0, 0, 1]), left)
    right = shift(send_right, [(0, 1), (1, 2)])
    left = shift(send_left, [(3, 2), (2, 1)])
    send_right = plus(pick([1, 2, 3, 3]), right)
    send_left = plus(pick([0, 0, 1, 2]), left)
    right = shift(send_right, [(0, 1), (1, 2), (2, 3)])
    left = shift(send_left, [(3, 2), (2, 1), (1, 0)])
    own = lax.dynamic_index_in_dim(parts, z, 0, keepdims=False)
    return own.astype(f32) + right.astype(f32) + left.astype(f32)


def grads_planes(pieces):
    n, dproj, o, dz, m, dgate, dup, eb, act = pieces
    me = lax.axis_index("dp")
    z, y, core = me // 4, (me // 2) % 2, me % 2
    y_bit, core_bit = 2, 1
    tokens = n.shape[0]
    share = act.shape[1] // 16
    m_all = plane_rows(m, y_bit, core_bit)
    eb_all = plane_rows(eb, y_bit, core_bit)
    n_all = plane_rows(n, y_bit, core_bit)

    def cols(*arrays):
        stacked = jnp.stack([a.T.reshape(4, 2, 2, share, tokens) for a in arrays])
        return plane_cols(stacked, y, core, y_bit, core_bit)

    act_c = cols(act)
    gu_c = cols(dgate, dup)
    dz_all = plane_rows(dz, y_bit, core_bit)
    attn_c = cols(jnp.concatenate([dproj, o], axis=1))
    wide = 4 * tokens
    down = dot_nn(act_c.reshape(4 * share, wide), eb_all)
    gate_up = dot_nn(gu_c.reshape(8 * share, wide), m_all).reshape(2, 4, share, -1)
    ffn = jnp.concatenate([gate_up, down.reshape(1, 4, share, -1)], axis=0).astype(bf16)
    ffn = ffn.transpose(1, 0, 2, 3).reshape(4, 3 * share, -1)
    ffn_total = line_sum(ffn, z)
    owners = jnp.arange(4, dtype=jnp.int32) * 4 + y * 2 + core
    is_qkv = owners * share < QKV_COLS
    from_n = dot_nn(attn_c.reshape(4 * share, wide), n_all).reshape(4, share, -1)
    from_dz = dot_nn(attn_c.reshape(4 * share, wide), dz_all).reshape(4, share, -1)
    attn = jnp.where(is_qkv[:, None, None], from_n, from_dz).astype(bf16)
    attn_total = line_sum(attn, z)
    return attn_total, ffn_total.reshape(3, share, -1)


def local(edge_data, segment_ids, attn_weight, ffn_weight, gains):
    micro = segment_ids.shape[0]
    leading = lax.axis_index("section") == 0
    tables = block_tables(segment_ids)
    block, width = edge_data.shape[2], edge_data.shape[3]
    x = edge_data[0].reshape(micro * block, width)
    attn_t = lax.all_gather(attn_weight[0].T, "dp", axis=0, tiled=True)
    ffn_t = lax.all_gather(ffn_weight[0].swapaxes(1, 2), "dp", axis=1, tiled=True)
    gain_row = gather_small(gains[0]).astype(f32)
    weights = (
        attn_t[:QKV_COLS],
        attn_t[QKV_COLS:],
        ffn_t[0],
        ffn_t[1],
        ffn_t[2],
        gain_row[:width],
        gain_row[width:],
    )
    first, _ = forward(x, weights, tables)
    received = lax.ppermute(first.astype(bf16), "section", [(0, 1)])
    u = jnp.where(leading, x, received)
    out, state = forward(u, weights, tables)
    first_grad, _, _ = backward(x, state, weights, tables)
    received = lax.ppermute(first_grad.astype(bf16), "section", [(1, 0)])
    e = jnp.where(leading, received, x)
    du, pieces, gain_grad = backward(e, state, weights, tables)
    if lax.axis_size("dp") == 16:
        attn_rows, ffn_rows = grads_planes(pieces)
    else:
        attn_rows, ffn_rows = grads_generic(pieces)
    gain_shard = scatter_small(gain_grad)
    edge_out = jnp.where(leading, du, out).astype(bf16).reshape(micro, block, width)
    return (
        edge_out[None],
        attn_rows.T[None],
        ffn_rows.swapaxes(1, 2)[None],
        gain_shard[None],
    )


def solution(mesh):
    in_specs = (
        P("section", None, "dp", None),
        P(None, "dp"),
        P("section", None, "dp"),
        P("section", None, None, "dp"),
        P("section", "dp"),
    )
    out_specs = (
        P("section", None, "dp", None),
        P("section", None, "dp"),
        P("section", None, None, "dp"),
        P("section", "dp"),
    )
    return jax.shard_map(local, mesh=mesh, in_specs=in_specs, out_specs=out_specs, check_vma=False)
```

```python
import jax
import jax.numpy as jnp
from jax import lax
from jax.sharding import PartitionSpec as P

QUERY_HEADS = 15
KEY_VALUE_HEADS = 5
HEAD_SIZE = 64
GROUP = QUERY_HEADS // KEY_VALUE_HEADS
Q_COLS = QUERY_HEADS * HEAD_SIZE
KV_COLS = KEY_VALUE_HEADS * HEAD_SIZE
QKV_COLS = Q_COLS + 2 * KV_COLS

epsilon = 1e-05
theta_base = 100000.0
Z2_BIT, Z1_BIT, Y_BIT, CORE_BIT = 8, 4, 2, 1
bf16 = jnp.bfloat16
f32 = jnp.float32


def dot_nn(a, b):
    return lax.dot_general(a, b, (((1,), (0,)), ((), ())), preferred_element_type=f32)


def dot_nt(a, b):
    return lax.dot_general(a, b, (((1,), (1,)), ((), ())), preferred_element_type=f32)


def rope(rows, cosine, sine):
    half = rows.shape[-1] // 2
    a, b = rows[..., :half], rows[..., half:]
    return jnp.concatenate([a * cosine - b * sine, b * cosine + a * sine], axis=-1)


def block_tables(segments):
    micro, block_len = segments.shape
    offsets = jnp.arange(block_len, dtype=jnp.int32)
    same = segments[:, :, None] == segments[:, None, :]
    start = jnp.min(jnp.where(same, offsets, block_len), axis=-1)
    positions = (offsets - start).astype(f32).reshape(-1)
    half = HEAD_SIZE // 2
    frequency = theta_base ** (-(2.0 * jnp.arange(half, dtype=f32)) / HEAD_SIZE)
    angles = positions[:, None] * frequency
    allowed = same & (offsets[:, None] >= offsets[None, :])
    eye = jnp.eye(micro, dtype=bool)
    full = allowed[:, :, None, :] & eye[:, None, :, None]
    total = micro * block_len
    return jnp.cos(angles), jnp.sin(angles), full.reshape(total, total)


def scores_of(q, k, allowed):
    s = jnp.einsum("tgrd,ugd->grtu", q, k, preferred_element_type=f32) * HEAD_SIZE**-0.5
    return jnp.where(allowed, s, -1000000000.0)


def forward(u, weights, tables):
    qkv_w, out_w, gate_w, up_w, down_w, gain_one, gain_two = weights
    cosine, sine, allowed = tables
    tokens = u.shape[0]
    u = u.astype(f32)
    r1 = lax.rsqrt(jnp.mean(u * u, axis=-1, keepdims=True) + epsilon)
    n = (u * r1 * gain_one).astype(bf16)
    proj = dot_nt(n, qkv_w)
    q = rope(
        proj[:, :Q_COLS].reshape(tokens, KEY_VALUE_HEADS, GROUP, HEAD_SIZE),
        cosine[:, None, None, :],
        sine[:, None, None, :],
    ).astype(bf16)
    k = rope(
        proj[:, Q_COLS : Q_COLS + KV_COLS].reshape(tokens, KEY_VALUE_HEADS, HEAD_SIZE),
        cosine[:, None, :],
        sine[:, None, :],
    ).astype(bf16)
    v = proj[:, Q_COLS + KV_COLS :].reshape(tokens, KEY_VALUE_HEADS, HEAD_SIZE).astype(bf16)
    masked = scores_of(q, k, allowed)
    peak = jnp.max(masked, axis=-1, keepdims=True)
    lse = peak + jnp.log(jnp.sum(jnp.exp(masked - peak), axis=-1, keepdims=True))
    prob = jnp.exp(masked - lse).astype(bf16)
    o = jnp.einsum("grtu,ugd->tgrd", prob, v, preferred_element_type=f32)
    o = o.reshape(tokens, Q_COLS).astype(bf16)
    h1 = u + dot_nn(o, out_w)
    r2 = lax.rsqrt(jnp.mean(h1 * h1, axis=-1, keepdims=True) + epsilon)
    m = (h1 * r2 * gain_two).astype(bf16)
    gate = dot_nt(m, gate_w)
    up = dot_nt(m, up_w)
    act = (jax.nn.silu(gate) * up).astype(bf16)
    out = h1 + dot_nn(act, down_w)
    return out, (u, r1, n, q, k, v, lse, o, h1, r2, m, gate, up, act)


def norm_back(grad, rows, r, gain):
    scaled = grad * gain
    part = r * scaled - rows * (r * r * r) * jnp.mean(scaled * rows, axis=-1, keepdims=True)
    return part, jnp.sum(grad * rows * r, axis=0)


def backward(e, state, weights, tables):
    qkv_w, out_w, gate_w, up_w, down_w, gain_one, gain_two = weights
    cosine, sine, allowed = tables
    u, r1, n, q, k, v, lse, o, h1, r2, m, gate, up, act = state
    tokens = u.shape[0]
    eb = e.astype(bf16)
    e = e.astype(f32)
    da = dot_nt(eb, down_w)
    sig = jax.nn.sigmoid(gate)
    dgate = (da * up * sig * (1.0 + gate * (1.0 - sig))).astype(bf16)
    dup = (da * gate * sig).astype(bf16)
    dm = dot_nn(dgate, gate_w) + dot_nn(dup, up_w)
    part, gain_two_grad = norm_back(dm, h1, r2, gain_two)
    dh1 = e + part
    dz = dh1.astype(bf16)
    do = dot_nt(dz, out_w).reshape(tokens, KEY_VALUE_HEADS, GROUP, HEAD_SIZE).astype(bf16)
    prob = jnp.exp(scores_of(q, k, allowed) - lse)
    dv = jnp.einsum("grtu,tgrd->ugd", prob.astype(bf16), do, preferred_element_type=f32)
    dp = jnp.einsum("tgrd,ugd->grtu", do, v, preferred_element_type=f32)
    ds = (prob * (dp - jnp.sum(dp * prob, axis=-1, keepdims=True))).astype(bf16)
    dq = jnp.einsum("grtu,ugd->tgrd", ds, k, preferred_element_type=f32) * HEAD_SIZE**-0.5
    dk = jnp.einsum("grtu,tgrd->ugd", ds, q, preferred_element_type=f32) * HEAD_SIZE**-0.5
    dq = rope(dq, cosine[:, None, None, :], -sine[:, None, None, :])
    dk = rope(dk, cosine[:, None, :], -sine[:, None, :])
    dproj = jnp.concatenate(
        [dq.reshape(tokens, Q_COLS), dk.reshape(tokens, KV_COLS), dv.reshape(tokens, KV_COLS)],
        axis=1,
    ).astype(bf16)
    dn = dot_nn(dproj, qkv_w)
    part, gain_one_grad = norm_back(dn, u, r1, gain_one)
    du = dh1 + part
    gain_grad = jnp.concatenate([gain_one_grad, gain_two_grad])
    return du, (n, dproj, o, dz, m, dgate, dup, eb, act), gain_grad


def flip(x, bit):
    size = lax.axis_size("dp")
    return lax.ppermute(x, "dp", [(i, i ^ bit) for i in range(size)])


def gather_small(row):
    size = lax.axis_size("dp")
    me = lax.axis_index("dp")
    bit = 1
    while bit < size:
        other = flip(row, bit)
        high = (me & bit) != 0
        row = jnp.concatenate([jnp.where(high, other, row), jnp.where(high, row, other)])
        bit *= 2
    return row


def scatter_small(row):
    size = lax.axis_size("dp")
    me = lax.axis_index("dp")
    bit = size // 2
    while bit >= 1:
        half = row.shape[0] // 2
        low, top = row[:half], row[half:]
        high = (me & bit) != 0
        row = jnp.where(high, top, low) + flip(jnp.where(high, low, top), bit)
        bit //= 2
    return row


def grads_generic(pieces):
    n, dproj, o, dz, m, dgate, dup, eb, act = pieces
    attn = jnp.concatenate([dot_nn(dproj.T, n), dot_nn(o.T, dz)], axis=0)
    both = [
        lax.psum_scatter(g, "dp", scatter_dimension=0, tiled=True)
        for g in (attn, dot_nn(dgate.T, m), dot_nn(dup.T, m), dot_nn(act.T, eb))
    ]
    return both[0], jnp.stack(both[1:])


def plane_rows(x):
    x = jnp.concatenate([x, flip(x, Y_BIT)], axis=0)
    return jnp.concatenate([x, flip(x, CORE_BIT)], axis=0)


def doubled(block, bits):
    block = block[None]
    for bit in bits:
        block = jnp.concatenate([block, flip(block, bit)], axis=0)
    return block


def doubled_in_order(block, bits, me):
    rows, width = block.shape
    have = []
    for bit in bits:
        other = flip(block, bit)
        high = (me & bit) != 0
        have = sorted(have + [bit], reverse=True)
        block = jnp.stack(
            [jnp.where(high, other, block), jnp.where(high, block, other)], axis=have.index(bit)
        )
    return block.reshape(-1, width)


def ffn_cols(*arrays):
    tokens, cols = arrays[0].shape
    share = cols // 16
    x = jnp.stack([a.T.reshape(2, 2, 2, 2, share, tokens) for a in arrays])
    x = jnp.concatenate([x[:, :, 0], flip(x[:, :, 1], Y_BIT)], axis=-1)
    return jnp.concatenate([x[:, 0], flip(x[:, 1], CORE_BIT)], axis=-1)


def attn_cols(array, y, core):
    tokens, cols = array.shape
    share = cols // 16
    x = array.T.reshape(2, 2, 2, 2, share, tokens)
    pick = lambda v, i: lax.dynamic_index_in_dim(v, i, 2, keepdims=False)
    x = jnp.concatenate([pick(x, y), flip(pick(x, 1 - y), Y_BIT)], axis=-1)
    return jnp.concatenate([pick(x, core), flip(pick(x, 1 - core), CORE_BIT)], axis=-1)


def halved(keep, send, bit):
    return keep.astype(f32) + flip(send.astype(bf16), bit).astype(f32)


def ffn_sum(parts):
    x = halved(parts[0], parts[1], Z1_BIT)
    return halved(x[0], x[1], Z2_BIT)


def attn_sum(parts, z2, z1):
    pick = lambda v, i, axis: lax.dynamic_index_in_dim(v, i, axis, keepdims=False)
    x = halved(pick(parts, z1, 1), pick(parts, 1 - z1, 1), Z1_BIT)
    return halved(pick(x, z2, 0), pick(x, 1 - z2, 0), Z2_BIT)


def grads_planes(pieces, me):
    n, dproj, o, dz, m, dgate, dup, eb, act = pieces
    z2, z1, y, core = (me >> 3) & 1, (me >> 2) & 1, (me >> 1) & 1, me & 1
    tokens = n.shape[0]
    share = act.shape[1] // 16
    wide = 4 * tokens
    m_all = plane_rows(m)
    n_all = plane_rows(n)
    act_c = ffn_cols(act)[0]
    o_c = attn_cols(jnp.concatenate([dproj, o], axis=1), y, core)
    eb_all = plane_rows(eb)

    def product(cols, rows):
        return dot_nn(cols.reshape(4 * share, wide), rows).reshape(2, 2, share, -1)

    down = ffn_sum(product(act_c, eb_all))
    gu_c = ffn_cols(dgate, dup)
    gate = ffn_sum(product(gu_c[0], m_all))
    up = ffn_sum(product(gu_c[1], m_all))
    dz_all = plane_rows(dz)
    owners = (jnp.arange(4, dtype=jnp.int32) * 4 + y * 2 + core).reshape(2, 2, 1, 1)
    is_qkv = owners * share < QKV_COLS
    attn = jnp.where(is_qkv, product(o_c, n_all), product(o_c, dz_all))
    attn = attn_sum(attn, z2, z1)
    return attn, jnp.stack([gate, up, down])


def local(edge_data, segment_ids, attn_weight, ffn_weight, gains):
    micro = segment_ids.shape[0]
    leading = lax.axis_index("section") == 0
    tables = block_tables(segment_ids)
    block, width = edge_data.shape[2], edge_data.shape[3]
    x = edge_data[0].reshape(micro * block, width)
    planes = lax.axis_size("dp") == 16
    me = lax.axis_index("dp")
    attn_own = attn_weight[0].T
    ffn_own = ffn_weight[0].swapaxes(1, 2)
    if planes:
        attn_t = doubled_in_order(attn_own, (Z2_BIT, Y_BIT, Z1_BIT, CORE_BIT), me)
        ffn_t = [
            doubled(ffn_own[i], (Z2_BIT, Z1_BIT, Y_BIT, CORE_BIT)).reshape(-1, width) for i in range(3)
        ]
    else:
        attn_t = lax.all_gather(attn_own, "dp", axis=0, tiled=True)
        ffn_t = lax.all_gather(ffn_own, "dp", axis=1, tiled=True)
    gain_row = gather_small(gains[0]).astype(f32)
    weights = (
        attn_t[:QKV_COLS],
        attn_t[QKV_COLS:],
        ffn_t[0],
        ffn_t[1],
        ffn_t[2],
        gain_row[:width],
        gain_row[width:],
    )
    first, _ = forward(x, weights, tables)
    received = lax.ppermute(first.astype(bf16), "section", [(0, 1)])
    u = jnp.where(leading, x, received)
    out, state = forward(u, weights, tables)
    first_grad, _, _ = backward(x, state, weights, tables)
    received = lax.ppermute(first_grad.astype(bf16), "section", [(1, 0)])
    e = jnp.where(leading, received, x)
    du, pieces, gain_grad = backward(e, state, weights, tables)
    if planes:
        attn_rows, ffn_rows = grads_planes(pieces, me)
    else:
        attn_rows, ffn_rows = grads_generic(pieces)
    gain_shard = scatter_small(gain_grad)
    edge_out = jnp.where(leading, du, out).astype(bf16).reshape(micro, block, width)
    return (
        edge_out[None],
        attn_rows.T[None],
        ffn_rows.swapaxes(1, 2)[None],
        gain_shard[None],
    )


def solution(mesh):
    in_specs = (
        P("section", None, "dp", None),
        P(None, "dp"),
        P("section", None, "dp"),
        P("section", None, None, "dp"),
        P("section", "dp"),
    )
    out_specs = (
        P("section", None, "dp", None),
        P("section", None, "dp"),
        P("section", None, None, "dp"),
        P("section", "dp"),
    )
    return jax.shard_map(local, mesh=mesh, in_specs=in_specs, out_specs=out_specs, check_vma=False)
```

```python
import jax
import jax.numpy as jnp
from jax import lax
from jax.sharding import PartitionSpec as P

QUERY_HEADS = 15
KEY_VALUE_HEADS = 5
HEAD_SIZE = 64
GROUP = QUERY_HEADS // KEY_VALUE_HEADS
Q_COLS = QUERY_HEADS * HEAD_SIZE
KV_COLS = KEY_VALUE_HEADS * HEAD_SIZE
QKV_COLS = Q_COLS + 2 * KV_COLS

epsilon = 1e-05
theta_base = 100000.0
Z2_BIT, Z1_BIT, Y_BIT, CORE_BIT = 8, 4, 2, 1
EXTRA_ROWS = 8
bf16 = jnp.bfloat16
f32 = jnp.float32


def dot_nn(a, b):
    return lax.dot_general(a, b, (((1,), (0,)), ((), ())), preferred_element_type=f32)


def dot_nt(a, b):
    return lax.dot_general(a, b, (((1,), (1,)), ((), ())), preferred_element_type=f32)


def rope(rows, cosine, sine):
    half = rows.shape[-1] // 2
    a, b = rows[..., :half], rows[..., half:]
    return jnp.concatenate([a * cosine - b * sine, b * cosine + a * sine], axis=-1)


def block_tables(segments):
    micro, block_len = segments.shape
    offsets = jnp.arange(block_len, dtype=jnp.int32)
    same = segments[:, :, None] == segments[:, None, :]
    start = jnp.min(jnp.where(same, offsets, block_len), axis=-1)
    positions = (offsets - start).astype(f32).reshape(-1)
    half = HEAD_SIZE // 2
    frequency = theta_base ** (-(2.0 * jnp.arange(half, dtype=f32)) / HEAD_SIZE)
    angles = positions[:, None] * frequency
    allowed = same & (offsets[:, None] >= offsets[None, :])
    eye = jnp.eye(micro, dtype=bool)
    full = allowed[:, :, None, :] & eye[:, None, :, None]
    total = micro * block_len
    return jnp.cos(angles), jnp.sin(angles), full.reshape(total, total)


def scores_of(q, k, allowed):
    s = jnp.einsum("tgrd,ugd->grtu", q, k, preferred_element_type=f32) * HEAD_SIZE**-0.5
    return jnp.where(allowed, s, -1000000000.0)


def forward(u, weights, tables):
    qkv_w, out_w, gate_w, up_w, down_w, gain_one, gain_two = weights
    cosine, sine, allowed = tables
    tokens = u.shape[0]
    u = u.astype(f32)
    r1 = lax.rsqrt(jnp.mean(u * u, axis=-1, keepdims=True) + epsilon)
    n = (u * r1 * gain_one).astype(bf16)
    proj = dot_nt(n, qkv_w)
    q = rope(
        proj[:, :Q_COLS].reshape(tokens, KEY_VALUE_HEADS, GROUP, HEAD_SIZE),
        cosine[:, None, None, :],
        sine[:, None, None, :],
    ).astype(bf16)
    k = rope(
        proj[:, Q_COLS : Q_COLS + KV_COLS].reshape(tokens, KEY_VALUE_HEADS, HEAD_SIZE),
        cosine[:, None, :],
        sine[:, None, :],
    ).astype(bf16)
    v = proj[:, Q_COLS + KV_COLS :].reshape(tokens, KEY_VALUE_HEADS, HEAD_SIZE).astype(bf16)
    masked = scores_of(q, k, allowed)
    peak = jnp.max(masked, axis=-1, keepdims=True)
    lse = peak + jnp.log(jnp.sum(jnp.exp(masked - peak), axis=-1, keepdims=True))
    prob = jnp.exp(masked - lse).astype(bf16)
    o = jnp.einsum("grtu,ugd->tgrd", prob, v, preferred_element_type=f32)
    o = o.reshape(tokens, Q_COLS).astype(bf16)
    h1 = u + dot_nn(o, out_w)
    r2 = lax.rsqrt(jnp.mean(h1 * h1, axis=-1, keepdims=True) + epsilon)
    m = (h1 * r2 * gain_two).astype(bf16)
    gate = [dot_nt(m, w) for w in gate_w]
    up = [dot_nt(m, w) for w in up_w]
    act = [(jax.nn.silu(g) * p).astype(bf16) for g, p in zip(gate, up)]
    out = h1
    for a, w in zip(act, down_w):
        out = out + dot_nn(a, w)
    return out, (u, r1, n, q, k, v, lse, o, h1, r2, m, gate, up, act)


def norm_back(grad, rows, r, gain):
    scaled = grad * gain
    part = r * scaled - rows * (r * r * r) * jnp.mean(scaled * rows, axis=-1, keepdims=True)
    return part, jnp.sum(grad * rows * r, axis=0)


def backward(e, state, weights, tables):
    qkv_w, out_w, gate_w, up_w, down_w, gain_one, gain_two = weights
    cosine, sine, allowed = tables
    u, r1, n, q, k, v, lse, o, h1, r2, m, gate, up, act = state
    tokens = u.shape[0]
    eb = e.astype(bf16)
    e = e.astype(f32)
    dgate, dup = [], []
    for g, p, w in zip(gate, up, down_w):
        da = dot_nt(eb, w)
        sig = jax.nn.sigmoid(g)
        dgate.append((da * p * sig * (1.0 + g * (1.0 - sig))).astype(bf16))
        dup.append((da * g * sig).astype(bf16))
    dm = 0.0
    for g, p, wg, wu in zip(dgate, dup, gate_w, up_w):
        dm = dm + dot_nn(g, wg) + dot_nn(p, wu)
    part, gain_two_grad = norm_back(dm, h1, r2, gain_two)
    dh1 = e + part
    dz = dh1.astype(bf16)
    do = dot_nt(dz, out_w).reshape(tokens, KEY_VALUE_HEADS, GROUP, HEAD_SIZE).astype(bf16)
    prob = jnp.exp(scores_of(q, k, allowed) - lse)
    dv = jnp.einsum("grtu,tgrd->ugd", prob.astype(bf16), do, preferred_element_type=f32)
    dp = jnp.einsum("tgrd,ugd->grtu", do, v, preferred_element_type=f32)
    ds = (prob * (dp - jnp.sum(dp * prob, axis=-1, keepdims=True))).astype(bf16)
    dq = jnp.einsum("grtu,ugd->tgrd", ds, k, preferred_element_type=f32) * HEAD_SIZE**-0.5
    dk = jnp.einsum("grtu,tgrd->ugd", ds, q, preferred_element_type=f32) * HEAD_SIZE**-0.5
    dq = rope(dq, cosine[:, None, None, :], -sine[:, None, None, :])
    dk = rope(dk, cosine[:, None, :], -sine[:, None, :])
    dproj = jnp.concatenate(
        [dq.reshape(tokens, Q_COLS), dk.reshape(tokens, KV_COLS), dv.reshape(tokens, KV_COLS)],
        axis=1,
    ).astype(bf16)
    dn = dot_nn(dproj, qkv_w)
    part, gain_one_grad = norm_back(dn, u, r1, gain_one)
    du = dh1 + part
    gain_grad = jnp.concatenate([gain_one_grad, gain_two_grad])
    return du, (n, dproj, o, dz, m, dgate, dup, eb, act), gain_grad


def flip(x, bit):
    size = lax.axis_size("dp")
    return lax.ppermute(x, "dp", [(i, i ^ bit) for i in range(size)])


def gather_small(row):
    size = lax.axis_size("dp")
    me = lax.axis_index("dp")
    bit = 1
    while bit < size:
        other = flip(row, bit)
        high = (me & bit) != 0
        row = jnp.concatenate([jnp.where(high, other, row), jnp.where(high, row, other)])
        bit *= 2
    return row


def scatter_small(row):
    size = lax.axis_size("dp")
    me = lax.axis_index("dp")
    bit = size // 2
    while bit >= 1:
        half = row.shape[0] // 2
        low, top = row[:half], row[half:]
        high = (me & bit) != 0
        row = jnp.where(high, top, low) + flip(jnp.where(high, low, top), bit)
        bit //= 2
    return row


def grads_generic(pieces):
    n, dproj, o, dz, m, dgate, dup, eb, act = pieces
    attn = jnp.concatenate([dot_nn(dproj.T, n), dot_nn(o.T, dz)], axis=0)
    dgate, dup, act = (jnp.concatenate(v, axis=1) for v in (dgate, dup, act))
    both = [
        lax.psum_scatter(g, "dp", scatter_dimension=0, tiled=True)
        for g in (attn, dot_nn(dgate.T, m), dot_nn(dup.T, m), dot_nn(act.T, eb))
    ]
    return both[0], jnp.stack(both[1:])


def z_pairs(x, pairs):
    return lax.ppermute(x, "dp", [(4 * a + i, 4 * b + i) for a, b in pairs for i in range(4)])


def inner_swap(x):
    return z_pairs(x, [(1, 2), (2, 1)])


def from_far(x, is_inner):
    inner = inner_swap(x)
    outer = z_pairs(inner, [(1, 0), (2, 3)])
    return jnp.where(is_inner, inner, outer)


def gather_ffn(block, is_inner):
    near = jnp.stack([block, flip(block, Z1_BIT)])
    far = from_far(near, is_inner)
    half = jnp.concatenate([near, far, flip(near, Y_BIT), flip(far, Y_BIT)], axis=0)
    half = half.reshape(-1, block.shape[1])
    return [half, flip(half, CORE_BIT)]


def gather_attn(block, me, is_inner):
    have = []
    for bit in (Z1_BIT, Y_BIT, Z2_BIT, CORE_BIT):
        other = from_far(block, is_inner) if bit == Z2_BIT else flip(block, bit)
        high = (me & bit) != 0
        have = sorted(have + [bit], reverse=True)
        block = jnp.stack(
            [jnp.where(high, other, block), jnp.where(high, block, other)], axis=have.index(bit)
        )
    return block.reshape(16, *block.shape[-2:])


def plane_rows(x):
    x = jnp.concatenate([x, flip(x, Y_BIT)], axis=0)
    return jnp.concatenate([x, flip(x, CORE_BIT)], axis=0)


def ffn_cols_y(own, other):
    tokens, cols = own.shape
    x = jnp.stack([own.T, other.T]).reshape(2, 2, 4, cols // 8, tokens)
    return jnp.concatenate([x[:, 0], flip(x[:, 1], Y_BIT)], axis=-1)


def ffn_cols_core(x):
    return jnp.concatenate([x[0], flip(x[1], CORE_BIT)], axis=-1)


def attn_cols(array, y, core):
    tokens, cols = array.shape
    share = cols // 16
    x = array.T.reshape(2, 2, 2, 2, share, tokens)
    pick = lambda v, i: lax.dynamic_index_in_dim(v, i, 2, keepdims=False)
    x = jnp.concatenate([pick(x, y), flip(pick(x, 1 - y), Y_BIT)], axis=-1)
    return jnp.concatenate([pick(x, core), flip(pick(x, 1 - core), CORE_BIT)], axis=-1)


def line_sum(near, far):
    far = far + z_pairs(far.astype(bf16), [(0, 1), (3, 2)]).astype(f32)
    return near + inner_swap(far.astype(bf16)).astype(f32)


def pair_sum(keep, send):
    return keep + flip(send.astype(bf16), Z1_BIT).astype(f32)


def ffn_sum(parts):
    near = line_sum(parts[:2], parts[2:])
    return pair_sum(near[0], near[1])


def attn_sum(parts, z2, z1):
    pick = lambda v, i: lax.dynamic_index_in_dim(v, i, 0, keepdims=False)
    near = line_sum(pick(parts, z2), pick(parts, 1 - z2))
    return pair_sum(pick(near, z1), pick(near, 1 - z1))


def early_exchange(state):
    n, m, act = state[2], state[10], state[13]
    return (
        jnp.concatenate([m, flip(m, Y_BIT)], axis=0),
        jnp.concatenate([n, flip(n, Y_BIT)], axis=0),
        ffn_cols_y(*act),
    )


def grads_planes(pieces, early, gain_grad, me):
    n, dproj, o, dz, m, dgate, dup, eb, act = pieces
    m_y, n_y, act_y = early
    z2, z1, y, core = (me >> 3) & 1, (me >> 2) & 1, (me >> 1) & 1, me & 1
    width = n.shape[1]
    over_core = lambda v: jnp.concatenate([v, flip(v, CORE_BIT)], axis=0)
    eb_all = plane_rows(eb)
    act_c = ffn_cols_core(act_y)
    share = act_c.shape[1]

    def product(cols, rows):
        return dot_nn(cols.reshape(4 * share, -1), rows).reshape(4, share, -1)

    down = ffn_sum(product(act_c, eb_all))
    m_all = over_core(m_y)
    gate = ffn_sum(product(ffn_cols_core(ffn_cols_y(*dgate)), m_all))
    up = ffn_sum(product(ffn_cols_core(ffn_cols_y(*dup)), m_all))
    n_all = over_core(n_y)
    dz_all = plane_rows(dz)
    o_c = attn_cols(jnp.concatenate([dproj, o], axis=1), y, core)
    owners = (jnp.arange(4, dtype=jnp.int32) * 4 + y * 2 + core).reshape(4, 1, 1)
    is_qkv = owners * share < QKV_COLS
    attn = jnp.where(is_qkv, product(o_c, n_all), product(o_c, dz_all))
    gain_grad = gain_grad + flip(gain_grad, CORE_BIT)
    gain_grad = gain_grad + flip(gain_grad, Y_BIT)
    gain_rows = gain_grad.reshape(4, 4, -1)
    gain_rows = lax.dynamic_index_in_dim(gain_rows, y * 2 + core, 1, keepdims=True)
    gain_share = gain_rows.shape[-1]
    gain_rows = jnp.pad(gain_rows, ((0, 0), (0, EXTRA_ROWS - 1), (0, width - gain_share)))
    parts = jnp.concatenate([attn, gain_rows], axis=1)
    attn = attn_sum(parts.reshape(2, 2, share + EXTRA_ROWS, width), z2, z1)
    return attn[:share], jnp.stack([gate, up, down]), attn[share : share + 1, :gain_share]


def local(edge_data, segment_ids, attn_weight, ffn_weight, gains):
    micro = segment_ids.shape[0]
    leading = lax.axis_index("section") == 0
    tables = block_tables(segment_ids)
    block, width = edge_data.shape[2], edge_data.shape[3]
    x = edge_data[0].reshape(micro * block, width)
    planes = lax.axis_size("dp") == 16
    me = lax.axis_index("dp")
    attn_own = attn_weight[0].T
    ffn_own = ffn_weight[0].swapaxes(1, 2)
    if planes:
        z = me // 4
        is_inner = (z == 1) | (z == 2)
        share = attn_own.shape[0]
        gain_rows = jnp.pad(gains, ((0, EXTRA_ROWS - 1), (0, width - gains.shape[1])))
        attn_all = gather_attn(jnp.concatenate([attn_own, gain_rows], axis=0), me, is_inner)
        gain_row = attn_all[:, share, : gains.shape[1]].reshape(-1).astype(f32)
        attn_t = attn_all[:, :share].reshape(-1, width)
        ffn_t = [gather_ffn(ffn_own[i], is_inner) for i in range(3)]
    else:
        attn_t = lax.all_gather(attn_own, "dp", axis=0, tiled=True)
        ffn_t = [[w] for w in lax.all_gather(ffn_own, "dp", axis=1, tiled=True)]
        gain_row = gather_small(gains[0]).astype(f32)
    weights = (
        attn_t[:QKV_COLS],
        attn_t[QKV_COLS:],
        ffn_t[0],
        ffn_t[1],
        ffn_t[2],
        gain_row[:width],
        gain_row[width:],
    )
    first, _ = forward(x, weights, tables)
    received = lax.ppermute(first.astype(bf16), "section", [(0, 1)])
    u = jnp.where(leading, x, received)
    out, state = forward(u, weights, tables)
    first_grad, _, _ = backward(x, state, weights, tables)
    first_grad = first_grad.astype(bf16)
    if planes:
        early = early_exchange(state)
        first_grad, early = lax.optimization_barrier((first_grad, early))
    received = lax.ppermute(first_grad, "section", [(1, 0)])
    e = jnp.where(leading, received, x)
    du, pieces, gain_grad = backward(e, state, weights, tables)
    if planes:
        attn_rows, ffn_rows, gain_shard = grads_planes(pieces, early, gain_grad, me)
    else:
        attn_rows, ffn_rows = grads_generic(pieces)
        gain_shard = scatter_small(gain_grad)[None]
    edge_out = jnp.where(leading, du, out).astype(bf16).reshape(micro, block, width)
    return (
        edge_out[None],
        attn_rows.T[None],
        ffn_rows.swapaxes(1, 2)[None],
        gain_shard,
    )


def solution(mesh):
    in_specs = (
        P("section", None, "dp", None),
        P(None, "dp"),
        P("section", None, "dp"),
        P("section", None, None, "dp"),
        P("section", "dp"),
    )
    out_specs = (
        P("section", None, "dp", None),
        P("section", None, "dp"),
        P("section", None, None, "dp"),
        P("section", "dp"),
    )
    return jax.shard_map(local, mesh=mesh, in_specs=in_specs, out_specs=out_specs, check_vma=False)
```

```python
import jax
import jax.numpy as jnp
from jax import lax
from jax.experimental import pallas as pl
from jax.experimental.pallas import tpu as pltpu
from jax.sharding import PartitionSpec as P

QUERY_HEADS = 15
KEY_VALUE_HEADS = 5
HEAD_SIZE = 64
GROUP = QUERY_HEADS // KEY_VALUE_HEADS
Q_COLS = QUERY_HEADS * HEAD_SIZE
KV_COLS = KEY_VALUE_HEADS * HEAD_SIZE
QKV_COLS = Q_COLS + 2 * KV_COLS

epsilon = 1e-05
theta_base = 100000.0
Z2_BIT, Z1_BIT, Y_BIT, CORE_BIT = 8, 4, 2, 1
EXTRA_ROWS = 8
bf16 = jnp.bfloat16
f32 = jnp.float32


def dot_nn(a, b):
    return lax.dot_general(a, b, (((1,), (0,)), ((), ())), preferred_element_type=f32)


def dot_nt(a, b):
    return lax.dot_general(a, b, (((1,), (1,)), ((), ())), preferred_element_type=f32)


def rope(rows, cosine, sine):
    half = rows.shape[-1] // 2
    a, b = rows[..., :half], rows[..., half:]
    return jnp.concatenate([a * cosine - b * sine, b * cosine + a * sine], axis=-1)


def block_tables(segments):
    micro, block_len = segments.shape
    offsets = jnp.arange(block_len, dtype=jnp.int32)
    same = segments[:, :, None] == segments[:, None, :]
    start = jnp.min(jnp.where(same, offsets, block_len), axis=-1)
    positions = (offsets - start).astype(f32).reshape(-1)
    half = HEAD_SIZE // 2
    frequency = theta_base ** (-(2.0 * jnp.arange(half, dtype=f32)) / HEAD_SIZE)
    angles = positions[:, None] * frequency
    allowed = same & (offsets[:, None] >= offsets[None, :])
    eye = jnp.eye(micro, dtype=bool)
    full = allowed[:, :, None, :] & eye[:, None, :, None]
    total = micro * block_len
    return jnp.cos(angles), jnp.sin(angles), full.reshape(total, total)


def scores_of(q, k, allowed):
    s = jnp.einsum("tgrd,ugd->grtu", q, k, preferred_element_type=f32) * HEAD_SIZE**-0.5
    return jnp.where(allowed, s, -1000000000.0)


def forward(u, weights, tables):
    qkv_w, out_w, ffn_w, gain_one, gain_two = weights
    cosine, sine, allowed = tables
    tokens = u.shape[0]
    u = u.astype(f32)
    r1 = lax.rsqrt(jnp.mean(u * u, axis=-1, keepdims=True) + epsilon)
    n = (u * r1 * gain_one).astype(bf16)
    proj = dot_nt(n, qkv_w)
    q = rope(
        proj[:, :Q_COLS].reshape(tokens, KEY_VALUE_HEADS, GROUP, HEAD_SIZE),
        cosine[:, None, None, :],
        sine[:, None, None, :],
    ).astype(bf16)
    k = rope(
        proj[:, Q_COLS : Q_COLS + KV_COLS].reshape(tokens, KEY_VALUE_HEADS, HEAD_SIZE),
        cosine[:, None, :],
        sine[:, None, :],
    ).astype(bf16)
    v = proj[:, Q_COLS + KV_COLS :].reshape(tokens, KEY_VALUE_HEADS, HEAD_SIZE).astype(bf16)
    masked = scores_of(q, k, allowed)
    peak = jnp.max(masked, axis=-1, keepdims=True)
    lse = peak + jnp.log(jnp.sum(jnp.exp(masked - peak), axis=-1, keepdims=True))
    prob = jnp.exp(masked - lse).astype(bf16)
    o = jnp.einsum("grtu,ugd->tgrd", prob, v, preferred_element_type=f32)
    o = o.reshape(tokens, Q_COLS).astype(bf16)
    h1 = u + dot_nn(o, out_w)
    r2 = lax.rsqrt(jnp.mean(h1 * h1, axis=-1, keepdims=True) + epsilon)
    m = (h1 * r2 * gain_two).astype(bf16)
    gate, up, act, out = ffn_forward(m, h1, ffn_w)
    return out, (u, r1, n, q, k, v, lse, o, h1, r2, m, gate, up, act)


def norm_back(grad, rows, r, gain):
    scaled = grad * gain
    part = r * scaled - rows * (r * r * r) * jnp.mean(scaled * rows, axis=-1, keepdims=True)
    return part, jnp.sum(grad * rows * r, axis=0)


def backward_ffn(eb, state, weights):
    gate, up = state[11], state[12]
    return ffn_backward(eb, gate, up, weights[2])


def backward_mid(e, dm, state, weights):
    out_w, gain_two = weights[1], weights[4]
    h1, r2 = state[8], state[9]
    part, gain_two_grad = norm_back(dm, h1, r2, gain_two)
    dh1 = e.astype(f32) + part
    dz = dh1.astype(bf16)
    return dh1, dz, dot_nt(dz, out_w).astype(bf16), gain_two_grad


def backward_attention(do, state, tables):
    cosine, sine, allowed = tables
    q, k, v, lse = state[3:7]
    tokens = do.shape[0]
    do = do.reshape(tokens, KEY_VALUE_HEADS, GROUP, HEAD_SIZE)
    prob = jnp.exp(scores_of(q, k, allowed) - lse)
    dv = jnp.einsum("grtu,tgrd->ugd", prob.astype(bf16), do, preferred_element_type=f32)
    dp = jnp.einsum("tgrd,ugd->grtu", do, v, preferred_element_type=f32)
    ds = (prob * (dp - jnp.sum(dp * prob, axis=-1, keepdims=True))).astype(bf16)
    dq = jnp.einsum("grtu,ugd->tgrd", ds, k, preferred_element_type=f32) * HEAD_SIZE**-0.5
    dk = jnp.einsum("grtu,tgrd->ugd", ds, q, preferred_element_type=f32) * HEAD_SIZE**-0.5
    dq = rope(dq, cosine[:, None, None, :], -sine[:, None, None, :])
    dk = rope(dk, cosine[:, None, :], -sine[:, None, :])
    return jnp.concatenate(
        [dq.reshape(tokens, Q_COLS), dk.reshape(tokens, KV_COLS), dv.reshape(tokens, KV_COLS)],
        axis=1,
    ).astype(bf16)


def backward_in(dproj, dh1, state, weights):
    qkv_w, gain_one = weights[0], weights[3]
    u, r1 = state[0], state[1]
    part, gain_one_grad = norm_back(dot_nn(dproj, qkv_w), u, r1, gain_one)
    return dh1 + part, gain_one_grad


def backward(e, state, weights, tables):
    dgate, dup, dm = backward_ffn(e.astype(bf16), state, weights)
    dh1, dz, do, gain_two_grad = backward_mid(e, dm, state, weights)
    dproj = backward_attention(do, state, tables)
    du, gain_one_grad = backward_in(dproj, dh1, state, weights)
    pieces = (state[2], dproj, state[7], dz, state[10], dgate, dup, e.astype(bf16), state[13])
    return du, pieces, jnp.concatenate([gain_one_grad, gain_two_grad])


def ffn_forward_kernel(m_ref, h1_ref, wg_ref, wu_ref, wd_ref, gate_ref, up_ref, act_ref, out_ref):
    flat = lambda ref: ref[...].reshape(-1, ref.shape[-1])
    m = m_ref[...]
    gate = dot_nt(m, flat(wg_ref))
    up = dot_nt(m, flat(wu_ref))
    act = (gate * jax.nn.sigmoid(gate) * up).astype(bf16)
    gate_ref[...] = gate
    up_ref[...] = up
    act_ref[...] = act
    add = dot_nn(act, flat(wd_ref))

    @pl.when(pl.program_id(0) == 0)
    def _():
        out_ref[...] = h1_ref[...] + add

    @pl.when(pl.program_id(0) > 0)
    def _():
        out_ref[...] += add


def ffn_backward_kernel(
    eb_ref, gate_ref, up_ref, wg_ref, wu_ref, wd_ref, dgate_ref, dup_ref, dm_ref
):
    flat = lambda ref: ref[...].reshape(-1, ref.shape[-1])
    da = dot_nt(eb_ref[...], flat(wd_ref))
    gate = gate_ref[...]
    sig = jax.nn.sigmoid(gate)
    dgate = (da * up_ref[...] * sig * (1.0 + gate * (1.0 - sig))).astype(bf16)
    dup = (da * gate * sig).astype(bf16)
    dgate_ref[...] = dgate
    dup_ref[...] = dup
    add = dot_nn(dgate, flat(wg_ref)) + dot_nn(dup, flat(wu_ref))

    @pl.when(pl.program_id(0) == 0)
    def _():
        dm_ref[...] = add

    @pl.when(pl.program_id(0) > 0)
    def _():
        dm_ref[...] += add


def weight_spec(w, matrix):
    lines, _, _, share, width = w.shape
    return pl.BlockSpec((lines, None, None, share, width), lambda i: (0, i, matrix, 0, 0))


def ffn_call(kernel, w, wholes, blocks, out_blocks):
    lines, steps, _, share, width = w.shape
    tokens, cols = wholes[0].shape[0], lines * share
    whole = pl.BlockSpec((tokens, width), lambda i: (0, 0))
    block = pl.BlockSpec((None, tokens, cols), lambda i: (i, 0, 0))
    return pl.pallas_call(
        kernel,
        grid=(steps,),
        in_specs=[whole] * len(wholes)
        + [block] * len(blocks)
        + [weight_spec(w, matrix) for matrix in (1, 2, 3)],
        out_specs=[block] * len(out_blocks) + [whole],
        out_shape=[jax.ShapeDtypeStruct((steps, tokens, cols), t) for t in out_blocks]
        + [jax.ShapeDtypeStruct((tokens, width), f32)],
        compiler_params=pltpu.CompilerParams(
            dimension_semantics=("arbitrary",), vmem_limit_bytes=40 * 1024 * 1024
        ),
        cost_estimate=pl.CostEstimate(
            flops=6 * tokens * steps * cols * width,
            bytes_accessed=6 * steps * cols * width,
            transcendentals=tokens * steps * cols,
        ),
    )(*wholes, *blocks, w, w, w)


def ffn_forward(m, h1, w):
    if w.ndim == 5:
        return ffn_call(ffn_forward_kernel, w, (m, h1), (), (f32, f32, bf16))
    gate, up = dot_nt(m, w[0]), dot_nt(m, w[1])
    act = (jax.nn.silu(gate) * up).astype(bf16)
    return gate, up, act, h1 + dot_nn(act, w[2])


def ffn_backward(eb, gate, up, w):
    if w.ndim == 5:
        return ffn_call(ffn_backward_kernel, w, (eb,), (gate, up), (bf16, bf16))
    da = dot_nt(eb, w[2])
    sig = jax.nn.sigmoid(gate)
    dgate = (da * up * sig * (1.0 + gate * (1.0 - sig))).astype(bf16)
    dup = (da * gate * sig).astype(bf16)
    return dgate, dup, dot_nn(dgate, w[0]) + dot_nn(dup, w[1])


def flip(x, bit):
    size = lax.axis_size("dp")
    return lax.ppermute(x, "dp", [(i, i ^ bit) for i in range(size)])


def gather_small(row):
    size = lax.axis_size("dp")
    me = lax.axis_index("dp")
    bit = 1
    while bit < size:
        other = flip(row, bit)
        high = (me & bit) != 0
        row = jnp.concatenate([jnp.where(high, other, row), jnp.where(high, row, other)])
        bit *= 2
    return row


def scatter_small(row):
    size = lax.axis_size("dp")
    me = lax.axis_index("dp")
    bit = size // 2
    while bit >= 1:
        half = row.shape[0] // 2
        low, top = row[:half], row[half:]
        high = (me & bit) != 0
        row = jnp.where(high, top, low) + flip(jnp.where(high, low, top), bit)
        bit //= 2
    return row


def grads_generic(pieces):
    n, dproj, o, dz, m, dgate, dup, eb, act = pieces
    attn = jnp.concatenate([dot_nn(dproj.T, n), dot_nn(o.T, dz)], axis=0)
    both = [
        lax.psum_scatter(g, "dp", scatter_dimension=0, tiled=True)
        for g in (attn, dot_nn(dgate.T, m), dot_nn(dup.T, m), dot_nn(act.T, eb))
    ]
    return both[0], jnp.stack(both[1:])


def z_pairs(x, pairs):
    return lax.ppermute(x, "dp", [(4 * a + i, 4 * b + i) for a, b in pairs for i in range(4)])


def inner_swap(x):
    return z_pairs(x, [(1, 2), (2, 1)])


def at(x, i):
    return lax.dynamic_index_in_dim(x, i, 0, keepdims=False)


def with_other(x, bit):
    return jnp.concatenate([x, flip(x, bit)], axis=0)


def cols_y(x, y):
    x = x.reshape(2, 2, *x.shape[1:])
    return jnp.concatenate([at(x, y), flip(at(x, 1 - y), Y_BIT)], axis=1)


def cols_core(x, core):
    return jnp.concatenate([at(x, core), flip(at(x, 1 - core), CORE_BIT)], axis=0)


def product(cols, rows):
    out = lax.dot_general(cols, rows, (((0,), (0,)), ((), ())), preferred_element_type=f32)
    return out.reshape(4, -1, rows.shape[1])


def direct_send(parts, z):
    size = 4
    received = []
    for k in (2, 1, 3):
        send = at(parts, (z + k) % size).astype(bf16)
        received.append(z_pairs(send, [(a, (a + k) % size) for a in range(size)]))
    return at(parts, z), received


def direct_total(own, received):
    return own + sum(r.astype(f32) for r in received)


def line_first(parts, z2):
    parts = parts.reshape(2, 2, *parts.shape[1:])
    far = at(parts, 1 - z2)
    return at(parts, z2), far + z_pairs(far.astype(bf16), [(0, 1), (3, 2)]).astype(f32)


def line_second(near, far):
    return near + inner_swap(far.astype(bf16)).astype(f32)


def line_third(near, z1):
    return at(near, z1) + flip(at(near, 1 - z1).astype(bf16), Z1_BIT).astype(f32)


tie = lax.optimization_barrier


def last_round(e, state, early, weights, tables, me):
    n, o, m, act = state[2], state[7], state[10], state[13]
    z, y, core = me // 4, (me >> 1) & 1, me & 1
    z2, z1 = z >> 1, z & 1
    m_all, n_all, act_c = early
    tokens, width = n.shape
    eb = e.astype(bf16)
    eb_y = with_other(eb, Y_BIT)
    dgate, dup, dm = backward_ffn(eb, state, weights)
    dgate, dup, dm, eb_y = tie((dgate, dup, dm, eb_y))
    gate_y = cols_y(dgate, y)
    up_y = cols_y(dup, y)
    eb_all = with_other(eb_y, CORE_BIT)
    dh1, dz, do, gain_two_grad = backward_mid(e, dm, state, weights)
    do, dz, eb_all, gate_y = tie((do, dz, eb_all, gate_y))
    down_near, down_far = line_first(product(act_c, eb_all), z2)
    gate_c = cols_core(gate_y, core)
    dz_y = with_other(dz, Y_BIT)
    dproj = backward_attention(do, state, tables)
    dproj, gate_c, dz_y, up_y, down_near, down_far = tie(
        (dproj, gate_c, dz_y, up_y, down_near, down_far)
    )
    gate_near, gate_far = line_first(product(gate_c, m_all), z2)
    down_near = line_second(down_near, down_far)
    up_c = cols_core(up_y, core)
    share = act_c.shape[1] // 4
    attn_cols = jnp.concatenate([dproj, o], axis=1).reshape(tokens, 4, 4, share)
    attn_cols = attn_cols.transpose(2, 0, 1, 3).reshape(4, tokens, 4 * share)
    attn_y = cols_y(attn_cols, y)
    dz_all = with_other(dz_y, CORE_BIT)
    du, gain_one_grad = backward_in(dproj, dh1, state, weights)
    gain_grad = jnp.concatenate([gain_one_grad, gain_two_grad])
    gain_grad, up_c, attn_y, dz_all, gate_near, gate_far = tie(
        (gain_grad, up_c, attn_y, dz_all, gate_near, gate_far)
    )
    up_own, up_received = direct_send(product(up_c, m_all), z)
    gate_near = line_second(gate_near, gate_far)
    attn_c = cols_core(attn_y, core)
    gain_grad = gain_grad + flip(gain_grad, CORE_BIT)
    gain_grad = gain_grad + flip(gain_grad, Y_BIT)
    owners = (jnp.arange(4, dtype=jnp.int32) * 4 + y * 2 + core).reshape(4, 1, 1)
    is_qkv = owners * share < QKV_COLS
    attn = jnp.where(is_qkv, product(attn_c, n_all), product(attn_c, dz_all))
    gain_rows = at(gain_grad.reshape(4, 4, -1).transpose(1, 0, 2), y * 2 + core)[:, None]
    gain_share = gain_rows.shape[-1]
    gain_rows = jnp.pad(gain_rows, ((0, 0), (0, EXTRA_ROWS - 1), (0, width - gain_share)))
    attn_own, attn_received = direct_send(jnp.concatenate([attn, gain_rows], axis=1), z)
    attn_received, up_received = tie((attn_received, up_received))
    down = line_third(down_near, z1)
    gate = line_third(gate_near, z1)
    up = direct_total(up_own, up_received)
    attn = direct_total(attn_own, attn_received)
    return (
        du,
        attn[:share],
        jnp.stack([gate, up, down]),
        attn[share : share + 1, :gain_share],
    )


def local(edge_data, segment_ids, attn_weight, ffn_weight, gains):
    micro = segment_ids.shape[0]
    leading = lax.axis_index("section") == 0
    tables = block_tables(segment_ids)
    block, width = edge_data.shape[2], edge_data.shape[3]
    x = edge_data[0].reshape(micro * block, width)
    planes = lax.axis_size("dp") == 16
    me = lax.axis_index("dp")
    attn_own = attn_weight[0].T
    ffn_own = ffn_weight[0].swapaxes(1, 2)
    share = attn_own.shape[0]
    if planes:
        own = jnp.concatenate([attn_own[None], ffn_own], axis=0).reshape(-1, width)
        everything = lax.all_gather(own, "dp", axis=0, tiled=True).reshape(4, 4, 4, share, width)
        attn_t = everything[:, :, 0].reshape(-1, width)
        ffn_t = everything
    else:
        attn_t = lax.all_gather(attn_own, "dp", axis=0, tiled=True)
        ffn_t = lax.all_gather(ffn_own, "dp", axis=1, tiled=True)
    gain_row = gather_small(gains[0]).astype(f32)
    weights = (
        attn_t[:QKV_COLS],
        attn_t[QKV_COLS:],
        ffn_t,
        gain_row[:width],
        gain_row[width:],
    )
    first, _ = forward(x, weights, tables)
    received = lax.ppermute(first.astype(bf16), "section", [(0, 1)])
    u = jnp.where(leading, x, received)
    out, state = forward(u, weights, tables)
    first_grad, _, _ = backward(x, state, weights, tables)
    first_grad = first_grad.astype(bf16)
    if planes:
        y, core = (me >> 1) & 1, me & 1
        n, m, act = state[2], state[10], state[13]
        early = (with_other(m, Y_BIT), with_other(n, Y_BIT), cols_y(act, y))
        first_grad, early = tie((first_grad, early))
        received = lax.ppermute(first_grad, "section", [(1, 0)])
        early = (
            with_other(early[0], CORE_BIT),
            with_other(early[1], CORE_BIT),
            cols_core(early[2], core),
        )
        received, early = tie((received, early))
        e = jnp.where(leading, received, x)
        du, attn_rows, ffn_rows, gain_shard = last_round(e, state, early, weights, tables, me)
    else:
        received = lax.ppermute(first_grad, "section", [(1, 0)])
        e = jnp.where(leading, received, x)
        du, pieces, gain_grad = backward(e, state, weights, tables)
        attn_rows, ffn_rows = grads_generic(pieces)
        gain_shard = scatter_small(gain_grad)[None]
    edge_out = jnp.where(leading, du, out).astype(bf16).reshape(micro, block, width)
    return (
        edge_out[None],
        attn_rows.T[None],
        ffn_rows.swapaxes(1, 2)[None],
        gain_shard,
    )


def solution(mesh):
    in_specs = (
        P("section", None, "dp", None),
        P(None, "dp"),
        P("section", None, "dp"),
        P("section", None, None, "dp"),
        P("section", "dp"),
    )
    out_specs = (
        P("section", None, "dp", None),
        P("section", None, "dp"),
        P("section", None, None, "dp"),
        P("section", "dp"),
    )
    return jax.shard_map(local, mesh=mesh, in_specs=in_specs, out_specs=out_specs, check_vma=False)
```

```python
import jax
import jax.numpy as jnp
from jax import lax
from jax.experimental import pallas as pl
from jax.experimental.pallas import tpu as pltpu
from jax.sharding import PartitionSpec as P

QUERY_HEADS = 15
KEY_VALUE_HEADS = 5
HEAD_SIZE = 64
GROUP = QUERY_HEADS // KEY_VALUE_HEADS
Q_COLS = QUERY_HEADS * HEAD_SIZE
KV_COLS = KEY_VALUE_HEADS * HEAD_SIZE
QKV_COLS = Q_COLS + 2 * KV_COLS

epsilon = 1e-05
theta_base = 100000.0
Z2_BIT, Z1_BIT, Y_BIT, CORE_BIT = 8, 4, 2, 1
EXTRA_ROWS = 8
bf16 = jnp.bfloat16
f32 = jnp.float32


def dot_nn(a, b):
    return lax.dot_general(a, b, (((1,), (0,)), ((), ())), preferred_element_type=f32)


def dot_nt(a, b):
    return lax.dot_general(a, b, (((1,), (1,)), ((), ())), preferred_element_type=f32)


def rope(rows, cosine, sine):
    half = rows.shape[-1] // 2
    a, b = rows[..., :half], rows[..., half:]
    return jnp.concatenate([a * cosine - b * sine, b * cosine + a * sine], axis=-1)


def block_tables(segments):
    micro, block_len = segments.shape
    offsets = jnp.arange(block_len, dtype=jnp.int32)
    same = segments[:, :, None] == segments[:, None, :]
    start = jnp.min(jnp.where(same, offsets, block_len), axis=-1)
    positions = (offsets - start).astype(f32).reshape(-1)
    half = HEAD_SIZE // 2
    frequency = theta_base ** (-(2.0 * jnp.arange(half, dtype=f32)) / HEAD_SIZE)
    angles = positions[:, None] * frequency
    allowed = same & (offsets[:, None] >= offsets[None, :])
    eye = jnp.eye(micro, dtype=bool)
    full = allowed[:, :, None, :] & eye[:, None, :, None]
    total = micro * block_len
    return jnp.cos(angles), jnp.sin(angles), full.reshape(total, total)


def scores_of(q, k, allowed):
    s = jnp.einsum("tgrd,ugd->grtu", q, k, preferred_element_type=f32) * HEAD_SIZE**-0.5
    return jnp.where(allowed, s, -1000000000.0)


def forward_attention(u, weights, tables):
    qkv_w, out_w, ffn_w, gain_one, gain_two = weights
    cosine, sine, allowed = tables
    tokens = u.shape[0]
    u = u.astype(f32)
    r1 = lax.rsqrt(jnp.mean(u * u, axis=-1, keepdims=True) + epsilon)
    n = (u * r1 * gain_one).astype(bf16)
    proj = dot_nt(n, qkv_w)
    q = rope(
        proj[:, :Q_COLS].reshape(tokens, KEY_VALUE_HEADS, GROUP, HEAD_SIZE),
        cosine[:, None, None, :],
        sine[:, None, None, :],
    ).astype(bf16)
    k = rope(
        proj[:, Q_COLS : Q_COLS + KV_COLS].reshape(tokens, KEY_VALUE_HEADS, HEAD_SIZE),
        cosine[:, None, :],
        sine[:, None, :],
    ).astype(bf16)
    v = proj[:, Q_COLS + KV_COLS :].reshape(tokens, KEY_VALUE_HEADS, HEAD_SIZE).astype(bf16)
    masked = scores_of(q, k, allowed)
    peak = jnp.max(masked, axis=-1, keepdims=True)
    lse = peak + jnp.log(jnp.sum(jnp.exp(masked - peak), axis=-1, keepdims=True))
    prob = jnp.exp(masked - lse).astype(bf16)
    o = jnp.einsum("grtu,ugd->tgrd", prob, v, preferred_element_type=f32)
    o = o.reshape(tokens, Q_COLS).astype(bf16)
    h1 = u + dot_nn(o, out_w)
    r2 = lax.rsqrt(jnp.mean(h1 * h1, axis=-1, keepdims=True) + epsilon)
    m = (h1 * r2 * gain_two).astype(bf16)
    return u, r1, n, q, k, v, lse, o, h1, r2, m


def forward(u, weights, tables):
    state = forward_attention(u, weights, tables)
    gate, up, act, out = ffn_forward(state[10], state[8], weights[2])
    return out, (*state, gate, up, act)


def norm_back(grad, rows, r, gain):
    scaled = grad * gain
    part = r * scaled - rows * (r * r * r) * jnp.mean(scaled * rows, axis=-1, keepdims=True)
    return part, jnp.sum(grad * rows * r, axis=0)


def backward_ffn(eb, state, weights):
    gate, up = state[11], state[12]
    return ffn_backward(eb, gate, up, weights[2])


def backward_mid(e, dm, state, weights):
    out_w, gain_two = weights[1], weights[4]
    h1, r2 = state[8], state[9]
    part, gain_two_grad = norm_back(dm, h1, r2, gain_two)
    dh1 = e.astype(f32) + part
    dz = dh1.astype(bf16)
    return dh1, dz, dot_nt(dz, out_w).astype(bf16), gain_two_grad


def backward_attention(do, state, tables):
    cosine, sine, allowed = tables
    q, k, v, lse = state[3:7]
    tokens = do.shape[0]
    do = do.reshape(tokens, KEY_VALUE_HEADS, GROUP, HEAD_SIZE)
    prob = jnp.exp(scores_of(q, k, allowed) - lse)
    dv = jnp.einsum("grtu,tgrd->ugd", prob.astype(bf16), do, preferred_element_type=f32)
    dp = jnp.einsum("tgrd,ugd->grtu", do, v, preferred_element_type=f32)
    ds = (prob * (dp - jnp.sum(dp * prob, axis=-1, keepdims=True))).astype(bf16)
    dq = jnp.einsum("grtu,ugd->tgrd", ds, k, preferred_element_type=f32) * HEAD_SIZE**-0.5
    dk = jnp.einsum("grtu,tgrd->ugd", ds, q, preferred_element_type=f32) * HEAD_SIZE**-0.5
    dq = rope(dq, cosine[:, None, None, :], -sine[:, None, None, :])
    dk = rope(dk, cosine[:, None, :], -sine[:, None, :])
    return jnp.concatenate(
        [dq.reshape(tokens, Q_COLS), dk.reshape(tokens, KV_COLS), dv.reshape(tokens, KV_COLS)],
        axis=1,
    ).astype(bf16)


def backward_in(dproj, dh1, state, weights):
    qkv_w, gain_one = weights[0], weights[3]
    u, r1 = state[0], state[1]
    part, gain_one_grad = norm_back(dot_nn(dproj, qkv_w), u, r1, gain_one)
    return dh1 + part, gain_one_grad


def backward(e, state, weights, tables):
    dgate, dup, dm = backward_ffn(e.astype(bf16), state, weights)
    dh1, dz, do, gain_two_grad = backward_mid(e, dm, state, weights)
    dproj = backward_attention(do, state, tables)
    du, gain_one_grad = backward_in(dproj, dh1, state, weights)
    pieces = (state[2], dproj, state[7], dz, state[10], dgate, dup, e.astype(bf16), state[13])
    return du, pieces, jnp.concatenate([gain_one_grad, gain_two_grad])


def ffn_forward_kernel(m_ref, h1_ref, wg_ref, wu_ref, wd_ref, gate_ref, up_ref, act_ref, out_ref):
    flat = lambda ref: ref[...].reshape(-1, ref.shape[-1])
    m = m_ref[...]
    gate = dot_nt(m, flat(wg_ref))
    up = dot_nt(m, flat(wu_ref))
    act = (gate * jax.nn.sigmoid(gate) * up).astype(bf16)
    gate_ref[...] = gate
    up_ref[...] = up
    act_ref[...] = act
    add = dot_nn(act, flat(wd_ref))

    @pl.when(pl.program_id(0) == 0)
    def _():
        out_ref[...] = h1_ref[...] + add

    @pl.when(pl.program_id(0) > 0)
    def _():
        out_ref[...] += add


def ffn_backward_kernel(
    eb_ref, gate_ref, up_ref, wg_ref, wu_ref, wd_ref, dgate_ref, dup_ref, dm_ref
):
    flat = lambda ref: ref[...].reshape(-1, ref.shape[-1])
    da = dot_nt(eb_ref[...], flat(wd_ref))
    gate = gate_ref[...]
    sig = jax.nn.sigmoid(gate)
    dgate = (da * up_ref[...] * sig * (1.0 + gate * (1.0 - sig))).astype(bf16)
    dup = (da * gate * sig).astype(bf16)
    dgate_ref[...] = dgate
    dup_ref[...] = dup
    add = dot_nn(dgate, flat(wg_ref)) + dot_nn(dup, flat(wu_ref))

    @pl.when(pl.program_id(0) == 0)
    def _():
        dm_ref[...] = add

    @pl.when(pl.program_id(0) > 0)
    def _():
        dm_ref[...] += add


def weight_spec(w, matrix):
    lines, _, _, share, width = w.shape
    return pl.BlockSpec((lines, None, None, share, width), lambda i: (0, i, matrix, 0, 0))


def ffn_call(kernel, w, wholes, blocks, out_blocks):
    lines, steps, _, share, width = w.shape
    tokens, cols = wholes[0].shape[0], lines * share
    whole = pl.BlockSpec((tokens, width), lambda i: (0, 0))
    block = pl.BlockSpec((None, tokens, cols), lambda i: (i, 0, 0))
    return pl.pallas_call(
        kernel,
        grid=(steps,),
        in_specs=[whole] * len(wholes)
        + [block] * len(blocks)
        + [weight_spec(w, matrix) for matrix in (1, 2, 3)],
        out_specs=[block] * len(out_blocks) + [whole],
        out_shape=[jax.ShapeDtypeStruct((steps, tokens, cols), t) for t in out_blocks]
        + [jax.ShapeDtypeStruct((tokens, width), f32)],
        compiler_params=pltpu.CompilerParams(
            dimension_semantics=("arbitrary",), vmem_limit_bytes=40 * 1024 * 1024
        ),
        cost_estimate=pl.CostEstimate(
            flops=6 * tokens * steps * cols * width,
            bytes_accessed=6 * steps * cols * width,
            transcendentals=tokens * steps * cols,
        ),
    )(*wholes, *blocks, w, w, w)


def ffn_forward(m, h1, w):
    if w.ndim == 5:
        return ffn_call(ffn_forward_kernel, w, (m, h1), (), (f32, f32, bf16))
    gate, up = dot_nt(m, w[0]), dot_nt(m, w[1])
    act = (jax.nn.silu(gate) * up).astype(bf16)
    return gate, up, act, h1 + dot_nn(act, w[2])


def ffn_backward(eb, gate, up, w):
    if w.ndim == 5:
        return ffn_call(ffn_backward_kernel, w, (eb,), (gate, up), (bf16, bf16))
    da = dot_nt(eb, w[2])
    sig = jax.nn.sigmoid(gate)
    dgate = (da * up * sig * (1.0 + gate * (1.0 - sig))).astype(bf16)
    dup = (da * gate * sig).astype(bf16)
    return dgate, dup, dot_nn(dgate, w[0]) + dot_nn(dup, w[1])


def flip(x, bit):
    size = lax.axis_size("dp")
    return lax.ppermute(x, "dp", [(i, i ^ bit) for i in range(size)])


def gather_small(row):
    size = lax.axis_size("dp")
    me = lax.axis_index("dp")
    bit = 1
    while bit < size:
        other = flip(row, bit)
        high = (me & bit) != 0
        row = jnp.concatenate([jnp.where(high, other, row), jnp.where(high, row, other)])
        bit *= 2
    return row


def scatter_small(row):
    size = lax.axis_size("dp")
    me = lax.axis_index("dp")
    bit = size // 2
    while bit >= 1:
        half = row.shape[0] // 2
        low, top = row[:half], row[half:]
        high = (me & bit) != 0
        row = jnp.where(high, top, low) + flip(jnp.where(high, low, top), bit)
        bit //= 2
    return row


def grads_generic(pieces):
    n, dproj, o, dz, m, dgate, dup, eb, act = pieces
    attn = jnp.concatenate([dot_nn(dproj.T, n), dot_nn(o.T, dz)], axis=0)
    both = [
        lax.psum_scatter(g, "dp", scatter_dimension=0, tiled=True)
        for g in (attn, dot_nn(dgate.T, m), dot_nn(dup.T, m), dot_nn(act.T, eb))
    ]
    return both[0], jnp.stack(both[1:])


def z_pairs(x, pairs):
    return lax.ppermute(x, "dp", [(4 * a + i, 4 * b + i) for a, b in pairs for i in range(4)])


def inner_swap(x):
    return z_pairs(x, [(1, 2), (2, 1)])


def at(x, i):
    return lax.dynamic_index_in_dim(x, i, 0, keepdims=False)


def with_other(x, bit):
    return jnp.concatenate([x, flip(x, bit)], axis=0)


def cols_y(x, y):
    x = x.reshape(2, 2, *x.shape[1:])
    return jnp.concatenate([at(x, y), flip(at(x, 1 - y), Y_BIT)], axis=1)


def cols_core(x, core):
    return jnp.concatenate([at(x, core), flip(at(x, 1 - core), CORE_BIT)], axis=0)


def product(cols, rows):
    out = lax.dot_general(cols, rows, (((0,), (0,)), ((), ())), preferred_element_type=f32)
    return out.reshape(4, -1, rows.shape[1])


LINE = 4


def direct_parts(parts, z):
    return at(parts, z), [at(parts, (z + k) % LINE).astype(bf16) for k in (2, 1, 3)]


def direct_send(sends):
    return [
        z_pairs(send, [(a, (a + k) % LINE) for a in range(LINE)])
        for k, send in zip((2, 1, 3), sends)
    ]


def direct_total(own, received):
    return own + sum(r.astype(f32) for r in received)


def line_first(parts, z2):
    parts = parts.reshape(2, 2, *parts.shape[1:])
    far = at(parts, 1 - z2)
    return at(parts, z2), far + z_pairs(far.astype(bf16), [(0, 1), (3, 2)]).astype(f32)


def line_second(near, far):
    return near + inner_swap(far.astype(bf16)).astype(f32)


def line_third(near, z1):
    return at(near, z1) + flip(at(near, 1 - z1).astype(bf16), Z1_BIT).astype(f32)


tie = lax.optimization_barrier


def middle_rounds(u, x, weights, tables, me):
    y, core = (me >> 1) & 1, me & 1
    state = forward_attention(u, weights, tables)
    n, m = state[2], state[10]
    gate, up, act, out = ffn_forward(m, state[8], weights[2])
    m_y, n_y = with_other(m, Y_BIT), with_other(n, Y_BIT)
    gate, up, act, out, m_y, n_y = tie((gate, up, act, out, m_y, n_y))
    state = (*state, gate, up, act)
    act_y = cols_y(act, y)
    m_all, n_all = with_other(m_y, CORE_BIT), with_other(n_y, CORE_BIT)
    _, _, dm = backward_ffn(x, state, weights)
    dm, act_y, m_all, n_all = tie((dm, act_y, m_all, n_all))
    act_c = cols_core(act_y, core)
    dh1, _, do, _ = backward_mid(x, dm, state, weights)
    dproj = backward_attention(do, state, tables)
    first_grad, _ = backward_in(dproj, dh1, state, weights)
    first_grad, act_c = tie((first_grad.astype(bf16), act_c))
    return out, state, first_grad, (m_all, n_all, act_c)


def last_round(e, state, early, weights, tables, me):
    o = state[7]
    z, y, core = me // 4, (me >> 1) & 1, me & 1
    z2, z1 = z >> 1, z & 1
    m_all, n_all, act_c = early
    tokens, width = o.shape[0], e.shape[1]
    share = act_c.shape[1] // 4
    eb = e.astype(bf16)
    eb_y = with_other(eb, Y_BIT)
    dgate, dup, dm = backward_ffn(eb, state, weights)
    dgate, dup, dm, eb_y = tie((dgate, dup, dm, eb_y))
    gate_y = cols_y(dgate, y)
    eb_all = with_other(eb_y, CORE_BIT)
    dh1, dz, do, gain_two_grad = backward_mid(e, dm, state, weights)
    do, dz, eb_all, dup = tie((do, dz, eb_all, dup))
    down_own, down_sends = direct_parts(product(act_c, eb_all), z)
    do, down_sends = tie((do, down_sends))
    down_two, down_one, down_three = direct_send(down_sends)
    gate_c = cols_core(gate_y, core)
    up_y = cols_y(dup, y)
    dproj = backward_attention(do, state, tables)
    dproj, gate_c, up_y, down_two = tie((dproj, gate_c, up_y, down_two))
    gate_near, gate_far = line_first(product(gate_c, m_all), z2)
    up_c = cols_core(up_y, core)
    attn_cols = jnp.concatenate([dproj, o], axis=1).reshape(tokens, 4, 4, share)
    attn_cols = attn_cols.transpose(2, 0, 1, 3).reshape(4, tokens, 4 * share)
    attn_y = cols_y(attn_cols, y)
    dz_y = with_other(dz, Y_BIT)
    gate_near, gate_far, up_c, attn_y, dz_y, down_one = tie(
        (gate_near, gate_far, up_c, attn_y, dz_y, down_one)
    )
    up_near, up_far = line_first(product(up_c, m_all), z2)
    gate_near = line_second(gate_near, gate_far)
    attn_c = cols_core(attn_y, core)
    dz_all = with_other(dz_y, CORE_BIT)
    du, gain_one_grad = backward_in(dproj, dh1, state, weights)
    gain_grad = jnp.concatenate([gain_one_grad, gain_two_grad])
    gain_grad = gain_grad + flip(gain_grad, CORE_BIT)
    gain_grad = gain_grad + flip(gain_grad, Y_BIT)
    attn_c, dz_all, gain_grad, up_near, up_far, gate_near, down_three = tie(
        (attn_c, dz_all, gain_grad, up_near, up_far, gate_near, down_three)
    )
    owners = (jnp.arange(4, dtype=jnp.int32) * 4 + y * 2 + core).reshape(4, 1, 1)
    is_qkv = owners * share < QKV_COLS
    attn = jnp.where(is_qkv, product(attn_c, n_all), product(attn_c, dz_all))
    gain_rows = at(gain_grad.reshape(4, 4, -1).transpose(1, 0, 2), y * 2 + core)[:, None]
    gain_share = gain_rows.shape[-1]
    gain_rows = jnp.pad(gain_rows, ((0, 0), (0, EXTRA_ROWS - 1), (0, width - gain_share)))
    attn_near, attn_far = line_first(jnp.concatenate([attn, gain_rows], axis=1), z2)
    up_near = line_second(up_near, up_far)
    gate = line_third(gate_near, z1)
    down = direct_total(down_own, (down_two, down_one, down_three))
    attn_near, attn_far, up_near, gate, down = tie((attn_near, attn_far, up_near, gate, down))
    attn_near = line_second(attn_near, attn_far)
    up = line_third(up_near, z1)
    attn = line_third(attn_near, z1)
    return (
        du,
        attn[:share],
        jnp.stack([gate, up, down]),
        attn[share : share + 1, :gain_share],
    )


def local(edge_data, segment_ids, attn_weight, ffn_weight, gains):
    micro = segment_ids.shape[0]
    leading = lax.axis_index("section") == 0
    tables = block_tables(segment_ids)
    block, width = edge_data.shape[2], edge_data.shape[3]
    x = edge_data[0].reshape(micro * block, width)
    planes = lax.axis_size("dp") == 16
    me = lax.axis_index("dp")
    attn_own = attn_weight[0].T
    ffn_own = ffn_weight[0].swapaxes(1, 2)
    share = attn_own.shape[0]
    if planes:
        own = jnp.concatenate([attn_own[None], ffn_own], axis=0).reshape(-1, width)
        everything = lax.all_gather(own, "dp", axis=0, tiled=True).reshape(4, 4, 4, share, width)
        attn_t = everything[:, :, 0].reshape(-1, width)
        ffn_t = everything
    else:
        attn_t = lax.all_gather(attn_own, "dp", axis=0, tiled=True)
        ffn_t = lax.all_gather(ffn_own, "dp", axis=1, tiled=True)
    gain_row = gather_small(gains[0]).astype(f32)
    weights = (
        attn_t[:QKV_COLS],
        attn_t[QKV_COLS:],
        ffn_t,
        gain_row[:width],
        gain_row[width:],
    )
    first, _ = forward(x, weights, tables)
    received = lax.ppermute(first.astype(bf16), "section", [(0, 1)])
    u = jnp.where(leading, x, received)
    if planes:
        out, state, first_grad, early = middle_rounds(u, x, weights, tables, me)
        received = lax.ppermute(first_grad, "section", [(1, 0)])
        e = jnp.where(leading, received, x)
        du, attn_rows, ffn_rows, gain_shard = last_round(e, state, early, weights, tables, me)
    else:
        out, state = forward(u, weights, tables)
        first_grad, _, _ = backward(x, state, weights, tables)
        received = lax.ppermute(first_grad.astype(bf16), "section", [(1, 0)])
        e = jnp.where(leading, received, x)
        du, pieces, gain_grad = backward(e, state, weights, tables)
        attn_rows, ffn_rows = grads_generic(pieces)
        gain_shard = scatter_small(gain_grad)[None]
    edge_out = jnp.where(leading, du, out).astype(bf16).reshape(micro, block, width)
    return (
        edge_out[None],
        attn_rows.T[None],
        ffn_rows.swapaxes(1, 2)[None],
        gain_shard,
    )


def solution(mesh):
    in_specs = (
        P("section", None, "dp", None),
        P(None, "dp"),
        P("section", None, "dp"),
        P("section", None, None, "dp"),
        P("section", "dp"),
    )
    out_specs = (
        P("section", None, "dp", None),
        P("section", None, "dp"),
        P("section", None, None, "dp"),
        P("section", "dp"),
    )
    return jax.shard_map(local, mesh=mesh, in_specs=in_specs, out_specs=out_specs, check_vma=False)
```

```python
import jax
import jax.numpy as jnp
from jax import lax
from jax.experimental import pallas as pl
from jax.experimental.pallas import tpu as pltpu
from jax.sharding import PartitionSpec as P

QUERY_HEADS = 15
KEY_VALUE_HEADS = 5
HEAD_SIZE = 64
GROUP = QUERY_HEADS // KEY_VALUE_HEADS
Q_COLS = QUERY_HEADS * HEAD_SIZE
KV_COLS = KEY_VALUE_HEADS * HEAD_SIZE
QKV_COLS = Q_COLS + 2 * KV_COLS

epsilon = 1e-05
theta_base = 100000.0
Z2_BIT, Z1_BIT, Y_BIT, CORE_BIT = 8, 4, 2, 1
EXTRA_ROWS = 8
bf16 = jnp.bfloat16
f32 = jnp.float32


def dot_nn(a, b):
    return lax.dot_general(a, b, (((1,), (0,)), ((), ())), preferred_element_type=f32)


def dot_nt(a, b):
    return lax.dot_general(a, b, (((1,), (1,)), ((), ())), preferred_element_type=f32)


def rope(rows, cosine, sine):
    half = rows.shape[-1] // 2
    a, b = rows[..., :half], rows[..., half:]
    return jnp.concatenate([a * cosine - b * sine, b * cosine + a * sine], axis=-1)


def block_tables(segments):
    micro, block_len = segments.shape
    offsets = jnp.arange(block_len, dtype=jnp.int32)
    same = segments[:, :, None] == segments[:, None, :]
    start = jnp.min(jnp.where(same, offsets, block_len), axis=-1)
    positions = (offsets - start).astype(f32).reshape(-1)
    half = HEAD_SIZE // 2
    frequency = theta_base ** (-(2.0 * jnp.arange(half, dtype=f32)) / HEAD_SIZE)
    angles = positions[:, None] * frequency
    allowed = same & (offsets[:, None] >= offsets[None, :])
    eye = jnp.eye(micro, dtype=bool)
    full = allowed[:, :, None, :] & eye[:, None, :, None]
    total = micro * block_len
    return jnp.cos(angles), jnp.sin(angles), full.reshape(total, total)


def scores_of(q, k, allowed):
    s = jnp.einsum("tgrd,ugd->grtu", q, k, preferred_element_type=f32) * HEAD_SIZE**-0.5
    return jnp.where(allowed, s, -1000000000.0)


def forward_attention(u, weights, tables):
    qkv_w, out_w, ffn_w, gain_one, gain_two = weights
    cosine, sine, allowed = tables
    tokens = u.shape[0]
    u = u.astype(f32)
    r1 = lax.rsqrt(jnp.mean(u * u, axis=-1, keepdims=True) + epsilon)
    n = (u * r1 * gain_one).astype(bf16)
    proj = dot_nt(n, qkv_w)
    q = rope(
        proj[:, :Q_COLS].reshape(tokens, KEY_VALUE_HEADS, GROUP, HEAD_SIZE),
        cosine[:, None, None, :],
        sine[:, None, None, :],
    ).astype(bf16)
    k = rope(
        proj[:, Q_COLS : Q_COLS + KV_COLS].reshape(tokens, KEY_VALUE_HEADS, HEAD_SIZE),
        cosine[:, None, :],
        sine[:, None, :],
    ).astype(bf16)
    v = proj[:, Q_COLS + KV_COLS :].reshape(tokens, KEY_VALUE_HEADS, HEAD_SIZE).astype(bf16)
    masked = scores_of(q, k, allowed)
    peak = jnp.max(masked, axis=-1, keepdims=True)
    lse = peak + jnp.log(jnp.sum(jnp.exp(masked - peak), axis=-1, keepdims=True))
    prob = jnp.exp(masked - lse).astype(bf16)
    o = jnp.einsum("grtu,ugd->tgrd", prob, v, preferred_element_type=f32)
    o = o.reshape(tokens, Q_COLS).astype(bf16)
    h1 = u + dot_nn(o, out_w)
    r2 = lax.rsqrt(jnp.mean(h1 * h1, axis=-1, keepdims=True) + epsilon)
    m = (h1 * r2 * gain_two).astype(bf16)
    return u, r1, n, q, k, v, lse, o, h1, r2, m


def forward(u, weights, tables):
    state = forward_attention(u, weights, tables)
    gate, up, act, out = ffn_forward(state[10], state[8], weights[2])
    return out, (*state, gate, up, act)


def norm_back(grad, rows, r, gain):
    scaled = grad * gain
    part = r * scaled - rows * (r * r * r) * jnp.mean(scaled * rows, axis=-1, keepdims=True)
    return part, jnp.sum(grad * rows * r, axis=0)


def backward_ffn(eb, state, weights):
    gate, up = state[11], state[12]
    return ffn_backward(eb, gate, up, weights[2])


def backward_mid(e, dm, state, weights):
    out_w, gain_two = weights[1], weights[4]
    h1, r2 = state[8], state[9]
    part, gain_two_grad = norm_back(dm, h1, r2, gain_two)
    dh1 = e.astype(f32) + part
    dz = dh1.astype(bf16)
    return dh1, dz, dot_nt(dz, out_w).astype(bf16), gain_two_grad


def backward_attention(do, state, tables):
    cosine, sine, allowed = tables
    q, k, v, lse = state[3:7]
    tokens = do.shape[0]
    do = do.reshape(tokens, KEY_VALUE_HEADS, GROUP, HEAD_SIZE)
    prob = jnp.exp(scores_of(q, k, allowed) - lse)
    dv = jnp.einsum("grtu,tgrd->ugd", prob.astype(bf16), do, preferred_element_type=f32)
    dp = jnp.einsum("tgrd,ugd->grtu", do, v, preferred_element_type=f32)
    ds = (prob * (dp - jnp.sum(dp * prob, axis=-1, keepdims=True))).astype(bf16)
    dq = jnp.einsum("grtu,ugd->tgrd", ds, k, preferred_element_type=f32) * HEAD_SIZE**-0.5
    dk = jnp.einsum("grtu,tgrd->ugd", ds, q, preferred_element_type=f32) * HEAD_SIZE**-0.5
    dq = rope(dq, cosine[:, None, None, :], -sine[:, None, None, :])
    dk = rope(dk, cosine[:, None, :], -sine[:, None, :])
    return jnp.concatenate(
        [dq.reshape(tokens, Q_COLS), dk.reshape(tokens, KV_COLS), dv.reshape(tokens, KV_COLS)],
        axis=1,
    ).astype(bf16)


def backward_in(dproj, dh1, state, weights):
    qkv_w, gain_one = weights[0], weights[3]
    u, r1 = state[0], state[1]
    part, gain_one_grad = norm_back(dot_nn(dproj, qkv_w), u, r1, gain_one)
    return dh1 + part, gain_one_grad


def backward(e, state, weights, tables):
    dgate, dup, dm = backward_ffn(e.astype(bf16), state, weights)
    dh1, dz, do, gain_two_grad = backward_mid(e, dm, state, weights)
    dproj = backward_attention(do, state, tables)
    du, gain_one_grad = backward_in(dproj, dh1, state, weights)
    pieces = (state[2], dproj, state[7], dz, state[10], dgate, dup, e.astype(bf16), state[13])
    return du, pieces, jnp.concatenate([gain_one_grad, gain_two_grad])


def ffn_forward_kernel(m_ref, h1_ref, wg_ref, wu_ref, wd_ref, gate_ref, up_ref, act_ref, out_ref):
    flat = lambda ref: ref[...].reshape(-1, ref.shape[-1])
    m = m_ref[...]
    gate = dot_nt(m, flat(wg_ref))
    up = dot_nt(m, flat(wu_ref))
    act = (gate * jax.nn.sigmoid(gate) * up).astype(bf16)
    gate_ref[...] = gate
    up_ref[...] = up
    act_ref[...] = act
    add = dot_nn(act, flat(wd_ref))

    @pl.when(pl.program_id(0) == 0)
    def _():
        out_ref[...] = h1_ref[...] + add

    @pl.when(pl.program_id(0) > 0)
    def _():
        out_ref[...] += add


def ffn_backward_kernel(
    eb_ref, gate_ref, up_ref, wg_ref, wu_ref, wd_ref, dgate_ref, dup_ref, dm_ref
):
    flat = lambda ref: ref[...].reshape(-1, ref.shape[-1])
    da = dot_nt(eb_ref[...], flat(wd_ref))
    gate = gate_ref[...]
    sig = jax.nn.sigmoid(gate)
    dgate = (da * up_ref[...] * sig * (1.0 + gate * (1.0 - sig))).astype(bf16)
    dup = (da * gate * sig).astype(bf16)
    dgate_ref[...] = dgate
    dup_ref[...] = dup
    add = dot_nn(dgate, flat(wg_ref)) + dot_nn(dup, flat(wu_ref))

    @pl.when(pl.program_id(0) == 0)
    def _():
        dm_ref[...] = add

    @pl.when(pl.program_id(0) > 0)
    def _():
        dm_ref[...] += add


def weight_spec(w, matrix):
    lines, _, _, share, width = w.shape
    return pl.BlockSpec((lines, None, None, share, width), lambda i: (0, i, matrix, 0, 0))


def ffn_call(kernel, w, wholes, blocks, out_blocks):
    lines, steps, _, share, width = w.shape
    tokens, cols = wholes[0].shape[0], lines * share
    whole = pl.BlockSpec((tokens, width), lambda i: (0, 0))
    block = pl.BlockSpec((None, tokens, cols), lambda i: (i, 0, 0))
    return pl.pallas_call(
        kernel,
        grid=(steps,),
        in_specs=[whole] * len(wholes)
        + [block] * len(blocks)
        + [weight_spec(w, matrix) for matrix in (1, 2, 3)],
        out_specs=[block] * len(out_blocks) + [whole],
        out_shape=[jax.ShapeDtypeStruct((steps, tokens, cols), t) for t in out_blocks]
        + [jax.ShapeDtypeStruct((tokens, width), f32)],
        compiler_params=pltpu.CompilerParams(
            dimension_semantics=("arbitrary",), vmem_limit_bytes=40 * 1024 * 1024
        ),
        cost_estimate=pl.CostEstimate(
            flops=6 * tokens * steps * cols * width,
            bytes_accessed=6 * steps * cols * width,
            transcendentals=tokens * steps * cols,
        ),
    )(*wholes, *blocks, w, w, w)


def ffn_forward(m, h1, w):
    if w.ndim == 5:
        return ffn_call(ffn_forward_kernel, w, (m, h1), (), (f32, f32, bf16))
    gate, up = dot_nt(m, w[0]), dot_nt(m, w[1])
    act = (jax.nn.silu(gate) * up).astype(bf16)
    return gate, up, act, h1 + dot_nn(act, w[2])


def ffn_backward(eb, gate, up, w):
    if w.ndim == 5:
        return ffn_call(ffn_backward_kernel, w, (eb,), (gate, up), (bf16, bf16))
    da = dot_nt(eb, w[2])
    sig = jax.nn.sigmoid(gate)
    dgate = (da * up * sig * (1.0 + gate * (1.0 - sig))).astype(bf16)
    dup = (da * gate * sig).astype(bf16)
    return dgate, dup, dot_nn(dgate, w[0]) + dot_nn(dup, w[1])


def flip(x, bit):
    size = lax.axis_size("dp")
    return lax.ppermute(x, "dp", [(i, i ^ bit) for i in range(size)])


def gather_small(row):
    size = lax.axis_size("dp")
    me = lax.axis_index("dp")
    bit = 1
    while bit < size:
        other = flip(row, bit)
        high = (me & bit) != 0
        row = jnp.concatenate([jnp.where(high, other, row), jnp.where(high, row, other)])
        bit *= 2
    return row


def scatter_small(row):
    size = lax.axis_size("dp")
    me = lax.axis_index("dp")
    bit = size // 2
    while bit >= 1:
        half = row.shape[0] // 2
        low, top = row[:half], row[half:]
        high = (me & bit) != 0
        row = jnp.where(high, top, low) + flip(jnp.where(high, low, top), bit)
        bit //= 2
    return row


def grads_generic(pieces):
    n, dproj, o, dz, m, dgate, dup, eb, act = pieces
    attn = jnp.concatenate([dot_nn(dproj.T, n), dot_nn(o.T, dz)], axis=0)
    both = [
        lax.psum_scatter(g, "dp", scatter_dimension=0, tiled=True)
        for g in (attn, dot_nn(dgate.T, m), dot_nn(dup.T, m), dot_nn(act.T, eb))
    ]
    return both[0], jnp.stack(both[1:])


def z_pairs(x, pairs):
    return lax.ppermute(x, "dp", [(4 * a + i, 4 * b + i) for a, b in pairs for i in range(4)])


def inner_swap(x):
    return z_pairs(x, [(1, 2), (2, 1)])


def at(x, i):
    return lax.dynamic_index_in_dim(x, i, 0, keepdims=False)


def with_other(x, bit):
    return jnp.concatenate([x, flip(x, bit)], axis=0)


def cols_y(x, y):
    x = x.reshape(2, 2, *x.shape[1:])
    return jnp.concatenate([at(x, y), flip(at(x, 1 - y), Y_BIT)], axis=1)


def cols_core(x, core):
    return at(x, core), flip(at(x, 1 - core), CORE_BIT)


def rows_core(x):
    return x, flip(x, CORE_BIT)


def product(cols, rows):
    out = sum(
        lax.dot_general(c, r, (((0,), (0,)), ((), ())), preferred_element_type=f32)
        for c, r in zip(cols, rows)
    )
    return out


def by_owner(parts):
    return parts.reshape(LINE, -1, parts.shape[-1])


LINE = 4
ORDER = (1, 2, 3)


def direct_parts(parts, z):
    return at(parts, z), [at(parts, (z + k) % LINE).astype(bf16) for k in ORDER]


def direct_send(sends):
    return [
        z_pairs(send, [(a, (a + k) % LINE) for a in range(LINE)])
        for k, send in zip(ORDER, sends)
    ]


def direct_total(own, received):
    return own + sum(r.astype(f32) for r in received)


def pair_first(parts, z1):
    parts = parts.reshape(2, 2, *parts.shape[1:]).swapaxes(0, 1)
    return at(parts, z1), flip(at(parts, 1 - z1).astype(bf16), Z1_BIT)


def pair_second(own, received, z2):
    total = own + received.astype(f32)
    return at(total, z2) + flip(at(total, 1 - z2).astype(bf16), Z2_BIT).astype(f32)


tie = lax.optimization_barrier


def middle_rounds(u, x, weights, tables, me):
    y, core = (me >> 1) & 1, me & 1
    state = forward_attention(u, weights, tables)
    n, m = state[2], state[10]
    gate, up, act, out = ffn_forward(m, state[8], weights[2])
    m_y, n_y = with_other(m, Y_BIT), with_other(n, Y_BIT)
    gate, up, act, out, m_y, n_y = tie((gate, up, act, out, m_y, n_y))
    state = (*state, gate, up, act)
    act_y = cols_y(act, y)
    m_all, n_all = rows_core(m_y), rows_core(n_y)
    _, _, dm = backward_ffn(x, state, weights)
    dm, act_y, m_all, n_all = tie((dm, act_y, m_all, n_all))
    act_c = cols_core(act_y, core)
    dh1, _, do, _ = backward_mid(x, dm, state, weights)
    dproj = backward_attention(do, state, tables)
    first_grad, _ = backward_in(dproj, dh1, state, weights)
    first_grad, act_c = tie((first_grad.astype(bf16), act_c))
    return out, state, first_grad, (m_all, n_all, act_c)


def last_round(e, state, early, weights, tables, me):
    o = state[7]
    z, y, core = me // 4, (me >> 1) & 1, me & 1
    z2, z1 = z >> 1, z & 1
    m_all, n_all, act_c = early
    tokens, width = o.shape[0], e.shape[1]
    share = act_c[0].shape[1] // LINE
    eb = e.astype(bf16)
    eb_y = with_other(eb, Y_BIT)
    dgate, dup, dm = backward_ffn(eb, state, weights)
    dgate, dup, dm, eb_y = tie((dgate, dup, dm, eb_y))
    eb_all = rows_core(eb_y)
    gate_y = cols_y(dgate, y)
    dh1, dz, do, gain_two_grad = backward_mid(e, dm, state, weights)
    do, dz, eb_all, dup = tie((do, dz, eb_all, dup))
    down_own, down_sends = direct_parts(by_owner(product(act_c, eb_all)), z)
    do, gate_y, down_sends = tie((do, gate_y, down_sends))
    down_one, down_two, down_three = direct_send(down_sends)
    gate_c = cols_core(gate_y, core)
    up_y = cols_y(dup, y)
    dproj = backward_attention(do, state, tables)
    dproj, gate_c, up_y, down_one = tie((dproj, gate_c, up_y, down_one))
    gate_own, gate_received = pair_first(by_owner(product(gate_c, m_all)), z1)
    up_c = cols_core(up_y, core)
    dz_y = with_other(dz, Y_BIT)
    attn_cols = jnp.concatenate([dproj, o], axis=1).reshape(tokens, 4, 4, share)
    attn_cols = attn_cols.transpose(2, 0, 1, 3).reshape(4, tokens, 4 * share)
    attn_y = cols_y(attn_cols, y)
    dproj, up_c, dz_y, attn_y, down_three = tie((dproj, up_c, dz_y, attn_y, down_three))
    up_own, up_received = pair_first(by_owner(product(up_c, m_all)), z1)
    attn_c = cols_core(attn_y, core)
    dz_all = rows_core(dz_y)
    du, gain_one_grad = backward_in(dproj, dh1, state, weights)
    gain_grad = jnp.concatenate([gain_one_grad, gain_two_grad])
    gain_grad = gain_grad + flip(gain_grad, CORE_BIT)
    gain_grad = gain_grad + flip(gain_grad, Y_BIT)
    gain_grad, attn_c, dz_all, gate_own, gate_received, down_two = tie(
        (gain_grad, attn_c, dz_all, gate_own, gate_received, down_two)
    )
    qkv_owners = QKV_COLS // share
    from_n = product([c[:, : -(-qkv_owners // 4) * share] for c in attn_c], n_all)
    from_dz = product([c[:, qkv_owners // 4 * share :] for c in attn_c], dz_all)
    shared = qkv_owners // 4 * share
    mixed = -(-qkv_owners // 4) * share - shared
    is_qkv = qkv_owners // 4 * 4 + y * 2 + core < qkv_owners
    both = jnp.where(is_qkv, from_n[shared:], from_dz[:mixed])
    attn = by_owner(jnp.concatenate([from_n[:shared], both, from_dz[mixed:]], axis=0))
    gain_rows = at(gain_grad.reshape(4, 4, -1).transpose(1, 0, 2), y * 2 + core)[:, None]
    gain_share = gain_rows.shape[-1]
    gain_rows = jnp.pad(gain_rows, ((0, 0), (0, EXTRA_ROWS - 1), (0, width - gain_share)))
    attn_own, attn_sends = direct_parts(jnp.concatenate([attn, gain_rows], axis=1), z)
    attn_received = direct_send(attn_sends)
    down_received = (down_one, down_two, down_three)
    gate = pair_second(gate_own, gate_received, z2)
    up = pair_second(up_own, up_received, z2)
    down = direct_total(down_own, down_received)
    attn = direct_total(attn_own, attn_received)
    return (
        du,
        attn[:share],
        jnp.stack([gate, up, down]),
        attn[share : share + 1, :gain_share],
    )


def local(edge_data, segment_ids, attn_weight, ffn_weight, gains):
    micro = segment_ids.shape[0]
    leading = lax.axis_index("section") == 0
    tables = block_tables(segment_ids)
    block, width = edge_data.shape[2], edge_data.shape[3]
    x = edge_data[0].reshape(micro * block, width)
    planes = lax.axis_size("dp") == 16
    me = lax.axis_index("dp")
    attn_own = attn_weight[0].T
    ffn_own = ffn_weight[0].swapaxes(1, 2)
    share = attn_own.shape[0]
    if planes:
        own = jnp.concatenate([attn_own[None], ffn_own], axis=0).reshape(-1, width)
        everything = lax.all_gather(own, "dp", axis=0, tiled=True).reshape(4, 4, 4, share, width)
        attn_t = everything[:, :, 0].reshape(-1, width)
        ffn_t = everything
    else:
        attn_t = lax.all_gather(attn_own, "dp", axis=0, tiled=True)
        ffn_t = lax.all_gather(ffn_own, "dp", axis=1, tiled=True)
    gain_row = gather_small(gains[0]).astype(f32)
    weights = (
        attn_t[:QKV_COLS],
        attn_t[QKV_COLS:],
        ffn_t,
        gain_row[:width],
        gain_row[width:],
    )
    first, _ = forward(x, weights, tables)
    received = lax.ppermute(first.astype(bf16), "section", [(0, 1)])
    u = jnp.where(leading, x, received)
    if planes:
        out, state, first_grad, early = middle_rounds(u, x, weights, tables, me)
        received = lax.ppermute(first_grad, "section", [(1, 0)])
        e = jnp.where(leading, received, x)
        du, attn_rows, ffn_rows, gain_shard = last_round(e, state, early, weights, tables, me)
    else:
        out, state = forward(u, weights, tables)
        first_grad, _, _ = backward(x, state, weights, tables)
        received = lax.ppermute(first_grad.astype(bf16), "section", [(1, 0)])
        e = jnp.where(leading, received, x)
        du, pieces, gain_grad = backward(e, state, weights, tables)
        attn_rows, ffn_rows = grads_generic(pieces)
        gain_shard = scatter_small(gain_grad)[None]
    edge_out = jnp.where(leading, du, out).astype(bf16).reshape(micro, block, width)
    return (
        edge_out[None],
        attn_rows.T[None],
        ffn_rows.swapaxes(1, 2)[None],
        gain_shard,
    )


def solution(mesh):
    in_specs = (
        P("section", None, "dp", None),
        P(None, "dp"),
        P("section", None, "dp"),
        P("section", None, None, "dp"),
        P("section", "dp"),
    )
    out_specs = (
        P("section", None, "dp", None),
        P("section", None, "dp"),
        P("section", None, None, "dp"),
        P("section", "dp"),
    )
    return jax.shard_map(local, mesh=mesh, in_specs=in_specs, out_specs=out_specs, check_vma=False)
```

```python
import jax
import jax.numpy as jnp
from jax import lax
from jax.experimental import pallas as pl
from jax.experimental.pallas import tpu as pltpu
from jax.sharding import PartitionSpec as P

QUERY_HEADS = 15
KEY_VALUE_HEADS = 5
HEAD_SIZE = 64
GROUP = QUERY_HEADS // KEY_VALUE_HEADS
Q_COLS = QUERY_HEADS * HEAD_SIZE
KV_COLS = KEY_VALUE_HEADS * HEAD_SIZE
QKV_COLS = Q_COLS + 2 * KV_COLS

epsilon = 1e-05
theta_base = 100000.0
Z2_BIT, Z1_BIT, Y_BIT, CORE_BIT = 8, 4, 2, 1
EXTRA_ROWS = 8
bf16 = jnp.bfloat16
f32 = jnp.float32


def dot_nn(a, b):
    return lax.dot_general(a, b, (((1,), (0,)), ((), ())), preferred_element_type=f32)


def dot_nt(a, b):
    return lax.dot_general(a, b, (((1,), (1,)), ((), ())), preferred_element_type=f32)


def rope(rows, cosine, sine):
    half = rows.shape[-1] // 2
    a, b = rows[..., :half], rows[..., half:]
    return jnp.concatenate([a * cosine - b * sine, b * cosine + a * sine], axis=-1)


def block_tables(segments):
    micro, block_len = segments.shape
    offsets = jnp.arange(block_len, dtype=jnp.int32)
    same = segments[:, :, None] == segments[:, None, :]
    start = jnp.min(jnp.where(same, offsets, block_len), axis=-1)
    positions = (offsets - start).astype(f32).reshape(-1)
    half = HEAD_SIZE // 2
    frequency = theta_base ** (-(2.0 * jnp.arange(half, dtype=f32)) / HEAD_SIZE)
    angles = positions[:, None] * frequency
    allowed = same & (offsets[:, None] >= offsets[None, :])
    eye = jnp.eye(micro, dtype=bool)
    full = allowed[:, :, None, :] & eye[:, None, :, None]
    total = micro * block_len
    return jnp.cos(angles), jnp.sin(angles), full.reshape(total, total)


def scores_of(q, k, allowed):
    s = jnp.einsum("tgrd,ugd->grtu", q, k, preferred_element_type=f32) * HEAD_SIZE**-0.5
    return jnp.where(allowed, s, -1000000000.0)


def forward_attention(u, weights, tables):
    qkv_w, out_w, ffn_w, gain_one, gain_two = weights
    cosine, sine, allowed = tables
    tokens = u.shape[0]
    u = u.astype(f32)
    r1 = lax.rsqrt(jnp.mean(u * u, axis=-1, keepdims=True) + epsilon)
    n = (u * r1 * gain_one).astype(bf16)
    proj = dot_nt(n, qkv_w)
    q = rope(
        proj[:, :Q_COLS].reshape(tokens, KEY_VALUE_HEADS, GROUP, HEAD_SIZE),
        cosine[:, None, None, :],
        sine[:, None, None, :],
    ).astype(bf16)
    k = rope(
        proj[:, Q_COLS : Q_COLS + KV_COLS].reshape(tokens, KEY_VALUE_HEADS, HEAD_SIZE),
        cosine[:, None, :],
        sine[:, None, :],
    ).astype(bf16)
    v = proj[:, Q_COLS + KV_COLS :].reshape(tokens, KEY_VALUE_HEADS, HEAD_SIZE).astype(bf16)
    masked = scores_of(q, k, allowed)
    peak = jnp.max(masked, axis=-1, keepdims=True)
    lse = peak + jnp.log(jnp.sum(jnp.exp(masked - peak), axis=-1, keepdims=True))
    prob = jnp.exp(masked - lse).astype(bf16)
    o = jnp.einsum("grtu,ugd->tgrd", prob, v, preferred_element_type=f32)
    o = o.reshape(tokens, Q_COLS).astype(bf16)
    h1 = u + dot_nn(o, out_w)
    r2 = lax.rsqrt(jnp.mean(h1 * h1, axis=-1, keepdims=True) + epsilon)
    m = (h1 * r2 * gain_two).astype(bf16)
    return u, r1, n, q, k, v, lse, o, h1, r2, m


def forward(u, weights, tables):
    state = forward_attention(u, weights, tables)
    gate, up, act, out = ffn_forward(state[10], state[8], weights[2])
    return out, (*state, gate, up, act)


def norm_back(grad, rows, r, gain):
    scaled = grad * gain
    part = r * scaled - rows * (r * r * r) * jnp.mean(scaled * rows, axis=-1, keepdims=True)
    return part, jnp.sum(grad * rows * r, axis=0)


def backward_ffn(eb, state, weights):
    gate, up = state[11], state[12]
    return ffn_backward(eb, gate, up, weights[2])


def backward_mid(e, dm, state, weights):
    out_w, gain_two = weights[1], weights[4]
    h1, r2 = state[8], state[9]
    part, gain_two_grad = norm_back(dm, h1, r2, gain_two)
    dh1 = e.astype(f32) + part
    dz = dh1.astype(bf16)
    return dh1, dz, dot_nt(dz, out_w).astype(bf16), gain_two_grad


def backward_attention(do, state, tables):
    cosine, sine, allowed = tables
    q, k, v, lse = state[3:7]
    tokens = do.shape[0]
    do = do.reshape(tokens, KEY_VALUE_HEADS, GROUP, HEAD_SIZE)
    prob = jnp.exp(scores_of(q, k, allowed) - lse)
    dv = jnp.einsum("grtu,tgrd->ugd", prob.astype(bf16), do, preferred_element_type=f32)
    dp = jnp.einsum("tgrd,ugd->grtu", do, v, preferred_element_type=f32)
    ds = (prob * (dp - jnp.sum(dp * prob, axis=-1, keepdims=True))).astype(bf16)
    dq = jnp.einsum("grtu,ugd->tgrd", ds, k, preferred_element_type=f32) * HEAD_SIZE**-0.5
    dk = jnp.einsum("grtu,tgrd->ugd", ds, q, preferred_element_type=f32) * HEAD_SIZE**-0.5
    dq = rope(dq, cosine[:, None, None, :], -sine[:, None, None, :])
    dk = rope(dk, cosine[:, None, :], -sine[:, None, :])
    return jnp.concatenate(
        [dq.reshape(tokens, Q_COLS), dk.reshape(tokens, KV_COLS), dv.reshape(tokens, KV_COLS)],
        axis=1,
    ).astype(bf16)


def backward_in(dproj, dh1, state, weights):
    qkv_w, gain_one = weights[0], weights[3]
    u, r1 = state[0], state[1]
    part, gain_one_grad = norm_back(dot_nn(dproj, qkv_w), u, r1, gain_one)
    return dh1 + part, gain_one_grad


def backward(e, state, weights, tables):
    dgate, dup, dm = backward_ffn(e.astype(bf16), state, weights)
    dh1, dz, do, gain_two_grad = backward_mid(e, dm, state, weights)
    dproj = backward_attention(do, state, tables)
    du, gain_one_grad = backward_in(dproj, dh1, state, weights)
    pieces = (state[2], dproj, state[7], dz, state[10], dgate, dup, e.astype(bf16), state[13])
    return du, pieces, jnp.concatenate([gain_one_grad, gain_two_grad])


def ffn_forward_kernel(m_ref, h1_ref, wg_ref, wu_ref, wd_ref, gate_ref, up_ref, act_ref, out_ref):
    flat = lambda ref: ref[...].reshape(-1, ref.shape[-1])
    m = m_ref[...]
    gate = dot_nt(m, flat(wg_ref))
    up = dot_nt(m, flat(wu_ref))
    act = (gate * jax.nn.sigmoid(gate) * up).astype(bf16)
    gate_ref[...] = gate
    up_ref[...] = up
    act_ref[...] = act
    add = dot_nn(act, flat(wd_ref))

    @pl.when(pl.program_id(0) == 0)
    def _():
        out_ref[...] = h1_ref[...] + add

    @pl.when(pl.program_id(0) > 0)
    def _():
        out_ref[...] += add


def ffn_backward_kernel(
    eb_ref, gate_ref, up_ref, wg_ref, wu_ref, wd_ref, dgate_ref, dup_ref, dm_ref
):
    flat = lambda ref: ref[...].reshape(-1, ref.shape[-1])
    da = dot_nt(eb_ref[...], flat(wd_ref))
    gate = gate_ref[...]
    sig = jax.nn.sigmoid(gate)
    dgate = (da * up_ref[...] * sig * (1.0 + gate * (1.0 - sig))).astype(bf16)
    dup = (da * gate * sig).astype(bf16)
    dgate_ref[...] = dgate
    dup_ref[...] = dup
    add = dot_nn(dgate, flat(wg_ref)) + dot_nn(dup, flat(wu_ref))

    @pl.when(pl.program_id(0) == 0)
    def _():
        dm_ref[...] = add

    @pl.when(pl.program_id(0) > 0)
    def _():
        dm_ref[...] += add


def weight_spec(w, matrix):
    lines, _, _, share, width = w.shape
    return pl.BlockSpec((lines, None, None, share, width), lambda i: (0, i, matrix, 0, 0))


def ffn_call(kernel, w, wholes, blocks, out_blocks):
    lines, steps, _, share, width = w.shape
    tokens, cols = wholes[0].shape[0], lines * share
    whole = pl.BlockSpec((tokens, width), lambda i: (0, 0))
    block = pl.BlockSpec((None, tokens, cols), lambda i: (i, 0, 0))
    return pl.pallas_call(
        kernel,
        grid=(steps,),
        in_specs=[whole] * len(wholes)
        + [block] * len(blocks)
        + [weight_spec(w, matrix) for matrix in (1, 2, 3)],
        out_specs=[block] * len(out_blocks) + [whole],
        out_shape=[jax.ShapeDtypeStruct((steps, tokens, cols), t) for t in out_blocks]
        + [jax.ShapeDtypeStruct((tokens, width), f32)],
        compiler_params=pltpu.CompilerParams(
            dimension_semantics=("arbitrary",), vmem_limit_bytes=40 * 1024 * 1024
        ),
        cost_estimate=pl.CostEstimate(
            flops=6 * tokens * steps * cols * width,
            bytes_accessed=6 * steps * cols * width,
            transcendentals=tokens * steps * cols,
        ),
    )(*wholes, *blocks, w, w, w)


def ffn_forward(m, h1, w):
    if w.ndim == 5:
        return ffn_call(ffn_forward_kernel, w, (m, h1), (), (f32, f32, bf16))
    gate, up = dot_nt(m, w[0]), dot_nt(m, w[1])
    act = (jax.nn.silu(gate) * up).astype(bf16)
    return gate, up, act, h1 + dot_nn(act, w[2])


def ffn_backward(eb, gate, up, w):
    if w.ndim == 5:
        return ffn_call(ffn_backward_kernel, w, (eb,), (gate, up), (bf16, bf16))
    da = dot_nt(eb, w[2])
    sig = jax.nn.sigmoid(gate)
    dgate = (da * up * sig * (1.0 + gate * (1.0 - sig))).astype(bf16)
    dup = (da * gate * sig).astype(bf16)
    return dgate, dup, dot_nn(dgate, w[0]) + dot_nn(dup, w[1])


def flip(x, bit):
    size = lax.axis_size("dp")
    return lax.ppermute(x, "dp", [(i, i ^ bit) for i in range(size)])


def gather_small(row):
    size = lax.axis_size("dp")
    me = lax.axis_index("dp")
    bit = 1
    while bit < size:
        other = flip(row, bit)
        high = (me & bit) != 0
        row = jnp.concatenate([jnp.where(high, other, row), jnp.where(high, row, other)])
        bit *= 2
    return row


def scatter_small(row):
    size = lax.axis_size("dp")
    me = lax.axis_index("dp")
    bit = size // 2
    while bit >= 1:
        half = row.shape[0] // 2
        low, top = row[:half], row[half:]
        high = (me & bit) != 0
        row = jnp.where(high, top, low) + flip(jnp.where(high, low, top), bit)
        bit //= 2
    return row


def grads_generic(pieces):
    n, dproj, o, dz, m, dgate, dup, eb, act = pieces
    attn = jnp.concatenate([dot_nn(dproj.T, n), dot_nn(o.T, dz)], axis=0)
    both = [
        lax.psum_scatter(g, "dp", scatter_dimension=0, tiled=True)
        for g in (attn, dot_nn(dgate.T, m), dot_nn(dup.T, m), dot_nn(act.T, eb))
    ]
    return both[0], jnp.stack(both[1:])


def z_pairs(x, pairs):
    return lax.ppermute(x, "dp", [(4 * a + i, 4 * b + i) for a, b in pairs for i in range(4)])


def inner_swap(x):
    return z_pairs(x, [(1, 2), (2, 1)])


def at(x, i):
    return lax.dynamic_index_in_dim(x, i, 0, keepdims=False)


def rows_of_plane(x):
    x_y = flip(x, Y_BIT)
    return x, x_y, flip(x, CORE_BIT), flip(x_y, CORE_BIT)


def cols_y(x, y):
    x = x.reshape(2, 2, *x.shape[1:])
    return flip(at(x, 1 - y), Y_BIT)


def cols_core(x, x_y, y, core):
    other = 1 - core
    return flip(jnp.stack([at(x, 2 * y + other), at(x_y, other)]), CORE_BIT)


def plane_kernel(n_rows, split, n_own, picks_ref, *refs):
    cols_ref, y_ref, core_ref = refs[:3]
    rows = [
        jnp.concatenate([r[...] for r in refs[3 + 4 * i : 7 + 4 * i]], axis=0) for i in range(n_rows)
    ]
    rest = refs[3 + 4 * n_rows :]
    extra_ref = rest[0] if n_rows == 2 else None
    outs, total = rest[n_rows - 1 : -1], rest[-1]
    cols = jnp.concatenate(
        [cols_ref[picks_ref[0]], y_ref[picks_ref[1]], core_ref[0], core_ref[1]], axis=0
    )
    share = total.shape[0] // LINE

    def dot(c, r):
        return lax.dot_general(c, r, (((0,), (0,)), ((), ())), preferred_element_type=f32)

    if n_rows == 1:
        total[...] = dot(cols, rows[0])
    else:
        low, top = split
        total[...] = dot(cols, rows[1])
        first = dot(cols, rows[0])
        total[: low * share] = first[: low * share]
        if top > low:

            @pl.when(picks_ref[2] > 0)
            def _():
                total[low * share : top * share] = first[low * share : top * share]

    slot = 3
    for number, ref in enumerate(outs):
        for i in range(ref.shape[0]):
            pick = picks_ref[slot]
            slot += 1
            block = total[pl.ds(pl.multiple_of(pick * share, 8), share)]
            ref[i, :share] = block.astype(ref.dtype)
            if extra_ref is not None:
                ref[i, share:] = extra_ref[pick].astype(ref.dtype)


def plane_product(cols, x_y, x_core, rows, picks, out_counts, split=None, extra=None):
    blocks, tokens, width_cols = cols.shape
    share, width = width_cols // LINE, rows[0][0].shape[1]
    tall = share + (0 if extra is None else extra.shape[1])
    operands = [cols, x_y, x_core, *[r for chunk in rows for r in chunk]]
    if extra is not None:
        operands.append(extra)
    whole = lambda v: pl.BlockSpec(v.shape, lambda i, picks, n=v.ndim: (0,) * n)
    shapes = [
        jax.ShapeDtypeStruct((count, tall, width), f32 if i == 0 else bf16)
        for i, count in enumerate(out_counts)
    ]
    kernel = lambda *refs: plane_kernel(len(rows), split, out_counts[0], *refs)
    return pl.pallas_call(
        kernel,
        grid_spec=pltpu.PrefetchScalarGridSpec(
            num_scalar_prefetch=1,
            grid=(1,),
            in_specs=[whole(v) for v in operands],
            out_specs=[whole(v) for v in shapes],
            scratch_shapes=[pltpu.VMEM((LINE * share, width), f32)],
        ),
        out_shape=shapes,
        compiler_params=pltpu.CompilerParams(
            dimension_semantics=("arbitrary",), vmem_limit_bytes=32 * 1024 * 1024
        ),
        cost_estimate=pl.CostEstimate(
            flops=8 * tokens * width_cols * width * len(rows),
            bytes_accessed=8 * tokens * (width_cols + width) + 8 * width_cols * width,
            transcendentals=0,
        ),
    )(jnp.stack([jnp.asarray(p, jnp.int32) for p in picks]), *operands)


LINE = 4
ORDER = (1, 2, 3)


def direct_send(sends):
    return [
        z_pairs(send[0], [(a, (a + k) % LINE) for a in range(LINE)])
        for k, send in zip(ORDER, sends)
    ]


def direct_total(own, received):
    return own + sum(r.astype(f32) for r in received)


def pair_second(own, received, z2):
    total = own + received.astype(f32)
    return at(total, z2) + flip(at(total, 1 - z2).astype(bf16), Z2_BIT).astype(f32)


tie = lax.optimization_barrier


def middle_rounds(u, x, weights, tables, me):
    y, core = (me >> 1) & 1, me & 1
    state = forward_attention(u, weights, tables)
    n, m = state[2], state[10]
    gate, up, act, out = ffn_forward(m, state[8], weights[2])
    m_y, n_y = flip(m, Y_BIT), flip(n, Y_BIT)
    gate, up, act, out, m_y, n_y = tie((gate, up, act, out, m_y, n_y))
    state = (*state, gate, up, act)
    act_y = cols_y(act, y)
    m_all = (m, m_y, flip(m, CORE_BIT), flip(m_y, CORE_BIT))
    n_all = (n, n_y, flip(n, CORE_BIT), flip(n_y, CORE_BIT))
    _, _, dm = backward_ffn(x, state, weights)
    dm, act_y, m_all, n_all = tie((dm, act_y, m_all, n_all))
    act_c = (act, act_y, cols_core(act, act_y, y, core))
    dh1, _, do, _ = backward_mid(x, dm, state, weights)
    dproj = backward_attention(do, state, tables)
    first_grad, _ = backward_in(dproj, dh1, state, weights)
    first_grad, act_c = tie((first_grad.astype(bf16), act_c))
    return out, state, first_grad, (m_all, n_all, act_c)


def last_round(e, state, early, weights, tables, me):
    o = state[7]
    z, y, core = me // 4, (me >> 1) & 1, me & 1
    z2, z1 = z >> 1, z & 1
    m_all, n_all, act_c = early
    tokens, width = o.shape[0], e.shape[1]
    share = act_c[0].shape[2] // LINE
    here = (2 * y + core, core)
    others = [(z + k) % LINE for k in ORDER]
    pairs = (z1, 2 + z1, 1 - z1, 3 - z1)
    eb = e.astype(bf16)
    eb_y, eb_c = flip(eb, Y_BIT), flip(eb, CORE_BIT)
    dgate, dup, dm = backward_ffn(eb, state, weights)
    dgate, dup, dm, eb_y, eb_c = tie((dgate, dup, dm, eb_y, eb_c))
    eb_all = (eb, eb_y, eb_c, flip(eb_y, CORE_BIT))
    gate_y = cols_y(dgate, y)
    dh1, dz, do, gain_two_grad = backward_mid(e, dm, state, weights)
    do, dz, eb_all, dup = tie((do, dz, eb_all, dup))
    down_own, *down_sends = plane_product(*act_c, [eb_all], (*here, 0, z, *others), (1, 1, 1, 1))
    do, dup, gate_y, down_sends = tie((do, dup, gate_y, down_sends))
    down_one, down_two, down_three = direct_send(down_sends)
    gate_c = cols_core(dgate, gate_y, y, core)
    up_y = cols_y(dup, y)
    gate_c, down_one = tie((gate_c, down_one))
    gate_own, gate_send = plane_product(dgate, gate_y, gate_c, [m_all], (*here, 0, *pairs), (2, 2))
    gate_own, gate_send, up_y = tie((gate_own, gate_send, up_y))
    gate_received = flip(gate_send, Z1_BIT)
    up_c = cols_core(dup, up_y, y, core)
    up_own, up_send = plane_product(dup, up_y, up_c, [m_all], (*here, 0, *pairs), (2, 2))
    do, dz, up_own, up_send, down_three = tie((do, dz, up_own, up_send, down_three))
    up_received = flip(up_send, Z1_BIT)
    dproj = backward_attention(do, state, tables)
    dz_y, dz_c = flip(dz, Y_BIT), flip(dz, CORE_BIT)
    attn_cols = jnp.concatenate([dproj, o], axis=1).reshape(tokens, 4, 4, share)
    attn_cols = attn_cols.transpose(2, 0, 1, 3).reshape(4, tokens, 4 * share)
    attn_y = cols_y(attn_cols, y)
    dproj, attn_y, dz_y, dz_c, gate_own, gate_received, down_two = tie(
        (dproj, attn_y, dz_y, dz_c, gate_own, gate_received, down_two)
    )
    dz_all = (dz, dz_y, dz_c, flip(dz_y, CORE_BIT))
    attn_c = cols_core(attn_cols, attn_y, y, core)
    du, gain_one_grad = backward_in(dproj, dh1, state, weights)
    gain_grad = jnp.concatenate([gain_one_grad, gain_two_grad])
    gain_grad = gain_grad + sum(
        flip(gain_grad, bit) for bit in (CORE_BIT, Y_BIT, CORE_BIT | Y_BIT)
    )
    gain_rows = at(gain_grad.reshape(4, 4, -1).transpose(1, 0, 2), y * 2 + core)[:, None]
    gain_share = gain_rows.shape[-1]
    gain_rows = jnp.pad(gain_rows, ((0, 0), (0, EXTRA_ROWS - 1), (0, width - gain_share)))
    qkv_owners = QKV_COLS // share
    is_qkv = (qkv_owners // 4 * 4 + y * 2 + core < qkv_owners).astype(jnp.int32)
    attn_own, *attn_sends = plane_product(
        attn_cols,
        attn_y,
        attn_c,
        [n_all, dz_all],
        (*here, is_qkv, z, *others),
        (1, 1, 1, 1),
        (qkv_owners // 4, -(-qkv_owners // 4)),
        gain_rows,
    )
    up_own, attn_own = tie((up_own, attn_own))
    attn_received = direct_send(attn_sends)
    down_received = (down_one, down_two, down_three)
    gate = pair_second(gate_own, gate_received, z2)
    up = pair_second(up_own, up_received, z2)
    down = direct_total(down_own[0], down_received)
    attn = direct_total(attn_own[0], attn_received)
    return (
        du,
        attn[:share],
        jnp.stack([gate, up, down]),
        attn[share : share + 1, :gain_share],
    )


def local(edge_data, segment_ids, attn_weight, ffn_weight, gains):
    micro = segment_ids.shape[0]
    leading = lax.axis_index("section") == 0
    tables = block_tables(segment_ids)
    block, width = edge_data.shape[2], edge_data.shape[3]
    x = edge_data[0].reshape(micro * block, width)
    planes = lax.axis_size("dp") == 16
    me = lax.axis_index("dp")
    attn_own = attn_weight[0].T
    ffn_own = ffn_weight[0].swapaxes(1, 2)
    share = attn_own.shape[0]
    if planes:
        own = jnp.concatenate([attn_own[None], ffn_own], axis=0).reshape(-1, width)
        everything = lax.all_gather(own, "dp", axis=0, tiled=True).reshape(4, 4, 4, share, width)
        attn_t = everything[:, :, 0].reshape(-1, width)
        ffn_t = everything
    else:
        attn_t = lax.all_gather(attn_own, "dp", axis=0, tiled=True)
        ffn_t = lax.all_gather(ffn_own, "dp", axis=1, tiled=True)
    gain_row = gather_small(gains[0]).astype(f32)
    weights = (
        attn_t[:QKV_COLS],
        attn_t[QKV_COLS:],
        ffn_t,
        gain_row[:width],
        gain_row[width:],
    )
    first, _ = forward(x, weights, tables)
    received = lax.ppermute(first.astype(bf16), "section", [(0, 1)])
    u = jnp.where(leading, x, received)
    if planes:
        out, state, first_grad, early = middle_rounds(u, x, weights, tables, me)
        received = lax.ppermute(first_grad, "section", [(1, 0)])
        e = jnp.where(leading, received, x)
        du, attn_rows, ffn_rows, gain_shard = last_round(e, state, early, weights, tables, me)
    else:
        out, state = forward(u, weights, tables)
        first_grad, _, _ = backward(x, state, weights, tables)
        received = lax.ppermute(first_grad.astype(bf16), "section", [(1, 0)])
        e = jnp.where(leading, received, x)
        du, pieces, gain_grad = backward(e, state, weights, tables)
        attn_rows, ffn_rows = grads_generic(pieces)
        gain_shard = scatter_small(gain_grad)[None]
    edge_out = jnp.where(leading, du, out).astype(bf16).reshape(micro, block, width)
    return (
        edge_out[None],
        attn_rows.T[None],
        ffn_rows.swapaxes(1, 2)[None],
        gain_shard,
    )


def solution(mesh):
    in_specs = (
        P("section", None, "dp", None),
        P(None, "dp"),
        P("section", None, "dp"),
        P("section", None, None, "dp"),
        P("section", "dp"),
    )
    out_specs = (
        P("section", None, "dp", None),
        P("section", None, "dp"),
        P("section", None, None, "dp"),
        P("section", "dp"),
    )
    return jax.shard_map(local, mesh=mesh, in_specs=in_specs, out_specs=out_specs, check_vma=False)
```

```python
import jax
import jax.numpy as jnp
from jax import lax
from jax.experimental import pallas as pl
from jax.experimental.pallas import tpu as pltpu
from jax.sharding import PartitionSpec as P

QUERY_HEADS = 15
KEY_VALUE_HEADS = 5
HEAD_SIZE = 64
GROUP = QUERY_HEADS // KEY_VALUE_HEADS
Q_COLS = QUERY_HEADS * HEAD_SIZE
KV_COLS = KEY_VALUE_HEADS * HEAD_SIZE
QKV_COLS = Q_COLS + 2 * KV_COLS

epsilon = 1e-05
theta_base = 100000.0
Z2_BIT, Z1_BIT, Y_BIT, CORE_BIT = 8, 4, 2, 1
EXTRA_ROWS = 8
bf16 = jnp.bfloat16
f32 = jnp.float32


def dot_nn(a, b):
    return lax.dot_general(a, b, (((1,), (0,)), ((), ())), preferred_element_type=f32)


def dot_nt(a, b):
    return lax.dot_general(a, b, (((1,), (1,)), ((), ())), preferred_element_type=f32)


def rope(rows, cosine, sine):
    half = rows.shape[-1] // 2
    a, b = rows[..., :half], rows[..., half:]
    return jnp.concatenate([a * cosine - b * sine, b * cosine + a * sine], axis=-1)


def block_tables(segments):
    micro, block_len = segments.shape
    offsets = jnp.arange(block_len, dtype=jnp.int32)
    same = segments[:, :, None] == segments[:, None, :]
    start = jnp.min(jnp.where(same, offsets, block_len), axis=-1)
    positions = (offsets - start).astype(f32).reshape(-1)
    half = HEAD_SIZE // 2
    frequency = theta_base ** (-(2.0 * jnp.arange(half, dtype=f32)) / HEAD_SIZE)
    angles = positions[:, None] * frequency
    allowed = same & (offsets[:, None] >= offsets[None, :])
    eye = jnp.eye(micro, dtype=bool)
    full = allowed[:, :, None, :] & eye[:, None, :, None]
    total = micro * block_len
    return jnp.cos(angles), jnp.sin(angles), full.reshape(total, total)


def scores_of(q, k, allowed):
    s = jnp.einsum("tgrd,ugd->grtu", q, k, preferred_element_type=f32) * HEAD_SIZE**-0.5
    return jnp.where(allowed, s, -1000000000.0)


def forward_attention(u, weights, tables):
    qkv_w, out_w, ffn_w, gain_one, gain_two = weights
    cosine, sine, allowed = tables
    tokens = u.shape[0]
    u = u.astype(f32)
    r1 = lax.rsqrt(jnp.mean(u * u, axis=-1, keepdims=True) + epsilon)
    n = (u * r1 * gain_one).astype(bf16)
    proj = dot_nt(n, qkv_w)
    q = rope(
        proj[:, :Q_COLS].reshape(tokens, KEY_VALUE_HEADS, GROUP, HEAD_SIZE),
        cosine[:, None, None, :],
        sine[:, None, None, :],
    ).astype(bf16)
    k = rope(
        proj[:, Q_COLS : Q_COLS + KV_COLS].reshape(tokens, KEY_VALUE_HEADS, HEAD_SIZE),
        cosine[:, None, :],
        sine[:, None, :],
    ).astype(bf16)
    v = proj[:, Q_COLS + KV_COLS :].reshape(tokens, KEY_VALUE_HEADS, HEAD_SIZE).astype(bf16)
    masked = scores_of(q, k, allowed)
    peak = jnp.max(masked, axis=-1, keepdims=True)
    lse = peak + jnp.log(jnp.sum(jnp.exp(masked - peak), axis=-1, keepdims=True))
    prob = jnp.exp(masked - lse).astype(bf16)
    o = jnp.einsum("grtu,ugd->tgrd", prob, v, preferred_element_type=f32)
    o = o.reshape(tokens, Q_COLS).astype(bf16)
    h1 = u + dot_nn(o, out_w)
    r2 = lax.rsqrt(jnp.mean(h1 * h1, axis=-1, keepdims=True) + epsilon)
    m = (h1 * r2 * gain_two).astype(bf16)
    return u, r1, n, q, k, v, lse, o, h1, r2, m


def forward(u, weights, tables):
    state = forward_attention(u, weights, tables)
    gate, up, act, out = ffn_forward(state[10], state[8], weights[2])
    return out, (*state, gate, up, act)


def norm_back(grad, rows, r, gain):
    scaled = grad * gain
    part = r * scaled - rows * (r * r * r) * jnp.mean(scaled * rows, axis=-1, keepdims=True)
    return part, jnp.sum(grad * rows * r, axis=0)


def backward_ffn(eb, state, weights):
    gate, up = state[11], state[12]
    return ffn_backward(eb, gate, up, weights[2])


def backward_mid(e, dm, state, weights):
    out_w, gain_two = weights[1], weights[4]
    h1, r2 = state[8], state[9]
    part, gain_two_grad = norm_back(dm, h1, r2, gain_two)
    dh1 = e.astype(f32) + part
    dz = dh1.astype(bf16)
    return dh1, dz, dot_nt(dz, out_w).astype(bf16), gain_two_grad


def backward_attention(do, state, tables):
    cosine, sine, allowed = tables
    q, k, v, lse = state[3:7]
    tokens = do.shape[0]
    do = do.reshape(tokens, KEY_VALUE_HEADS, GROUP, HEAD_SIZE)
    prob = jnp.exp(scores_of(q, k, allowed) - lse)
    dv = jnp.einsum("grtu,tgrd->ugd", prob.astype(bf16), do, preferred_element_type=f32)
    dp = jnp.einsum("tgrd,ugd->grtu", do, v, preferred_element_type=f32)
    ds = (prob * (dp - jnp.sum(dp * prob, axis=-1, keepdims=True))).astype(bf16)
    dq = jnp.einsum("grtu,ugd->tgrd", ds, k, preferred_element_type=f32) * HEAD_SIZE**-0.5
    dk = jnp.einsum("grtu,tgrd->ugd", ds, q, preferred_element_type=f32) * HEAD_SIZE**-0.5
    dq = rope(dq, cosine[:, None, None, :], -sine[:, None, None, :])
    dk = rope(dk, cosine[:, None, :], -sine[:, None, :])
    return jnp.concatenate(
        [dq.reshape(tokens, Q_COLS), dk.reshape(tokens, KV_COLS), dv.reshape(tokens, KV_COLS)],
        axis=1,
    ).astype(bf16)


def backward_in(dproj, dh1, state, weights):
    qkv_w, gain_one = weights[0], weights[3]
    u, r1 = state[0], state[1]
    part, gain_one_grad = norm_back(dot_nn(dproj, qkv_w), u, r1, gain_one)
    return dh1 + part, gain_one_grad


def backward(e, state, weights, tables):
    dgate, dup, dm = backward_ffn(e.astype(bf16), state, weights)
    dh1, dz, do, gain_two_grad = backward_mid(e, dm, state, weights)
    dproj = backward_attention(do, state, tables)
    du, gain_one_grad = backward_in(dproj, dh1, state, weights)
    pieces = (state[2], dproj, state[7], dz, state[10], dgate, dup, e.astype(bf16), state[13])
    return du, pieces, jnp.concatenate([gain_one_grad, gain_two_grad])


def ffn_forward_kernel(m_ref, h1_ref, wg_ref, wu_ref, wd_ref, gate_ref, up_ref, act_ref, out_ref):
    flat = lambda ref: ref[...].reshape(-1, ref.shape[-1])
    m = m_ref[...]
    gate = dot_nt(m, flat(wg_ref))
    up = dot_nt(m, flat(wu_ref))
    act = (gate * jax.nn.sigmoid(gate) * up).astype(bf16)
    gate_ref[...] = gate
    up_ref[...] = up
    act_ref[...] = act
    add = dot_nn(act, flat(wd_ref))

    @pl.when(pl.program_id(0) == 0)
    def _():
        out_ref[...] = h1_ref[...] + add

    @pl.when(pl.program_id(0) > 0)
    def _():
        out_ref[...] += add


def ffn_backward_kernel(
    eb_ref, gate_ref, up_ref, wg_ref, wu_ref, wd_ref, both_ref, dm_ref
):
    flat = lambda ref: ref[...].reshape(-1, ref.shape[-1])
    da = dot_nt(eb_ref[...], flat(wd_ref))
    gate = gate_ref[...]
    sig = jax.nn.sigmoid(gate)
    dgate = (da * up_ref[...] * sig * (1.0 + gate * (1.0 - sig))).astype(bf16)
    dup = (da * gate * sig).astype(bf16)
    both_ref[0] = dgate
    both_ref[1] = dup
    add = dot_nn(dgate, flat(wg_ref)) + dot_nn(dup, flat(wu_ref))

    @pl.when(pl.program_id(0) == 0)
    def _():
        dm_ref[...] = add

    @pl.when(pl.program_id(0) > 0)
    def _():
        dm_ref[...] += add


def weight_spec(w, matrix):
    lines, _, _, share, width = w.shape
    return pl.BlockSpec((lines, None, None, share, width), lambda i: (0, i, matrix, 0, 0))


def ffn_call(kernel, w, wholes, blocks, out_blocks):
    lines, steps, _, share, width = w.shape
    tokens, cols = wholes[0].shape[0], lines * share
    whole = pl.BlockSpec((tokens, width), lambda i: (0, 0))
    block = pl.BlockSpec((None, tokens, cols), lambda i: (i, 0, 0))
    out_specs = [
        pl.BlockSpec((None, *shape), lambda i, n=len(shape): (i,) + (0,) * n) for shape, _ in out_blocks
    ]
    return pl.pallas_call(
        kernel,
        grid=(steps,),
        in_specs=[whole] * len(wholes)
        + [block] * len(blocks)
        + [weight_spec(w, matrix) for matrix in (1, 2, 3)],
        out_specs=out_specs + [whole],
        out_shape=[jax.ShapeDtypeStruct((steps, *shape), t) for shape, t in out_blocks]
        + [jax.ShapeDtypeStruct((tokens, width), f32)],
        compiler_params=pltpu.CompilerParams(
            dimension_semantics=("arbitrary",), vmem_limit_bytes=40 * 1024 * 1024
        ),
        cost_estimate=pl.CostEstimate(
            flops=6 * tokens * steps * cols * width,
            bytes_accessed=6 * steps * cols * width,
            transcendentals=tokens * steps * cols,
        ),
    )(*wholes, *blocks, w, w, w)


def ffn_forward(m, h1, w):
    if w.ndim == 5:
        shape = (m.shape[0], w.shape[0] * w.shape[3])
        return ffn_call(ffn_forward_kernel, w, (m, h1), (), [(shape, t) for t in (f32, f32, bf16)])
    gate, up = dot_nt(m, w[0]), dot_nt(m, w[1])
    act = (jax.nn.silu(gate) * up).astype(bf16)
    return gate, up, act, h1 + dot_nn(act, w[2])


def ffn_backward(eb, gate, up, w):
    if w.ndim == 5:
        shape = (2, eb.shape[0], w.shape[0] * w.shape[3])
        both, dm = ffn_call(ffn_backward_kernel, w, (eb,), (gate, up), [(shape, bf16)])
        return both, both, dm
    da = dot_nt(eb, w[2])
    sig = jax.nn.sigmoid(gate)
    dgate = (da * up * sig * (1.0 + gate * (1.0 - sig))).astype(bf16)
    dup = (da * gate * sig).astype(bf16)
    return dgate, dup, dot_nn(dgate, w[0]) + dot_nn(dup, w[1])


def flip(x, bit):
    size = lax.axis_size("dp")
    return lax.ppermute(x, "dp", [(i, i ^ bit) for i in range(size)])


def gather_small(row):
    size = lax.axis_size("dp")
    me = lax.axis_index("dp")
    bit = 1
    while bit < size:
        other = flip(row, bit)
        high = (me & bit) != 0
        row = jnp.concatenate([jnp.where(high, other, row), jnp.where(high, row, other)])
        bit *= 2
    return row


def scatter_small(row):
    size = lax.axis_size("dp")
    me = lax.axis_index("dp")
    bit = size // 2
    while bit >= 1:
        half = row.shape[0] // 2
        low, top = row[:half], row[half:]
        high = (me & bit) != 0
        row = jnp.where(high, top, low) + flip(jnp.where(high, low, top), bit)
        bit //= 2
    return row


def grads_generic(pieces):
    n, dproj, o, dz, m, dgate, dup, eb, act = pieces
    attn = jnp.concatenate([dot_nn(dproj.T, n), dot_nn(o.T, dz)], axis=0)
    both = [
        lax.psum_scatter(g, "dp", scatter_dimension=0, tiled=True)
        for g in (attn, dot_nn(dgate.T, m), dot_nn(dup.T, m), dot_nn(act.T, eb))
    ]
    return both[0], jnp.stack(both[1:])


def z_pairs(x, pairs):
    return lax.ppermute(x, "dp", [(4 * a + i, 4 * b + i) for a, b in pairs for i in range(4)])


def inner_swap(x):
    return z_pairs(x, [(1, 2), (2, 1)])


def at(x, i):
    return lax.dynamic_index_in_dim(x, i, 0, keepdims=False)


def rows_of_plane(x):
    x_y = flip(x, Y_BIT)
    return x, x_y, flip(x, CORE_BIT), flip(x_y, CORE_BIT)


def cols_y(x, y):
    x = x.reshape(2, 2, *x.shape[1:])
    return flip(at(x, 1 - y), Y_BIT)


def cols_core(x, x_y, y, core):
    other = 1 - core
    return flip(jnp.stack([at(x, 2 * y + other), at(x_y, other)]), CORE_BIT)


def plane_kernel(n_rows, split, n_own, picks_ref, *refs):
    cols_ref, y_ref, core_ref = refs[:3]
    rows = [
        jnp.concatenate([r[...] for r in refs[3 + 4 * i : 7 + 4 * i]], axis=0) for i in range(n_rows)
    ]
    rest = refs[3 + 4 * n_rows :]
    extra_ref = rest[0] if n_rows == 2 else None
    outs, total = rest[n_rows - 1 : -1], rest[-1]
    kinds = cols_ref.shape[1]
    height = total.shape[0] // kinds
    share = height // LINE

    def cols_of(j):
        return jnp.concatenate(
            [cols_ref[picks_ref[0], j], y_ref[picks_ref[1], j], core_ref[0, j], core_ref[1, j]], axis=0
        )

    def dot(c, r):
        return lax.dot_general(c, r, (((0,), (0,)), ((), ())), preferred_element_type=f32)

    if n_rows == 1:
        for j in range(kinds):
            total[j * height : (j + 1) * height] = dot(cols_of(j), rows[0])
    else:
        low, top = split
        cols = cols_of(0)
        total[...] = dot(cols, rows[1])
        first = dot(cols, rows[0])
        total[: low * share] = first[: low * share]
        if top > low:

            @pl.when(picks_ref[2] > 0)
            def _():
                total[low * share : top * share] = first[low * share : top * share]

    slot = 3
    for number, ref in enumerate(outs):
        for i in range(ref.shape[0]):
            pick = picks_ref[slot]
            slot += 1
            for j in range(kinds):
                block = total[pl.ds(pl.multiple_of(j * height + pick * share, 8), share)]
                ref[i, j * share : (j + 1) * share] = block.astype(ref.dtype)
            if extra_ref is not None:
                ref[i, share:] = extra_ref[pick].astype(ref.dtype)


def plane_product(cols, x_y, x_core, rows, picks, out_counts, split=None, extra=None):
    _, kinds, tokens, width_cols = cols.shape
    share, width = width_cols // LINE, rows[0][0].shape[1]
    tall = kinds * share + (0 if extra is None else extra.shape[1])
    operands = [cols, x_y, x_core, *[r for chunk in rows for r in chunk]]
    if extra is not None:
        operands.append(extra)
    whole = lambda v: pl.BlockSpec(v.shape, lambda i, picks, n=v.ndim: (0,) * n)
    shapes = [
        jax.ShapeDtypeStruct((count, tall, width), f32 if i == 0 else bf16)
        for i, count in enumerate(out_counts)
    ]
    kernel = lambda *refs: plane_kernel(len(rows), split, out_counts[0], *refs)
    return pl.pallas_call(
        kernel,
        grid_spec=pltpu.PrefetchScalarGridSpec(
            num_scalar_prefetch=1,
            grid=(1,),
            in_specs=[whole(v) for v in operands],
            out_specs=[whole(v) for v in shapes],
            scratch_shapes=[pltpu.VMEM((kinds * LINE * share, width), f32)],
        ),
        out_shape=shapes,
        compiler_params=pltpu.CompilerParams(
            dimension_semantics=("arbitrary",), vmem_limit_bytes=32 * 1024 * 1024
        ),
        cost_estimate=pl.CostEstimate(
            flops=8 * tokens * kinds * width_cols * width * len(rows),
            bytes_accessed=8 * tokens * (kinds * width_cols + width) + 4 * kinds * width_cols * width,
            transcendentals=0,
        ),
    )(jnp.stack([jnp.asarray(p, jnp.int32) for p in picks]), *operands)


LINE = 4
ORDER = (1, 2, 3)


def direct_send(sends):
    return [
        z_pairs(send[0], [(a, (a + k) % LINE) for a in range(LINE)])
        for k, send in zip(ORDER, sends)
    ]


def direct_total(own, received):
    return own + sum(r.astype(f32) for r in received)


def pair_second(own, received, z2):
    total = own + received.astype(f32)
    return at(total, z2) + flip(at(total, 1 - z2).astype(bf16), Z2_BIT).astype(f32)


tie = lax.optimization_barrier


def middle_rounds(u, x, weights, tables, me):
    y, core = (me >> 1) & 1, me & 1
    state = forward_attention(u, weights, tables)
    n, m = state[2], state[10]
    gate, up, act, out = ffn_forward(m, state[8], weights[2])
    m_y, n_y = flip(m, Y_BIT), flip(n, Y_BIT)
    gate, up, act, out, m_y, n_y = tie((gate, up, act, out, m_y, n_y))
    state = (*state, gate, up, act)
    act = act[:, None]
    act_y = cols_y(act, y)
    m_all = (m, m_y, flip(m, CORE_BIT), flip(m_y, CORE_BIT))
    n_all = (n, n_y, flip(n, CORE_BIT), flip(n_y, CORE_BIT))
    _, _, dm = backward_ffn(x, state, weights)
    dm, act_y, m_all, n_all = tie((dm, act_y, m_all, n_all))
    act_c = (act, act_y, cols_core(act, act_y, y, core))
    dh1, _, do, _ = backward_mid(x, dm, state, weights)
    dproj = backward_attention(do, state, tables)
    first_grad, _ = backward_in(dproj, dh1, state, weights)
    first_grad, act_c = tie((first_grad.astype(bf16), act_c))
    return out, state, first_grad, (m_all, n_all, act_c)


def last_round(e, state, early, weights, tables, me):
    o = state[7]
    z, y, core = me // 4, (me >> 1) & 1, me & 1
    z2, z1 = z >> 1, z & 1
    m_all, n_all, act_c = early
    tokens, width = o.shape[0], e.shape[1]
    share = act_c[0].shape[3] // LINE
    here = (2 * y + core, core)
    others = [(z + k) % LINE for k in ORDER]
    eb = e.astype(bf16)
    eb_y, eb_c = flip(eb, Y_BIT), flip(eb, CORE_BIT)
    both, _, dm = backward_ffn(eb, state, weights)
    both, dm, eb_y, eb_c = tie((both, dm, eb_y, eb_c))
    both_y = cols_y(both, y)
    eb_yc = flip(eb_y, CORE_BIT)
    dm, eb_yc = tie((dm, eb_yc))
    direct = (*here, 0, z, *others)
    ones = (1, 1, 1, 1)
    down_own, *down_sends = plane_product(*act_c, [(eb, eb_y, eb_c, eb_yc)], direct, ones)
    dm, down_sends = tie((dm, down_sends))
    down_one, down_two, down_three = direct_send(down_sends)
    dh1, dz, do, gain_two_grad = backward_mid(e, dm, state, weights)
    do, dz, both_y, down_one = tie((do, dz, both_y, down_one))
    both_c = cols_core(both, both_y, y, core)
    both_own, *both_sends = plane_product(both, both_y, both_c, [m_all], direct, ones)
    do, dz, both_sends = tie((do, dz, both_sends))
    both_one, both_two, both_three = direct_send(both_sends)
    dproj = backward_attention(do, state, tables)
    dproj, down_two, down_three = tie((dproj, down_two, down_three))
    attn_cols = jnp.concatenate([dproj, o], axis=1).reshape(tokens, 4, 4, share)
    attn_cols = attn_cols.transpose(2, 0, 1, 3).reshape(4, 1, tokens, 4 * share)
    attn_y = cols_y(attn_cols, y)
    dz_y, dz_c = flip(dz, Y_BIT), flip(dz, CORE_BIT)
    du, gain_one_grad = backward_in(dproj, dh1, state, weights)
    gain_grad = jnp.concatenate([gain_one_grad, gain_two_grad])
    gain_grad, attn_y, dz_y, dz_c, both_one = tie((gain_grad, attn_y, dz_y, dz_c, both_one))
    gain_grad = gain_grad + flip(gain_grad, CORE_BIT)
    gain_grad = gain_grad + flip(gain_grad, Y_BIT)
    dz_all = (dz, dz_y, dz_c, flip(dz_y, CORE_BIT))
    attn_c = cols_core(attn_cols, attn_y, y, core)
    gain_grad, dz_all, attn_c, both_two = tie((gain_grad, dz_all, attn_c, both_two))
    gain_rows = at(gain_grad.reshape(4, 4, -1).transpose(1, 0, 2), y * 2 + core)[:, None]
    gain_share = gain_rows.shape[-1]
    gain_rows = jnp.pad(gain_rows, ((0, 0), (0, EXTRA_ROWS - 1), (0, width - gain_share)))
    qkv_owners = QKV_COLS // share
    is_qkv = (qkv_owners // 4 * 4 + y * 2 + core < qkv_owners).astype(jnp.int32)
    attn_own, attn_send = plane_product(
        attn_cols,
        attn_y,
        attn_c,
        [n_all, dz_all],
        (*here, is_qkv, z1, 2 + z1, 1 - z1, 3 - z1),
        (2, 2),
        (qkv_owners // 4, -(-qkv_owners // 4)),
        gain_rows,
    )
    attn_received = flip(attn_send, Z1_BIT)
    attn_own, attn_received, both_three = tie((attn_own, attn_received, both_three))
    attn = pair_second(attn_own, attn_received, z2)
    down = direct_total(down_own[0], (down_one, down_two, down_three))
    both = direct_total(both_own[0], (both_one, both_two, both_three))
    return (
        du,
        attn[:share],
        jnp.concatenate([both, down]).reshape(3, share, width),
        attn[share : share + 1, :gain_share],
    )


def local(edge_data, segment_ids, attn_weight, ffn_weight, gains):
    micro = segment_ids.shape[0]
    leading = lax.axis_index("section") == 0
    tables = block_tables(segment_ids)
    block, width = edge_data.shape[2], edge_data.shape[3]
    x = edge_data[0].reshape(micro * block, width)
    planes = lax.axis_size("dp") == 16
    me = lax.axis_index("dp")
    attn_own = attn_weight[0].T
    ffn_own = ffn_weight[0].swapaxes(1, 2)
    share = attn_own.shape[0]
    if planes:
        own = jnp.concatenate([attn_own[None], ffn_own], axis=0).reshape(-1, width)
        everything = lax.all_gather(own, "dp", axis=0, tiled=True).reshape(4, 4, 4, share, width)
        attn_t = everything[:, :, 0].reshape(-1, width)
        ffn_t = everything
    else:
        attn_t = lax.all_gather(attn_own, "dp", axis=0, tiled=True)
        ffn_t = lax.all_gather(ffn_own, "dp", axis=1, tiled=True)
    gain_row = gather_small(gains[0]).astype(f32)
    weights = (
        attn_t[:QKV_COLS],
        attn_t[QKV_COLS:],
        ffn_t,
        gain_row[:width],
        gain_row[width:],
    )
    first, _ = forward(x, weights, tables)
    received = lax.ppermute(first.astype(bf16), "section", [(0, 1)])
    u = jnp.where(leading, x, received)
    if planes:
        out, state, first_grad, early = middle_rounds(u, x, weights, tables, me)
        received = lax.ppermute(first_grad, "section", [(1, 0)])
        e = jnp.where(leading, received, x)
        du, attn_rows, ffn_rows, gain_shard = last_round(e, state, early, weights, tables, me)
    else:
        out, state = forward(u, weights, tables)
        first_grad, _, _ = backward(x, state, weights, tables)
        received = lax.ppermute(first_grad.astype(bf16), "section", [(1, 0)])
        e = jnp.where(leading, received, x)
        du, pieces, gain_grad = backward(e, state, weights, tables)
        attn_rows, ffn_rows = grads_generic(pieces)
        gain_shard = scatter_small(gain_grad)[None]
    edge_out = jnp.where(leading, du, out).astype(bf16).reshape(micro, block, width)
    return (
        edge_out[None],
        attn_rows.T[None],
        ffn_rows.swapaxes(1, 2)[None],
        gain_shard,
    )


def solution(mesh):
    in_specs = (
        P("section", None, "dp", None),
        P(None, "dp"),
        P("section", None, "dp"),
        P("section", None, None, "dp"),
        P("section", "dp"),
    )
    out_specs = (
        P("section", None, "dp", None),
        P("section", None, "dp"),
        P("section", None, None, "dp"),
        P("section", "dp"),
    )
    return jax.shard_map(local, mesh=mesh, in_specs=in_specs, out_specs=out_specs, check_vma=False)
```

```python
import jax
import jax.numpy as jnp
from jax import lax
from jax.experimental import pallas as pl
from jax.experimental.pallas import tpu as pltpu
from jax.sharding import PartitionSpec as P

QUERY_HEADS = 15
KEY_VALUE_HEADS = 5
HEAD_SIZE = 64
GROUP = QUERY_HEADS // KEY_VALUE_HEADS
Q_COLS = QUERY_HEADS * HEAD_SIZE
KV_COLS = KEY_VALUE_HEADS * HEAD_SIZE
QKV_COLS = Q_COLS + 2 * KV_COLS

epsilon = 1e-05
theta_base = 100000.0
Z2_BIT, Z1_BIT, Y_BIT, CORE_BIT = 8, 4, 2, 1
EXTRA_ROWS = 8
bf16 = jnp.bfloat16
f32 = jnp.float32


def dot_nn(a, b):
    return lax.dot_general(a, b, (((1,), (0,)), ((), ())), preferred_element_type=f32)


def dot_nt(a, b):
    return lax.dot_general(a, b, (((1,), (1,)), ((), ())), preferred_element_type=f32)


def rope(rows, cosine, sine):
    half = rows.shape[-1] // 2
    a, b = rows[..., :half], rows[..., half:]
    return jnp.concatenate([a * cosine - b * sine, b * cosine + a * sine], axis=-1)


def block_tables(segments):
    micro, block_len = segments.shape
    offsets = jnp.arange(block_len, dtype=jnp.int32)
    same = segments[:, :, None] == segments[:, None, :]
    start = jnp.min(jnp.where(same, offsets, block_len), axis=-1)
    positions = (offsets - start).astype(f32).reshape(-1)
    half = HEAD_SIZE // 2
    frequency = theta_base ** (-(2.0 * jnp.arange(half, dtype=f32)) / HEAD_SIZE)
    angles = positions[:, None] * frequency
    allowed = same & (offsets[:, None] >= offsets[None, :])
    eye = jnp.eye(micro, dtype=bool)
    full = allowed[:, :, None, :] & eye[:, None, :, None]
    total = micro * block_len
    return jnp.cos(angles), jnp.sin(angles), full.reshape(total, total)


def scores_of(q, k, allowed):
    s = jnp.einsum("tgrd,ugd->grtu", q, k, preferred_element_type=f32) * HEAD_SIZE**-0.5
    return jnp.where(allowed, s, -1000000000.0)


def forward_attention(u, weights, tables):
    qkv_w, out_w, ffn_w, gain_one, gain_two = weights
    cosine, sine, allowed = tables
    tokens = u.shape[0]
    u = u.astype(f32)
    r1 = lax.rsqrt(jnp.mean(u * u, axis=-1, keepdims=True) + epsilon)
    n = (u * r1 * gain_one).astype(bf16)
    proj = dot_nt(n, qkv_w)
    q = rope(
        proj[:, :Q_COLS].reshape(tokens, KEY_VALUE_HEADS, GROUP, HEAD_SIZE),
        cosine[:, None, None, :],
        sine[:, None, None, :],
    ).astype(bf16)
    k = rope(
        proj[:, Q_COLS : Q_COLS + KV_COLS].reshape(tokens, KEY_VALUE_HEADS, HEAD_SIZE),
        cosine[:, None, :],
        sine[:, None, :],
    ).astype(bf16)
    v = proj[:, Q_COLS + KV_COLS :].reshape(tokens, KEY_VALUE_HEADS, HEAD_SIZE).astype(bf16)
    masked = scores_of(q, k, allowed)
    peak = jnp.max(masked, axis=-1, keepdims=True)
    lse = peak + jnp.log(jnp.sum(jnp.exp(masked - peak), axis=-1, keepdims=True))
    prob = jnp.exp(masked - lse).astype(bf16)
    o = jnp.einsum("grtu,ugd->tgrd", prob, v, preferred_element_type=f32)
    o = o.reshape(tokens, Q_COLS).astype(bf16)
    h1 = u + dot_nn(o, out_w)
    r2 = lax.rsqrt(jnp.mean(h1 * h1, axis=-1, keepdims=True) + epsilon)
    m = (h1 * r2 * gain_two).astype(bf16)
    return u, r1, n, q, k, v, lse, o, h1, r2, m


def forward(u, weights, tables):
    state = forward_attention(u, weights, tables)
    gate, up, act, out = ffn_forward(state[10], state[8], weights[2])
    return out, (*state, gate, up, act)


def norm_back(grad, rows, r, gain):
    scaled = grad * gain
    part = r * scaled - rows * (r * r * r) * jnp.mean(scaled * rows, axis=-1, keepdims=True)
    return part, jnp.sum(grad * rows * r, axis=0)


def backward_ffn(eb, state, weights):
    gate, up = state[11], state[12]
    return ffn_backward(eb, gate, up, weights[2])


def backward_mid(e, dm, state, weights):
    out_w, gain_two = weights[1], weights[4]
    h1, r2 = state[8], state[9]
    part, gain_two_grad = norm_back(dm, h1, r2, gain_two)
    dh1 = e.astype(f32) + part
    dz = dh1.astype(bf16)
    return dh1, dz, dot_nt(dz, out_w).astype(bf16), gain_two_grad


def backward_attention(do, state, tables):
    cosine, sine, allowed = tables
    q, k, v, lse = state[3:7]
    tokens = do.shape[0]
    do = do.reshape(tokens, KEY_VALUE_HEADS, GROUP, HEAD_SIZE)
    prob = jnp.exp(scores_of(q, k, allowed) - lse)
    dv = jnp.einsum("grtu,tgrd->ugd", prob.astype(bf16), do, preferred_element_type=f32)
    dp = jnp.einsum("tgrd,ugd->grtu", do, v, preferred_element_type=f32)
    ds = (prob * (dp - jnp.sum(dp * prob, axis=-1, keepdims=True))).astype(bf16)
    dq = jnp.einsum("grtu,ugd->tgrd", ds, k, preferred_element_type=f32) * HEAD_SIZE**-0.5
    dk = jnp.einsum("grtu,tgrd->ugd", ds, q, preferred_element_type=f32) * HEAD_SIZE**-0.5
    dq = rope(dq, cosine[:, None, None, :], -sine[:, None, None, :])
    dk = rope(dk, cosine[:, None, :], -sine[:, None, :])
    return jnp.concatenate(
        [dq.reshape(tokens, Q_COLS), dk.reshape(tokens, KV_COLS), dv.reshape(tokens, KV_COLS)],
        axis=1,
    ).astype(bf16)


def backward_in(dproj, dh1, state, weights):
    qkv_w, gain_one = weights[0], weights[3]
    u, r1 = state[0], state[1]
    part, gain_one_grad = norm_back(dot_nn(dproj, qkv_w), u, r1, gain_one)
    return dh1 + part, gain_one_grad


def backward(e, state, weights, tables):
    dgate, dup, dm = backward_ffn(e.astype(bf16), state, weights)
    dh1, dz, do, gain_two_grad = backward_mid(e, dm, state, weights)
    dproj = backward_attention(do, state, tables)
    du, gain_one_grad = backward_in(dproj, dh1, state, weights)
    pieces = (state[2], dproj, state[7], dz, state[10], dgate, dup, e.astype(bf16), state[13])
    return du, pieces, jnp.concatenate([gain_one_grad, gain_two_grad])


def ffn_forward_kernel(m_ref, h1_ref, wg_ref, wu_ref, wd_ref, gate_ref, up_ref, act_ref, out_ref):
    flat = lambda ref: ref[...].reshape(-1, ref.shape[-1])
    m = m_ref[...]
    gate = dot_nt(m, flat(wg_ref))
    up = dot_nt(m, flat(wu_ref))
    act = (gate * jax.nn.sigmoid(gate) * up).astype(bf16)
    gate_ref[...] = gate
    up_ref[...] = up
    act_ref[...] = act
    add = dot_nn(act, flat(wd_ref))

    @pl.when(pl.program_id(0) == 0)
    def _():
        out_ref[...] = h1_ref[...] + add

    @pl.when(pl.program_id(0) > 0)
    def _():
        out_ref[...] += add


def ffn_backward_kernel(
    eb_ref, gate_ref, up_ref, wg_ref, wu_ref, wd_ref, both_ref, dm_ref
):
    flat = lambda ref: ref[...].reshape(-1, ref.shape[-1])
    da = dot_nt(eb_ref[...], flat(wd_ref))
    gate = gate_ref[...]
    sig = jax.nn.sigmoid(gate)
    dgate = (da * up_ref[...] * sig * (1.0 + gate * (1.0 - sig))).astype(bf16)
    dup = (da * gate * sig).astype(bf16)
    both_ref[0] = dgate
    both_ref[1] = dup
    add = dot_nn(dgate, flat(wg_ref)) + dot_nn(dup, flat(wu_ref))

    @pl.when(pl.program_id(0) == 0)
    def _():
        dm_ref[...] = add

    @pl.when(pl.program_id(0) > 0)
    def _():
        dm_ref[...] += add


def weight_spec(w, matrix):
    lines, _, _, share, width = w.shape
    return pl.BlockSpec((lines, None, None, share, width), lambda i: (0, i, matrix, 0, 0))


def ffn_call(kernel, w, wholes, blocks, out_blocks):
    lines, steps, _, share, width = w.shape
    tokens, cols = wholes[0].shape[0], lines * share
    whole = pl.BlockSpec((tokens, width), lambda i: (0, 0))
    block = pl.BlockSpec((None, tokens, cols), lambda i: (i, 0, 0))
    out_specs = [
        pl.BlockSpec((None, *shape), lambda i, n=len(shape): (i,) + (0,) * n) for shape, _ in out_blocks
    ]
    return pl.pallas_call(
        kernel,
        grid=(steps,),
        in_specs=[whole] * len(wholes)
        + [block] * len(blocks)
        + [weight_spec(w, matrix) for matrix in (1, 2, 3)],
        out_specs=out_specs + [whole],
        out_shape=[jax.ShapeDtypeStruct((steps, *shape), t) for shape, t in out_blocks]
        + [jax.ShapeDtypeStruct((tokens, width), f32)],
        compiler_params=pltpu.CompilerParams(
            dimension_semantics=("arbitrary",), vmem_limit_bytes=40 * 1024 * 1024
        ),
        cost_estimate=pl.CostEstimate(
            flops=6 * tokens * steps * cols * width,
            bytes_accessed=6 * steps * cols * width,
            transcendentals=tokens * steps * cols,
        ),
    )(*wholes, *blocks, w, w, w)


def ffn_forward(m, h1, w):
    if w.ndim == 5:
        shape = (m.shape[0], w.shape[0] * w.shape[3])
        return ffn_call(ffn_forward_kernel, w, (m, h1), (), [(shape, t) for t in (f32, f32, bf16)])
    gate, up = dot_nt(m, w[0]), dot_nt(m, w[1])
    act = (jax.nn.silu(gate) * up).astype(bf16)
    return gate, up, act, h1 + dot_nn(act, w[2])


def ffn_backward(eb, gate, up, w):
    if w.ndim == 5:
        shape = (2, eb.shape[0], w.shape[0] * w.shape[3])
        both, dm = ffn_call(ffn_backward_kernel, w, (eb,), (gate, up), [(shape, bf16)])
        return both, both, dm
    da = dot_nt(eb, w[2])
    sig = jax.nn.sigmoid(gate)
    dgate = (da * up * sig * (1.0 + gate * (1.0 - sig))).astype(bf16)
    dup = (da * gate * sig).astype(bf16)
    return dgate, dup, dot_nn(dgate, w[0]) + dot_nn(dup, w[1])


def flip(x, bit):
    size = lax.axis_size("dp")
    return lax.ppermute(x, "dp", [(i, i ^ bit) for i in range(size)])


def gather_small(row):
    size = lax.axis_size("dp")
    me = lax.axis_index("dp")
    bit = 1
    while bit < size:
        other = flip(row, bit)
        high = (me & bit) != 0
        row = jnp.concatenate([jnp.where(high, other, row), jnp.where(high, row, other)])
        bit *= 2
    return row


def scatter_small(row):
    size = lax.axis_size("dp")
    me = lax.axis_index("dp")
    bit = size // 2
    while bit >= 1:
        half = row.shape[0] // 2
        low, top = row[:half], row[half:]
        high = (me & bit) != 0
        row = jnp.where(high, top, low) + flip(jnp.where(high, low, top), bit)
        bit //= 2
    return row


def grads_generic(pieces):
    n, dproj, o, dz, m, dgate, dup, eb, act = pieces
    attn = jnp.concatenate([dot_nn(dproj.T, n), dot_nn(o.T, dz)], axis=0)
    both = [
        lax.psum_scatter(g, "dp", scatter_dimension=0, tiled=True)
        for g in (attn, dot_nn(dgate.T, m), dot_nn(dup.T, m), dot_nn(act.T, eb))
    ]
    return both[0], jnp.stack(both[1:])


def z_pairs(x, pairs):
    return lax.ppermute(x, "dp", [(4 * a + i, 4 * b + i) for a, b in pairs for i in range(4)])


def inner_swap(x):
    return z_pairs(x, [(1, 2), (2, 1)])


def at(x, i):
    return lax.dynamic_index_in_dim(x, i, 0, keepdims=False)


def rows_of_plane(x):
    x_y = flip(x, Y_BIT)
    return x, x_y, flip(x, CORE_BIT), flip(x_y, CORE_BIT)


def cols_y(x, y):
    x = x.reshape(2, 2, *x.shape[1:])
    return flip(at(x, 1 - y), Y_BIT)


def cols_core(x, x_y, y, core):
    other = 1 - core
    return flip(jnp.stack([at(x, 2 * y + other), at(x_y, other)]), CORE_BIT)


def plane_kernel(n_rows, split, n_own, picks_ref, *refs):
    cols_ref, y_ref, core_ref = refs[:3]
    rows = [
        jnp.concatenate([r[...] for r in refs[3 + 4 * i : 7 + 4 * i]], axis=0) for i in range(n_rows)
    ]
    rest = refs[3 + 4 * n_rows :]
    extra_ref = rest[0] if n_rows == 2 else None
    outs, total = rest[n_rows - 1 : -1], rest[-1]
    kinds = cols_ref.shape[1]
    height = total.shape[0] // kinds
    share = height // LINE

    def cols_of(j):
        return jnp.concatenate(
            [cols_ref[picks_ref[0], j], y_ref[picks_ref[1], j], core_ref[0, j], core_ref[1, j]], axis=0
        )

    def dot(c, r):
        return lax.dot_general(c, r, (((0,), (0,)), ((), ())), preferred_element_type=f32)

    if n_rows == 1:
        for j in range(kinds):
            total[j * height : (j + 1) * height] = dot(cols_of(j), rows[0])
    else:
        low, top = split
        cols = cols_of(0)
        total[...] = dot(cols, rows[1])
        first = dot(cols, rows[0])
        total[: low * share] = first[: low * share]
        if top > low:

            @pl.when(picks_ref[2] > 0)
            def _():
                total[low * share : top * share] = first[low * share : top * share]

    slot = 3
    for number, ref in enumerate(outs):
        for i in range(ref.shape[0]):
            pick = picks_ref[slot]
            slot += 1
            for j in range(kinds):
                block = total[pl.ds(pl.multiple_of(j * height + pick * share, 8), share)]
                ref[i, j * share : (j + 1) * share] = block.astype(ref.dtype)
            if extra_ref is not None:
                ref[i, share:] = extra_ref[pick].astype(ref.dtype)


def plane_product(cols, x_y, x_core, rows, picks, out_counts, split=None, extra=None):
    _, kinds, tokens, width_cols = cols.shape
    share, width = width_cols // LINE, rows[0][0].shape[1]
    tall = kinds * share + (0 if extra is None else extra.shape[1])
    operands = [cols, x_y, x_core, *[r for chunk in rows for r in chunk]]
    if extra is not None:
        operands.append(extra)
    whole = lambda v: pl.BlockSpec(v.shape, lambda i, picks, n=v.ndim: (0,) * n)
    shapes = [
        jax.ShapeDtypeStruct((count, tall, width), f32 if i == 0 else bf16)
        for i, count in enumerate(out_counts)
    ]
    kernel = lambda *refs: plane_kernel(len(rows), split, out_counts[0], *refs)
    return pl.pallas_call(
        kernel,
        grid_spec=pltpu.PrefetchScalarGridSpec(
            num_scalar_prefetch=1,
            grid=(1,),
            in_specs=[whole(v) for v in operands],
            out_specs=[whole(v) for v in shapes],
            scratch_shapes=[pltpu.VMEM((kinds * LINE * share, width), f32)],
        ),
        out_shape=shapes,
        compiler_params=pltpu.CompilerParams(
            dimension_semantics=("arbitrary",), vmem_limit_bytes=32 * 1024 * 1024
        ),
        cost_estimate=pl.CostEstimate(
            flops=8 * tokens * kinds * width_cols * width * len(rows),
            bytes_accessed=8 * tokens * (kinds * width_cols + width) + 4 * kinds * width_cols * width,
            transcendentals=0,
        ),
    )(jnp.stack([jnp.asarray(p, jnp.int32) for p in picks]), *operands)


LINE = 4
ORDER = (1, 2, 3)


def direct_send(sends):
    return [
        z_pairs(send[0], [(a, (a + k) % LINE) for a in range(LINE)])
        for k, send in zip(ORDER, sends)
    ]


def direct_total(own, received):
    return own + sum(r.astype(f32) for r in received)


def pair_second(own, received, z2):
    total = own + received.astype(f32)
    return at(total, z2) + flip(at(total, 1 - z2).astype(bf16), Z2_BIT).astype(f32)


tie = lax.optimization_barrier


def middle_rounds(u, x, weights, tables, me):
    y, core = (me >> 1) & 1, me & 1
    state = forward_attention(u, weights, tables)
    n, m = state[2], state[10]
    gate, up, act, out = ffn_forward(m, state[8], weights[2])
    m_y, n_y = flip(m, Y_BIT), flip(n, Y_BIT)
    gate, up, act, out, m_y, n_y = tie((gate, up, act, out, m_y, n_y))
    state = (*state, gate, up, act)
    act = act[:, None]
    act_y = cols_y(act, y)
    m_all = (m, m_y, flip(m, CORE_BIT), flip(m_y, CORE_BIT))
    n_all = (n, n_y, flip(n, CORE_BIT), flip(n_y, CORE_BIT))
    _, _, dm = backward_ffn(x, state, weights)
    dm, act_y, m_all, n_all = tie((dm, act_y, m_all, n_all))
    act_c = (act, act_y, cols_core(act, act_y, y, core))
    dh1, _, do, _ = backward_mid(x, dm, state, weights)
    dproj = backward_attention(do, state, tables)
    first_grad, _ = backward_in(dproj, dh1, state, weights)
    first_grad, act_c = tie((first_grad.astype(bf16), act_c))
    return out, state, first_grad, (m_all, n_all, act_c)


def last_round(e, state, early, weights, tables, me):
    o = state[7]
    z, y, core = me // 4, (me >> 1) & 1, me & 1
    z2, z1 = z >> 1, z & 1
    m_all, n_all, act_c = early
    tokens, width = o.shape[0], e.shape[1]
    share = act_c[0].shape[3] // LINE
    here = (2 * y + core, core)
    others = [(z + k) % LINE for k in ORDER]
    eb = e.astype(bf16)
    eb_y, eb_c = flip(eb, Y_BIT), flip(eb, CORE_BIT)
    both, _, dm = backward_ffn(eb, state, weights)
    both, dm, eb_y, eb_c = tie((both, dm, eb_y, eb_c))
    both_y = cols_y(both, y)
    eb_yc = flip(eb_y, CORE_BIT)
    dm, eb_yc = tie((dm, eb_yc))
    direct = (*here, 0, z, *others)
    ones = (1, 1, 1, 1)
    down_own, *down_sends = plane_product(*act_c, [(eb, eb_y, eb_c, eb_yc)], direct, ones)
    dm, down_sends = tie((dm, down_sends))
    down_one, down_two, down_three = direct_send(down_sends)
    dh1, dz, do, gain_two_grad = backward_mid(e, dm, state, weights)
    do, dz, both_y, down_one = tie((do, dz, both_y, down_one))
    both_c = cols_core(both, both_y, y, core)
    both_c, down_two = tie((both_c, down_two))
    both_own, *both_sends = plane_product(both, both_y, both_c, [m_all], direct, ones)
    do, dz, both_sends = tie((do, dz, both_sends))
    both_one, both_two, both_three = direct_send(both_sends)
    dproj = backward_attention(do, state, tables)
    dproj, down_three = tie((dproj, down_three))
    attn_cols = jnp.concatenate([dproj, o], axis=1).reshape(tokens, 4, 4, share)
    attn_cols = attn_cols.transpose(2, 0, 1, 3).reshape(4, 1, tokens, 4 * share)
    attn_y = cols_y(attn_cols, y)
    dz_y, dz_c = flip(dz, Y_BIT), flip(dz, CORE_BIT)
    du, gain_one_grad = backward_in(dproj, dh1, state, weights)
    gain_grad = jnp.concatenate([gain_one_grad, gain_two_grad])
    gain_grad = gain_grad + flip(gain_grad, CORE_BIT)
    gain_grad = gain_grad + flip(gain_grad, Y_BIT)
    dz_all = (dz, dz_y, dz_c, flip(dz_y, CORE_BIT))
    attn_c = cols_core(attn_cols, attn_y, y, core)
    gain_grad, dz_all, attn_c, both_one = tie((gain_grad, dz_all, attn_c, both_one))
    gain_rows = at(gain_grad.reshape(4, 4, -1).transpose(1, 0, 2), y * 2 + core)[:, None]
    gain_share = gain_rows.shape[-1]
    gain_rows = jnp.pad(gain_rows, ((0, 0), (0, EXTRA_ROWS - 1), (0, width - gain_share)))
    qkv_owners = QKV_COLS // share
    is_qkv = (qkv_owners // 4 * 4 + y * 2 + core < qkv_owners).astype(jnp.int32)
    attn_own, attn_send = plane_product(
        attn_cols,
        attn_y,
        attn_c,
        [n_all, dz_all],
        (*here, is_qkv, z1, 2 + z1, 1 - z1, 3 - z1),
        (2, 2),
        (qkv_owners // 4, -(-qkv_owners // 4)),
        gain_rows,
    )
    attn_received = flip(attn_send, Z1_BIT)
    attn_own, attn_received, both_two, both_three = tie(
        (attn_own, attn_received, both_two, both_three)
    )
    attn = pair_second(attn_own, attn_received, z2)
    down = direct_total(down_own[0], (down_one, down_two, down_three))
    both = direct_total(both_own[0], (both_one, both_two, both_three))
    return (
        du,
        attn[:share],
        jnp.concatenate([both, down]).reshape(3, share, width),
        attn[share : share + 1, :gain_share],
    )


def local(edge_data, segment_ids, attn_weight, ffn_weight, gains):
    micro = segment_ids.shape[0]
    leading = lax.axis_index("section") == 0
    tables = block_tables(segment_ids)
    block, width = edge_data.shape[2], edge_data.shape[3]
    x = edge_data[0].reshape(micro * block, width)
    planes = lax.axis_size("dp") == 16
    me = lax.axis_index("dp")
    attn_own = attn_weight[0].T
    ffn_own = ffn_weight[0].swapaxes(1, 2)
    share = attn_own.shape[0]
    if planes:
        own = jnp.concatenate([attn_own[None], ffn_own], axis=0).reshape(-1, width)
        everything = lax.all_gather(own, "dp", axis=0, tiled=True).reshape(4, 4, 4, share, width)
        attn_t = everything[:, :, 0].reshape(-1, width)
        ffn_t = everything
    else:
        attn_t = lax.all_gather(attn_own, "dp", axis=0, tiled=True)
        ffn_t = lax.all_gather(ffn_own, "dp", axis=1, tiled=True)
    gain_row = gather_small(gains[0]).astype(f32)
    weights = (
        attn_t[:QKV_COLS],
        attn_t[QKV_COLS:],
        ffn_t,
        gain_row[:width],
        gain_row[width:],
    )
    first, _ = forward(x, weights, tables)
    received = lax.ppermute(first.astype(bf16), "section", [(0, 1)])
    u = jnp.where(leading, x, received)
    if planes:
        out, state, first_grad, early = middle_rounds(u, x, weights, tables, me)
        received = lax.ppermute(first_grad, "section", [(1, 0)])
        e = jnp.where(leading, received, x)
        du, attn_rows, ffn_rows, gain_shard = last_round(e, state, early, weights, tables, me)
    else:
        out, state = forward(u, weights, tables)
        first_grad, _, _ = backward(x, state, weights, tables)
        received = lax.ppermute(first_grad.astype(bf16), "section", [(1, 0)])
        e = jnp.where(leading, received, x)
        du, pieces, gain_grad = backward(e, state, weights, tables)
        attn_rows, ffn_rows = grads_generic(pieces)
        gain_shard = scatter_small(gain_grad)[None]
    edge_out = jnp.where(leading, du, out).astype(bf16).reshape(micro, block, width)
    return (
        edge_out[None],
        attn_rows.T[None],
        ffn_rows.swapaxes(1, 2)[None],
        gain_shard,
    )


def solution(mesh):
    in_specs = (
        P("section", None, "dp", None),
        P(None, "dp"),
        P("section", None, "dp"),
        P("section", None, None, "dp"),
        P("section", "dp"),
    )
    out_specs = (
        P("section", None, "dp", None),
        P("section", None, "dp"),
        P("section", None, None, "dp"),
        P("section", "dp"),
    )
    return jax.shard_map(local, mesh=mesh, in_specs=in_specs, out_specs=out_specs, check_vma=False)
```

```python
import jax
import jax.numpy as jnp
from jax import lax
from jax.experimental import pallas as pl
from jax.experimental.pallas import tpu as pltpu
from jax.sharding import PartitionSpec as P

QUERY_HEADS = 15
KEY_VALUE_HEADS = 5
HEAD_SIZE = 64
GROUP = QUERY_HEADS // KEY_VALUE_HEADS
Q_COLS = QUERY_HEADS * HEAD_SIZE
KV_COLS = KEY_VALUE_HEADS * HEAD_SIZE
QKV_COLS = Q_COLS + 2 * KV_COLS

epsilon = 1e-05
theta_base = 100000.0
Z2_BIT, Z1_BIT, Y_BIT, CORE_BIT = 8, 4, 2, 1
EXTRA_ROWS = 8
bf16 = jnp.bfloat16
f32 = jnp.float32


def dot_nn(a, b):
    return lax.dot_general(a, b, (((1,), (0,)), ((), ())), preferred_element_type=f32)


def dot_nt(a, b):
    return lax.dot_general(a, b, (((1,), (1,)), ((), ())), preferred_element_type=f32)


def rope(rows, cosine, sine):
    half = rows.shape[-1] // 2
    a, b = rows[..., :half], rows[..., half:]
    return jnp.concatenate([a * cosine - b * sine, b * cosine + a * sine], axis=-1)


def block_tables(segments):
    micro, block_len = segments.shape
    offsets = jnp.arange(block_len, dtype=jnp.int32)
    same = segments[:, :, None] == segments[:, None, :]
    start = jnp.min(jnp.where(same, offsets, block_len), axis=-1)
    positions = (offsets - start).astype(f32).reshape(-1)
    half = HEAD_SIZE // 2
    frequency = theta_base ** (-(2.0 * jnp.arange(half, dtype=f32)) / HEAD_SIZE)
    angles = positions[:, None] * frequency
    allowed = same & (offsets[:, None] >= offsets[None, :])
    eye = jnp.eye(micro, dtype=bool)
    full = allowed[:, :, None, :] & eye[:, None, :, None]
    total = micro * block_len
    return jnp.cos(angles), jnp.sin(angles), full.reshape(total, total)


def scores_of(q, k, allowed):
    s = jnp.einsum("tgrd,ugd->grtu", q, k, preferred_element_type=f32) * HEAD_SIZE**-0.5
    return jnp.where(allowed, s, -1000000000.0)


def forward_attention(u, weights, tables):
    qkv_w, out_w, ffn_w, gain_one, gain_two = weights
    cosine, sine, allowed = tables
    tokens = u.shape[0]
    u = u.astype(f32)
    r1 = lax.rsqrt(jnp.mean(u * u, axis=-1, keepdims=True) + epsilon)
    n = (u * r1 * gain_one).astype(bf16)
    proj = dot_nt(n, qkv_w)
    q = rope(
        proj[:, :Q_COLS].reshape(tokens, KEY_VALUE_HEADS, GROUP, HEAD_SIZE),
        cosine[:, None, None, :],
        sine[:, None, None, :],
    ).astype(bf16)
    k = rope(
        proj[:, Q_COLS : Q_COLS + KV_COLS].reshape(tokens, KEY_VALUE_HEADS, HEAD_SIZE),
        cosine[:, None, :],
        sine[:, None, :],
    ).astype(bf16)
    v = proj[:, Q_COLS + KV_COLS :].reshape(tokens, KEY_VALUE_HEADS, HEAD_SIZE).astype(bf16)
    masked = scores_of(q, k, allowed)
    peak = jnp.max(masked, axis=-1, keepdims=True)
    lse = peak + jnp.log(jnp.sum(jnp.exp(masked - peak), axis=-1, keepdims=True))
    prob = jnp.exp(masked - lse).astype(bf16)
    o = jnp.einsum("grtu,ugd->tgrd", prob, v, preferred_element_type=f32)
    o = o.reshape(tokens, Q_COLS).astype(bf16)
    h1 = u + dot_nn(o, out_w)
    r2 = lax.rsqrt(jnp.mean(h1 * h1, axis=-1, keepdims=True) + epsilon)
    m = (h1 * r2 * gain_two).astype(bf16)
    return u, r1, n, q, k, v, lse, o, h1, r2, m


def forward(u, weights, tables):
    state = forward_attention(u, weights, tables)
    gate, up, act, out = ffn_forward(state[10], state[8], weights[2])
    return out, (*state, gate, up, act)


def norm_back(grad, rows, r, gain):
    scaled = grad * gain
    part = r * scaled - rows * (r * r * r) * jnp.mean(scaled * rows, axis=-1, keepdims=True)
    return part, jnp.sum(grad * rows * r, axis=0)


def backward_ffn(eb, state, weights):
    gate, up = state[11], state[12]
    return ffn_backward(eb, gate, up, weights[2])


def backward_mid(e, dm, state, weights):
    out_w, gain_two = weights[1], weights[4]
    h1, r2 = state[8], state[9]
    part, gain_two_grad = norm_back(dm, h1, r2, gain_two)
    dh1 = e.astype(f32) + part
    dz = dh1.astype(bf16)
    return dh1, dz, dot_nt(dz, out_w).astype(bf16), gain_two_grad


def backward_attention(do, state, tables):
    cosine, sine, allowed = tables
    q, k, v, lse = state[3:7]
    tokens = do.shape[0]
    do = do.reshape(tokens, KEY_VALUE_HEADS, GROUP, HEAD_SIZE)
    prob = jnp.exp(scores_of(q, k, allowed) - lse)
    dv = jnp.einsum("grtu,tgrd->ugd", prob.astype(bf16), do, preferred_element_type=f32)
    dp = jnp.einsum("tgrd,ugd->grtu", do, v, preferred_element_type=f32)
    ds = (prob * (dp - jnp.sum(dp * prob, axis=-1, keepdims=True))).astype(bf16)
    dq = jnp.einsum("grtu,ugd->tgrd", ds, k, preferred_element_type=f32) * HEAD_SIZE**-0.5
    dk = jnp.einsum("grtu,tgrd->ugd", ds, q, preferred_element_type=f32) * HEAD_SIZE**-0.5
    dq = rope(dq, cosine[:, None, None, :], -sine[:, None, None, :])
    dk = rope(dk, cosine[:, None, :], -sine[:, None, :])
    return jnp.concatenate(
        [dq.reshape(tokens, Q_COLS), dk.reshape(tokens, KV_COLS), dv.reshape(tokens, KV_COLS)],
        axis=1,
    ).astype(bf16)


def backward_in(dproj, dh1, state, weights):
    qkv_w, gain_one = weights[0], weights[3]
    u, r1 = state[0], state[1]
    part, gain_one_grad = norm_back(dot_nn(dproj, qkv_w), u, r1, gain_one)
    return dh1 + part, gain_one_grad


def backward(e, state, weights, tables):
    dgate, dup, dm = backward_ffn(e.astype(bf16), state, weights)
    dh1, dz, do, gain_two_grad = backward_mid(e, dm, state, weights)
    dproj = backward_attention(do, state, tables)
    du, gain_one_grad = backward_in(dproj, dh1, state, weights)
    pieces = (state[2], dproj, state[7], dz, state[10], dgate, dup, e.astype(bf16), state[13])
    return du, pieces, jnp.concatenate([gain_one_grad, gain_two_grad])


def ffn_forward_kernel(m_ref, h1_ref, wg_ref, wu_ref, wd_ref, gate_ref, up_ref, act_ref, out_ref):
    flat = lambda ref: ref[...].reshape(-1, ref.shape[-1])
    m = m_ref[...]
    gate = dot_nt(m, flat(wg_ref))
    up = dot_nt(m, flat(wu_ref))
    act = (gate * jax.nn.sigmoid(gate) * up).astype(bf16)
    gate_ref[...] = gate
    up_ref[...] = up
    act_ref[...] = act
    add = dot_nn(act, flat(wd_ref))

    @pl.when(pl.program_id(0) == 0)
    def _():
        out_ref[...] = h1_ref[...] + add

    @pl.when(pl.program_id(0) > 0)
    def _():
        out_ref[...] += add


def ffn_backward_kernel(
    eb_ref, gate_ref, up_ref, wg_ref, wu_ref, wd_ref, both_ref, dm_ref
):
    flat = lambda ref: ref[...].reshape(-1, ref.shape[-1])
    da = dot_nt(eb_ref[...], flat(wd_ref))
    gate = gate_ref[...]
    sig = jax.nn.sigmoid(gate)
    dgate = (da * up_ref[...] * sig * (1.0 + gate * (1.0 - sig))).astype(bf16)
    dup = (da * gate * sig).astype(bf16)
    both_ref[0] = dgate
    both_ref[1] = dup
    add = dot_nn(dgate, flat(wg_ref)) + dot_nn(dup, flat(wu_ref))

    @pl.when(pl.program_id(0) == 0)
    def _():
        dm_ref[...] = add

    @pl.when(pl.program_id(0) > 0)
    def _():
        dm_ref[...] += add


def weight_spec(w, matrix):
    lines, _, _, share, width = w.shape
    return pl.BlockSpec((lines, None, None, share, width), lambda i: (0, i, matrix, 0, 0))


def ffn_call(kernel, w, wholes, blocks, out_blocks):
    lines, steps, _, share, width = w.shape
    tokens, cols = wholes[0].shape[0], lines * share
    whole = pl.BlockSpec((tokens, width), lambda i: (0, 0))
    block = pl.BlockSpec((None, tokens, cols), lambda i: (i, 0, 0))
    out_specs = [
        pl.BlockSpec((None, *shape), lambda i, n=len(shape): (i,) + (0,) * n) for shape, _ in out_blocks
    ]
    return pl.pallas_call(
        kernel,
        grid=(steps,),
        in_specs=[whole] * len(wholes)
        + [block] * len(blocks)
        + [weight_spec(w, matrix) for matrix in (1, 2, 3)],
        out_specs=out_specs + [whole],
        out_shape=[jax.ShapeDtypeStruct((steps, *shape), t) for shape, t in out_blocks]
        + [jax.ShapeDtypeStruct((tokens, width), f32)],
        compiler_params=pltpu.CompilerParams(
            dimension_semantics=("arbitrary",), vmem_limit_bytes=40 * 1024 * 1024
        ),
        cost_estimate=pl.CostEstimate(
            flops=6 * tokens * steps * cols * width,
            bytes_accessed=6 * steps * cols * width,
            transcendentals=tokens * steps * cols,
        ),
    )(*wholes, *blocks, w, w, w)


def ffn_forward(m, h1, w):
    if w.ndim == 5:
        shape = (m.shape[0], w.shape[0] * w.shape[3])
        return ffn_call(ffn_forward_kernel, w, (m, h1), (), [(shape, t) for t in (f32, f32, bf16)])
    gate, up = dot_nt(m, w[0]), dot_nt(m, w[1])
    act = (jax.nn.silu(gate) * up).astype(bf16)
    return gate, up, act, h1 + dot_nn(act, w[2])


def ffn_backward(eb, gate, up, w):
    if w.ndim == 5:
        shape = (2, eb.shape[0], w.shape[0] * w.shape[3])
        both, dm = ffn_call(ffn_backward_kernel, w, (eb,), (gate, up), [(shape, bf16)])
        return both, both, dm
    da = dot_nt(eb, w[2])
    sig = jax.nn.sigmoid(gate)
    dgate = (da * up * sig * (1.0 + gate * (1.0 - sig))).astype(bf16)
    dup = (da * gate * sig).astype(bf16)
    return dgate, dup, dot_nn(dgate, w[0]) + dot_nn(dup, w[1])


def flip(x, bit):
    size = lax.axis_size("dp")
    return lax.ppermute(x, "dp", [(i, i ^ bit) for i in range(size)])


def gather_small(row):
    size = lax.axis_size("dp")
    me = lax.axis_index("dp")
    bit = 1
    while bit < size:
        other = flip(row, bit)
        high = (me & bit) != 0
        row = jnp.concatenate([jnp.where(high, other, row), jnp.where(high, row, other)])
        bit *= 2
    return row


def scatter_small(row):
    size = lax.axis_size("dp")
    me = lax.axis_index("dp")
    bit = size // 2
    while bit >= 1:
        half = row.shape[0] // 2
        low, top = row[:half], row[half:]
        high = (me & bit) != 0
        row = jnp.where(high, top, low) + flip(jnp.where(high, low, top), bit)
        bit //= 2
    return row


def grads_generic(pieces):
    n, dproj, o, dz, m, dgate, dup, eb, act = pieces
    attn = jnp.concatenate([dot_nn(dproj.T, n), dot_nn(o.T, dz)], axis=0)
    both = [
        lax.psum_scatter(g, "dp", scatter_dimension=0, tiled=True)
        for g in (attn, dot_nn(dgate.T, m), dot_nn(dup.T, m), dot_nn(act.T, eb))
    ]
    return both[0], jnp.stack(both[1:])


def z_pairs(x, pairs):
    return lax.ppermute(x, "dp", [(4 * a + i, 4 * b + i) for a, b in pairs for i in range(4)])


def inner_swap(x):
    return z_pairs(x, [(1, 2), (2, 1)])


def at(x, i):
    return lax.dynamic_index_in_dim(x, i, 0, keepdims=False)


def rows_of_plane(x):
    x_y = flip(x, Y_BIT)
    return x, x_y, flip(x, CORE_BIT), flip(x_y, CORE_BIT)


def cols_y(x, y):
    x = x.reshape(2, 2, *x.shape[1:])
    return flip(at(x, 1 - y), Y_BIT)


def cols_core(x, x_y, y, core):
    other = 1 - core
    return flip(jnp.stack([at(x, 2 * y + other), at(x_y, other)]), CORE_BIT)


def plane_kernel(n_rows, split, n_own, picks_ref, *refs):
    cols_ref, y_ref, core_ref = refs[:3]
    rows = [
        jnp.concatenate([r[...] for r in refs[3 + 4 * i : 7 + 4 * i]], axis=0) for i in range(n_rows)
    ]
    rest = refs[3 + 4 * n_rows :]
    extra_ref = rest[0] if n_rows == 2 else None
    outs, total = rest[n_rows - 1 : -1], rest[-1]
    kinds = cols_ref.shape[1]
    height = total.shape[0] // kinds
    share = height // LINE

    def cols_of(j):
        return jnp.concatenate(
            [cols_ref[picks_ref[0], j], y_ref[picks_ref[1], j], core_ref[0, j], core_ref[1, j]], axis=0
        )

    def dot(c, r):
        return lax.dot_general(c, r, (((0,), (0,)), ((), ())), preferred_element_type=f32)

    if n_rows == 1:
        for j in range(kinds):
            total[j * height : (j + 1) * height] = dot(cols_of(j), rows[0])
    else:
        low, top = split
        cols = cols_of(0)
        total[...] = dot(cols, rows[1])
        first = dot(cols, rows[0])
        total[: low * share] = first[: low * share]
        if top > low:

            @pl.when(picks_ref[2] > 0)
            def _():
                total[low * share : top * share] = first[low * share : top * share]

    slot = 3
    for number, ref in enumerate(outs):
        for i in range(ref.shape[0]):
            pick = picks_ref[slot]
            slot += 1
            for j in range(kinds):
                block = total[pl.ds(pl.multiple_of(j * height + pick * share, 8), share)]
                ref[i, j * share : (j + 1) * share] = block.astype(ref.dtype)
            if extra_ref is not None:
                ref[i, share:] = extra_ref[pick].astype(ref.dtype)


def plane_product(cols, x_y, x_core, rows, picks, out_counts, split=None, extra=None):
    _, kinds, tokens, width_cols = cols.shape
    share, width = width_cols // LINE, rows[0][0].shape[1]
    tall = kinds * share + (0 if extra is None else extra.shape[1])
    operands = [cols, x_y, x_core, *[r for chunk in rows for r in chunk]]
    if extra is not None:
        operands.append(extra)
    whole = lambda v: pl.BlockSpec(v.shape, lambda i, picks, n=v.ndim: (0,) * n)
    shapes = [
        jax.ShapeDtypeStruct((count, tall, width), f32 if i == 0 else bf16)
        for i, count in enumerate(out_counts)
    ]
    kernel = lambda *refs: plane_kernel(len(rows), split, out_counts[0], *refs)
    return pl.pallas_call(
        kernel,
        grid_spec=pltpu.PrefetchScalarGridSpec(
            num_scalar_prefetch=1,
            grid=(1,),
            in_specs=[whole(v) for v in operands],
            out_specs=[whole(v) for v in shapes],
            scratch_shapes=[pltpu.VMEM((kinds * LINE * share, width), f32)],
        ),
        out_shape=shapes,
        compiler_params=pltpu.CompilerParams(
            dimension_semantics=("arbitrary",), vmem_limit_bytes=32 * 1024 * 1024
        ),
        cost_estimate=pl.CostEstimate(
            flops=8 * tokens * kinds * width_cols * width * len(rows),
            bytes_accessed=8 * tokens * (kinds * width_cols + width) + 4 * kinds * width_cols * width,
            transcendentals=0,
        ),
    )(jnp.stack([jnp.asarray(p, jnp.int32) for p in picks]), *operands)


LINE = 4


def pair_middle(own, received, z2):
    total = own + received.astype(f32)
    return at(total, z2), at(total, 1 - z2).astype(bf16)


tie = lax.optimization_barrier


def middle_rounds(u, x, weights, tables, me):
    y, core = (me >> 1) & 1, me & 1
    state = forward_attention(u, weights, tables)
    n, m = state[2], state[10]
    gate, up, act, out = ffn_forward(m, state[8], weights[2])
    m_y, n_y = flip(m, Y_BIT), flip(n, Y_BIT)
    gate, up, act, out, m_y, n_y = tie((gate, up, act, out, m_y, n_y))
    state = (*state, gate, up, act)
    act = act[:, None]
    act_y = cols_y(act, y)
    m_all = (m, m_y, flip(m, CORE_BIT), flip(m_y, CORE_BIT))
    n_all = (n, n_y, flip(n, CORE_BIT), flip(n_y, CORE_BIT))
    _, _, dm = backward_ffn(x, state, weights)
    dm, act_y, m_all, n_all = tie((dm, act_y, m_all, n_all))
    act_c = (act, act_y, cols_core(act, act_y, y, core))
    dh1, _, do, _ = backward_mid(x, dm, state, weights)
    dproj = backward_attention(do, state, tables)
    first_grad, _ = backward_in(dproj, dh1, state, weights)
    first_grad, act_c = tie((first_grad.astype(bf16), act_c))
    return out, state, first_grad, (m_all, n_all, act_c)


def last_round(e, state, early, weights, tables, me):
    o = state[7]
    z, y, core = me // 4, (me >> 1) & 1, me & 1
    z2, z1 = z >> 1, z & 1
    m_all, n_all, act_c = early
    tokens, width = o.shape[0], e.shape[1]
    share = act_c[0].shape[3] // LINE
    here = (2 * y + core, core)
    eb = e.astype(bf16)
    eb_y, eb_c = flip(eb, Y_BIT), flip(eb, CORE_BIT)
    both, _, dm = backward_ffn(eb, state, weights)
    both, dm, eb_y, eb_c = tie((both, dm, eb_y, eb_c))
    both_y = cols_y(both, y)
    eb_yc = flip(eb_y, CORE_BIT)
    dm, eb_yc = tie((dm, eb_yc))
    pairs = (z1, 2 + z1, 1 - z1, 3 - z1)
    down_own, down_send = plane_product(*act_c, [(eb, eb_y, eb_c, eb_yc)], (*here, 0, *pairs), (2, 2))
    dm, down_own, down_send = tie((dm, down_own, down_send))
    down_received = flip(down_send, Z1_BIT)
    dh1, dz, do, gain_two_grad = backward_mid(e, dm, state, weights)
    do, dz, both_y, down_own, down_received = tie((do, dz, both_y, down_own, down_received))
    both_c = cols_core(both, both_y, y, core)
    down, down_send = pair_middle(down_own, down_received, z2)
    down_received = flip(down_send, Z2_BIT)
    both_own, both_send = plane_product(both, both_y, both_c, [m_all], (*here, 0, *pairs), (2, 2))
    do, dz, both_own, both_send = tie((do, dz, both_own, both_send))
    both_received = flip(both_send, Z1_BIT)
    dproj = backward_attention(do, state, tables)
    dproj, down_received = tie((dproj, down_received))
    attn_cols = jnp.concatenate([dproj, o], axis=1).reshape(tokens, 4, 4, share)
    attn_cols = attn_cols.transpose(2, 0, 1, 3).reshape(4, 1, tokens, 4 * share)
    attn_y = cols_y(attn_cols, y)
    dz_y, dz_c = flip(dz, Y_BIT), flip(dz, CORE_BIT)
    du, gain_one_grad = backward_in(dproj, dh1, state, weights)
    gain_grad = jnp.concatenate([gain_one_grad, gain_two_grad])
    gain_grad, attn_y, dz_y, dz_c, both_own, both_received = tie(
        (gain_grad, attn_y, dz_y, dz_c, both_own, both_received)
    )
    both, both_send = pair_middle(both_own, both_received, z2)
    both_received = flip(both_send, Z2_BIT)
    gain_grad = gain_grad + flip(gain_grad, CORE_BIT)
    gain_grad = gain_grad + flip(gain_grad, Y_BIT)
    dz_all = (dz, dz_y, dz_c, flip(dz_y, CORE_BIT))
    attn_c = cols_core(attn_cols, attn_y, y, core)
    gain_rows = at(gain_grad.reshape(4, 4, -1).transpose(1, 0, 2), y * 2 + core)[:, None]
    gain_share = gain_rows.shape[-1]
    gain_rows = jnp.pad(gain_rows, ((0, 0), (0, EXTRA_ROWS - 1), (0, width - gain_share)))
    qkv_owners = QKV_COLS // share
    is_qkv = (qkv_owners // 4 * 4 + y * 2 + core < qkv_owners).astype(jnp.int32)
    attn_own, attn_send = plane_product(
        attn_cols,
        attn_y,
        attn_c,
        [n_all, dz_all],
        (*here, is_qkv, *pairs),
        (2, 2),
        (qkv_owners // 4, -(-qkv_owners // 4)),
        gain_rows,
    )
    attn_received = flip(attn_send, Z1_BIT)
    attn_own, attn_received, both_received = tie((attn_own, attn_received, both_received))
    attn, attn_send = pair_middle(attn_own, attn_received, z2)
    attn_received = flip(attn_send, Z2_BIT)
    down = down + down_received.astype(f32)
    both = both + both_received.astype(f32)
    attn = attn + attn_received.astype(f32)
    return (
        du,
        attn[:share],
        jnp.concatenate([both, down]).reshape(3, share, width),
        attn[share : share + 1, :gain_share],
    )


def local(edge_data, segment_ids, attn_weight, ffn_weight, gains):
    micro = segment_ids.shape[0]
    leading = lax.axis_index("section") == 0
    tables = block_tables(segment_ids)
    block, width = edge_data.shape[2], edge_data.shape[3]
    x = edge_data[0].reshape(micro * block, width)
    planes = lax.axis_size("dp") == 16
    me = lax.axis_index("dp")
    attn_own = attn_weight[0].T
    ffn_own = ffn_weight[0].swapaxes(1, 2)
    share = attn_own.shape[0]
    if planes:
        own = jnp.concatenate([attn_own[None], ffn_own], axis=0).reshape(-1, width)
        everything = lax.all_gather(own, "dp", axis=0, tiled=True).reshape(4, 4, 4, share, width)
        attn_t = everything[:, :, 0].reshape(-1, width)
        ffn_t = everything
    else:
        attn_t = lax.all_gather(attn_own, "dp", axis=0, tiled=True)
        ffn_t = lax.all_gather(ffn_own, "dp", axis=1, tiled=True)
    gain_row = gather_small(gains[0]).astype(f32)
    weights = (
        attn_t[:QKV_COLS],
        attn_t[QKV_COLS:],
        ffn_t,
        gain_row[:width],
        gain_row[width:],
    )
    first, _ = forward(x, weights, tables)
    received = lax.ppermute(first.astype(bf16), "section", [(0, 1)])
    u = jnp.where(leading, x, received)
    if planes:
        out, state, first_grad, early = middle_rounds(u, x, weights, tables, me)
        received = lax.ppermute(first_grad, "section", [(1, 0)])
        e = jnp.where(leading, received, x)
        du, attn_rows, ffn_rows, gain_shard = last_round(e, state, early, weights, tables, me)
    else:
        out, state = forward(u, weights, tables)
        first_grad, _, _ = backward(x, state, weights, tables)
        received = lax.ppermute(first_grad.astype(bf16), "section", [(1, 0)])
        e = jnp.where(leading, received, x)
        du, pieces, gain_grad = backward(e, state, weights, tables)
        attn_rows, ffn_rows = grads_generic(pieces)
        gain_shard = scatter_small(gain_grad)[None]
    edge_out = jnp.where(leading, du, out).astype(bf16).reshape(micro, block, width)
    return (
        edge_out[None],
        attn_rows.T[None],
        ffn_rows.swapaxes(1, 2)[None],
        gain_shard,
    )


def solution(mesh):
    in_specs = (
        P("section", None, "dp", None),
        P(None, "dp"),
        P("section", None, "dp"),
        P("section", None, None, "dp"),
        P("section", "dp"),
    )
    out_specs = (
        P("section", None, "dp", None),
        P("section", None, "dp"),
        P("section", None, None, "dp"),
        P("section", "dp"),
    )
    return jax.shard_map(local, mesh=mesh, in_specs=in_specs, out_specs=out_specs, check_vma=False)
```

```python
import jax
import jax.numpy as jnp
from jax import lax
from jax.experimental import pallas as pl
from jax.experimental.pallas import tpu as pltpu
from jax.sharding import PartitionSpec as P

QUERY_HEADS = 15
KEY_VALUE_HEADS = 5
HEAD_SIZE = 64
GROUP = QUERY_HEADS // KEY_VALUE_HEADS
Q_COLS = QUERY_HEADS * HEAD_SIZE
KV_COLS = KEY_VALUE_HEADS * HEAD_SIZE
QKV_COLS = Q_COLS + 2 * KV_COLS

epsilon = 1e-05
theta_base = 100000.0
Z2_BIT, Z1_BIT, Y_BIT, CORE_BIT = 8, 4, 2, 1
EXTRA_ROWS = 8
bf16 = jnp.bfloat16
f32 = jnp.float32


def dot_nn(a, b):
    return lax.dot_general(a, b, (((1,), (0,)), ((), ())), preferred_element_type=f32)


def dot_nt(a, b):
    return lax.dot_general(a, b, (((1,), (1,)), ((), ())), preferred_element_type=f32)


def rope(rows, cosine, sine):
    half = rows.shape[-1] // 2
    a, b = rows[..., :half], rows[..., half:]
    return jnp.concatenate([a * cosine - b * sine, b * cosine + a * sine], axis=-1)


def block_tables(segments):
    micro, block_len = segments.shape
    offsets = jnp.arange(block_len, dtype=jnp.int32)
    same = segments[:, :, None] == segments[:, None, :]
    start = jnp.min(jnp.where(same, offsets, block_len), axis=-1)
    positions = (offsets - start).astype(f32).reshape(-1)
    half = HEAD_SIZE // 2
    frequency = theta_base ** (-(2.0 * jnp.arange(half, dtype=f32)) / HEAD_SIZE)
    angles = positions[:, None] * frequency
    allowed = same & (offsets[:, None] >= offsets[None, :])
    eye = jnp.eye(micro, dtype=bool)
    full = allowed[:, :, None, :] & eye[:, None, :, None]
    total = micro * block_len
    return jnp.cos(angles), jnp.sin(angles), full.reshape(total, total)


def scores_of(q, k, allowed):
    s = jnp.einsum("tgrd,ugd->grtu", q, k, preferred_element_type=f32) * HEAD_SIZE**-0.5
    return jnp.where(allowed, s, -1000000000.0)


def forward_attention(u, weights, tables):
    qkv_w, out_w, ffn_w, gain_one, gain_two = weights
    cosine, sine, allowed = tables
    tokens = u.shape[0]
    u = u.astype(f32)
    r1 = lax.rsqrt(jnp.mean(u * u, axis=-1, keepdims=True) + epsilon)
    n = (u * r1 * gain_one).astype(bf16)
    proj = dot_nt(n, qkv_w)
    q = rope(
        proj[:, :Q_COLS].reshape(tokens, KEY_VALUE_HEADS, GROUP, HEAD_SIZE),
        cosine[:, None, None, :],
        sine[:, None, None, :],
    ).astype(bf16)
    k = rope(
        proj[:, Q_COLS : Q_COLS + KV_COLS].reshape(tokens, KEY_VALUE_HEADS, HEAD_SIZE),
        cosine[:, None, :],
        sine[:, None, :],
    ).astype(bf16)
    v = proj[:, Q_COLS + KV_COLS :].reshape(tokens, KEY_VALUE_HEADS, HEAD_SIZE).astype(bf16)
    masked = scores_of(q, k, allowed)
    peak = jnp.max(masked, axis=-1, keepdims=True)
    lse = peak + jnp.log(jnp.sum(jnp.exp(masked - peak), axis=-1, keepdims=True))
    prob = jnp.exp(masked - lse).astype(bf16)
    o = jnp.einsum("grtu,ugd->tgrd", prob, v, preferred_element_type=f32)
    o = o.reshape(tokens, Q_COLS).astype(bf16)
    h1 = u + dot_nn(o, out_w)
    r2 = lax.rsqrt(jnp.mean(h1 * h1, axis=-1, keepdims=True) + epsilon)
    m = (h1 * r2 * gain_two).astype(bf16)
    return u, r1, n, q, k, v, lse, o, h1, r2, m


def forward(u, weights, tables):
    state = forward_attention(u, weights, tables)
    gate, up, act, out = ffn_forward(state[10], state[8], weights[2])
    return out, (*state, gate, up, act)


def norm_back(grad, rows, r, gain):
    scaled = grad * gain
    part = r * scaled - rows * (r * r * r) * jnp.mean(scaled * rows, axis=-1, keepdims=True)
    return part, jnp.sum(grad * rows * r, axis=0)


def backward_ffn(eb, state, weights):
    gate, up = state[11], state[12]
    return ffn_backward(eb, gate, up, weights[2])


def backward_mid(e, dm, state, weights):
    out_w, gain_two = weights[1], weights[4]
    h1, r2 = state[8], state[9]
    part, gain_two_grad = norm_back(dm, h1, r2, gain_two)
    dh1 = e.astype(f32) + part
    dz = dh1.astype(bf16)
    return dh1, dz, dot_nt(dz, out_w).astype(bf16), gain_two_grad


def backward_attention(do, state, tables):
    cosine, sine, allowed = tables
    q, k, v, lse = state[3:7]
    tokens = do.shape[0]
    do = do.reshape(tokens, KEY_VALUE_HEADS, GROUP, HEAD_SIZE)
    prob = jnp.exp(scores_of(q, k, allowed) - lse)
    dv = jnp.einsum("grtu,tgrd->ugd", prob.astype(bf16), do, preferred_element_type=f32)
    dp = jnp.einsum("tgrd,ugd->grtu", do, v, preferred_element_type=f32)
    ds = (prob * (dp - jnp.sum(dp * prob, axis=-1, keepdims=True))).astype(bf16)
    dq = jnp.einsum("grtu,ugd->tgrd", ds, k, preferred_element_type=f32) * HEAD_SIZE**-0.5
    dk = jnp.einsum("grtu,tgrd->ugd", ds, q, preferred_element_type=f32) * HEAD_SIZE**-0.5
    dq = rope(dq, cosine[:, None, None, :], -sine[:, None, None, :])
    dk = rope(dk, cosine[:, None, :], -sine[:, None, :])
    return jnp.concatenate(
        [dq.reshape(tokens, Q_COLS), dk.reshape(tokens, KV_COLS), dv.reshape(tokens, KV_COLS)],
        axis=1,
    ).astype(bf16)


def backward_in(dproj, dh1, state, weights):
    qkv_w, gain_one = weights[0], weights[3]
    u, r1 = state[0], state[1]
    part, gain_one_grad = norm_back(dot_nn(dproj, qkv_w), u, r1, gain_one)
    return dh1 + part, gain_one_grad


def backward(e, state, weights, tables):
    dgate, dup, dm = backward_ffn(e.astype(bf16), state, weights)
    dh1, dz, do, gain_two_grad = backward_mid(e, dm, state, weights)
    dproj = backward_attention(do, state, tables)
    du, gain_one_grad = backward_in(dproj, dh1, state, weights)
    pieces = (state[2], dproj, state[7], dz, state[10], dgate, dup, e.astype(bf16), state[13])
    return du, pieces, jnp.concatenate([gain_one_grad, gain_two_grad])


def ffn_forward_kernel(m_ref, h1_ref, wg_ref, wu_ref, wd_ref, gate_ref, up_ref, act_ref, out_ref):
    flat = lambda ref: ref[...].reshape(-1, ref.shape[-1])
    m = m_ref[...]
    gate = dot_nt(m, flat(wg_ref))
    up = dot_nt(m, flat(wu_ref))
    act = (gate * jax.nn.sigmoid(gate) * up).astype(bf16)
    gate_ref[...] = gate
    up_ref[...] = up
    act_ref[...] = act
    add = dot_nn(act, flat(wd_ref))

    @pl.when(pl.program_id(0) == 0)
    def _():
        out_ref[...] = h1_ref[...] + add

    @pl.when(pl.program_id(0) > 0)
    def _():
        out_ref[...] += add


def ffn_backward_kernel(
    eb_ref, gate_ref, up_ref, wg_ref, wu_ref, wd_ref, both_ref, dm_ref
):
    flat = lambda ref: ref[...].reshape(-1, ref.shape[-1])
    da = dot_nt(eb_ref[...], flat(wd_ref))
    gate = gate_ref[...]
    sig = jax.nn.sigmoid(gate)
    dgate = (da * up_ref[...] * sig * (1.0 + gate * (1.0 - sig))).astype(bf16)
    dup = (da * gate * sig).astype(bf16)
    both_ref[0] = dgate
    both_ref[1] = dup
    add = dot_nn(dgate, flat(wg_ref)) + dot_nn(dup, flat(wu_ref))

    @pl.when(pl.program_id(0) == 0)
    def _():
        dm_ref[...] = add

    @pl.when(pl.program_id(0) > 0)
    def _():
        dm_ref[...] += add


def weight_spec(w, matrix):
    lines, _, _, share, width = w.shape
    return pl.BlockSpec((lines, None, None, share, width), lambda i: (0, i, matrix, 0, 0))


def ffn_call(kernel, w, wholes, blocks, out_blocks):
    lines, steps, _, share, width = w.shape
    tokens, cols = wholes[0].shape[0], lines * share
    whole = pl.BlockSpec((tokens, width), lambda i: (0, 0))
    block = pl.BlockSpec((None, tokens, cols), lambda i: (i, 0, 0))
    out_specs = [
        pl.BlockSpec((None, *shape), lambda i, n=len(shape): (i,) + (0,) * n) for shape, _ in out_blocks
    ]
    return pl.pallas_call(
        kernel,
        grid=(steps,),
        in_specs=[whole] * len(wholes)
        + [block] * len(blocks)
        + [weight_spec(w, matrix) for matrix in (1, 2, 3)],
        out_specs=out_specs + [whole],
        out_shape=[jax.ShapeDtypeStruct((steps, *shape), t) for shape, t in out_blocks]
        + [jax.ShapeDtypeStruct((tokens, width), f32)],
        compiler_params=pltpu.CompilerParams(
            dimension_semantics=("arbitrary",), vmem_limit_bytes=40 * 1024 * 1024
        ),
        cost_estimate=pl.CostEstimate(
            flops=6 * tokens * steps * cols * width,
            bytes_accessed=6 * steps * cols * width,
            transcendentals=tokens * steps * cols,
        ),
    )(*wholes, *blocks, w, w, w)


def ffn_forward(m, h1, w):
    if w.ndim == 5:
        shape = (m.shape[0], w.shape[0] * w.shape[3])
        return ffn_call(ffn_forward_kernel, w, (m, h1), (), [(shape, t) for t in (f32, f32, bf16)])
    gate, up = dot_nt(m, w[0]), dot_nt(m, w[1])
    act = (jax.nn.silu(gate) * up).astype(bf16)
    return gate, up, act, h1 + dot_nn(act, w[2])


def ffn_backward(eb, gate, up, w):
    if w.ndim == 5:
        shape = (2, eb.shape[0], w.shape[0] * w.shape[3])
        both, dm = ffn_call(ffn_backward_kernel, w, (eb,), (gate, up), [(shape, bf16)])
        return both, both, dm
    da = dot_nt(eb, w[2])
    sig = jax.nn.sigmoid(gate)
    dgate = (da * up * sig * (1.0 + gate * (1.0 - sig))).astype(bf16)
    dup = (da * gate * sig).astype(bf16)
    return dgate, dup, dot_nn(dgate, w[0]) + dot_nn(dup, w[1])


def flip(x, bit):
    size = lax.axis_size("dp")
    return lax.ppermute(x, "dp", [(i, i ^ bit) for i in range(size)])


def gather_small(row):
    size = lax.axis_size("dp")
    me = lax.axis_index("dp")
    bit = 1
    while bit < size:
        other = flip(row, bit)
        high = (me & bit) != 0
        row = jnp.concatenate([jnp.where(high, other, row), jnp.where(high, row, other)])
        bit *= 2
    return row


def scatter_small(row):
    size = lax.axis_size("dp")
    me = lax.axis_index("dp")
    bit = size // 2
    while bit >= 1:
        half = row.shape[0] // 2
        low, top = row[:half], row[half:]
        high = (me & bit) != 0
        row = jnp.where(high, top, low) + flip(jnp.where(high, low, top), bit)
        bit //= 2
    return row


def grads_generic(pieces):
    n, dproj, o, dz, m, dgate, dup, eb, act = pieces
    attn = jnp.concatenate([dot_nn(dproj.T, n), dot_nn(o.T, dz)], axis=0)
    both = [
        lax.psum_scatter(g, "dp", scatter_dimension=0, tiled=True)
        for g in (attn, dot_nn(dgate.T, m), dot_nn(dup.T, m), dot_nn(act.T, eb))
    ]
    return both[0], jnp.stack(both[1:])


def z_pairs(x, pairs):
    return lax.ppermute(x, "dp", [(4 * a + i, 4 * b + i) for a, b in pairs for i in range(4)])


def inner_swap(x):
    return z_pairs(x, [(1, 2), (2, 1)])


def at(x, i):
    return lax.dynamic_index_in_dim(x, i, 0, keepdims=False)


def rows_of_plane(x):
    x_y = flip(x, Y_BIT)
    return x, x_y, flip(x, CORE_BIT), flip(x_y, CORE_BIT)


def cols_y(x, y):
    x = x.reshape(2, 2, *x.shape[1:])
    return flip(at(x, 1 - y), Y_BIT)


def cols_core(x, x_y, y, core):
    other = 1 - core
    return flip(jnp.stack([at(x, 2 * y + other), at(x_y, other)]), CORE_BIT)


def plane_kernel(n_rows, split, out_kinds, picks_ref, *refs):
    cols_ref, y_ref, core_ref = refs[:3]
    rows = [
        jnp.concatenate([r[...] for r in refs[3 + 4 * i : 7 + 4 * i]], axis=0) for i in range(n_rows)
    ]
    rest = refs[3 + 4 * n_rows :]
    extra_ref = rest[0] if n_rows == 2 else None
    outs, total = rest[n_rows - 1 : -1], rest[-1]
    kinds = cols_ref.shape[1]
    height = total.shape[0] // kinds
    share = height // LINE

    def cols_of(j):
        return jnp.concatenate(
            [cols_ref[picks_ref[0], j], y_ref[picks_ref[1], j], core_ref[0, j], core_ref[1, j]], axis=0
        )

    def dot(c, r):
        return lax.dot_general(c, r, (((0,), (0,)), ((), ())), preferred_element_type=f32)

    if n_rows == 1:
        for j in range(kinds):
            total[j * height : (j + 1) * height] = dot(cols_of(j), rows[0])
    else:
        low, top = split
        cols = cols_of(0)
        total[...] = dot(cols, rows[1])
        first = dot(cols, rows[0])
        total[: low * share] = first[: low * share]
        if top > low:

            @pl.when(picks_ref[2] > 0)
            def _():
                total[low * share : top * share] = first[low * share : top * share]

    slot = 3
    for number, ref in enumerate(outs):
        for i in range(ref.shape[0]):
            pick = picks_ref[slot]
            slot += 1
            first = out_kinds[number][0]
            for j in out_kinds[number]:
                block = total[pl.ds(pl.multiple_of(j * height + pick * share, 8), share)]
                ref[i, (j - first) * share : (j - first + 1) * share] = block.astype(ref.dtype)
            if extra_ref is not None:
                ref[i, share:] = extra_ref[pick].astype(ref.dtype)


def plane_product(cols, x_y, x_core, rows, picks, split=None, extra=None):
    _, kinds, tokens, width_cols = cols.shape
    share, width = width_cols // LINE, rows[0][0].shape[1]
    out_kinds = [tuple(range(kinds)), *((j,) for j in range(kinds))]
    more = 0 if extra is None else extra.shape[1]
    operands = [cols, x_y, x_core, *[r for chunk in rows for r in chunk]]
    if extra is not None:
        operands.append(extra)
    whole = lambda v: pl.BlockSpec(v.shape, lambda i, picks, n=v.ndim: (0,) * n)
    shapes = [
        jax.ShapeDtypeStruct((2, len(k) * share + more, width), f32 if i == 0 else bf16)
        for i, k in enumerate(out_kinds)
    ]
    kernel = lambda *refs: plane_kernel(len(rows), split, out_kinds, *refs)
    return pl.pallas_call(
        kernel,
        grid_spec=pltpu.PrefetchScalarGridSpec(
            num_scalar_prefetch=1,
            grid=(1,),
            in_specs=[whole(v) for v in operands],
            out_specs=[whole(v) for v in shapes],
            scratch_shapes=[pltpu.VMEM((kinds * LINE * share, width), f32)],
        ),
        out_shape=shapes,
        compiler_params=pltpu.CompilerParams(
            dimension_semantics=("arbitrary",), vmem_limit_bytes=32 * 1024 * 1024
        ),
        cost_estimate=pl.CostEstimate(
            flops=8 * tokens * kinds * width_cols * width * len(rows),
            bytes_accessed=8 * tokens * (kinds * width_cols + width) + 4 * kinds * width_cols * width,
            transcendentals=0,
        ),
    )(jnp.stack([jnp.asarray(p, jnp.int32) for p in picks]), *operands)


LINE = 4


def pair_middle(own, received, z2):
    total = own + received.astype(f32)
    return at(total, z2), at(total, 1 - z2).astype(bf16)


tie = lax.optimization_barrier


def middle_rounds(u, x, weights, tables, me):
    y, core = (me >> 1) & 1, me & 1
    state = forward_attention(u, weights, tables)
    n, m = state[2], state[10]
    gate, up, act, out = ffn_forward(m, state[8], weights[2])
    m_y, n_y = flip(m, Y_BIT), flip(n, Y_BIT)
    gate, up, act, out, m_y, n_y = tie((gate, up, act, out, m_y, n_y))
    state = (*state, gate, up, act)
    act = act[:, None]
    act_y = cols_y(act, y)
    m_all = (m, m_y, flip(m, CORE_BIT), flip(m_y, CORE_BIT))
    n_all = (n, n_y, flip(n, CORE_BIT), flip(n_y, CORE_BIT))
    _, _, dm = backward_ffn(x, state, weights)
    dm, act_y, m_all, n_all = tie((dm, act_y, m_all, n_all))
    act_c = (act, act_y, cols_core(act, act_y, y, core))
    dh1, _, do, _ = backward_mid(x, dm, state, weights)
    dproj = backward_attention(do, state, tables)
    first_grad, _ = backward_in(dproj, dh1, state, weights)
    first_grad, act_c = tie((first_grad.astype(bf16), act_c))
    return out, state, first_grad, (m_all, n_all, act_c)


def last_round(e, state, early, weights, tables, me):
    o = state[7]
    z, y, core = me // 4, (me >> 1) & 1, me & 1
    z2, z1 = z >> 1, z & 1
    m_all, n_all, act_c = early
    tokens, width = o.shape[0], e.shape[1]
    share = act_c[0].shape[3] // LINE
    here = (2 * y + core, core)
    eb = e.astype(bf16)
    eb_y, eb_c = flip(eb, Y_BIT), flip(eb, CORE_BIT)
    both, _, dm = backward_ffn(eb, state, weights)
    both, dm, eb_y, eb_c = tie((both, dm, eb_y, eb_c))
    both_y = cols_y(both, y)
    eb_yc = flip(eb_y, CORE_BIT)
    dm, eb_yc = tie((dm, eb_yc))
    pairs = (z1, 2 + z1, 1 - z1, 3 - z1)
    down_own, down_send = plane_product(*act_c, [(eb, eb_y, eb_c, eb_yc)], (*here, 0, *pairs))
    dm, down_own, down_send = tie((dm, down_own, down_send))
    down_received = flip(down_send, Z1_BIT)
    dh1, dz, do, gain_two_grad = backward_mid(e, dm, state, weights)
    do, dz, both_y, down_own, down_received = tie((do, dz, both_y, down_own, down_received))
    both_c = cols_core(both, both_y, y, core)
    down, down_send = pair_middle(down_own, down_received, z2)
    down_received = flip(down_send, Z2_BIT)
    both_own, gate_send, up_send = plane_product(
        both, both_y, both_c, [m_all], (*here, 0, *pairs, *pairs[2:])
    )
    do, dz, both_own, gate_send, up_send = tie((do, dz, both_own, gate_send, up_send))
    gate_received, up_received = flip(gate_send, Z1_BIT), flip(up_send, Z1_BIT)
    dproj = backward_attention(do, state, tables)
    dproj, down_received = tie((dproj, down_received))
    attn_cols = jnp.concatenate([dproj, o], axis=1).reshape(tokens, 4, 4, share)
    attn_cols = attn_cols.transpose(2, 0, 1, 3).reshape(4, 1, tokens, 4 * share)
    attn_y = cols_y(attn_cols, y)
    dz_y, dz_c = flip(dz, Y_BIT), flip(dz, CORE_BIT)
    du, gain_one_grad = backward_in(dproj, dh1, state, weights)
    gain_grad = jnp.concatenate([gain_one_grad, gain_two_grad])
    gain_grad, attn_y, dz_y, dz_c, both_own, gate_received = tie(
        (gain_grad, attn_y, dz_y, dz_c, both_own, gate_received)
    )
    gate, gate_send = pair_middle(both_own[:, :share], gate_received, z2)
    gate_received = flip(gate_send, Z2_BIT)
    gain_grad = gain_grad + flip(gain_grad, CORE_BIT)
    gain_grad = gain_grad + flip(gain_grad, Y_BIT)
    dz_all = (dz, dz_y, dz_c, flip(dz_y, CORE_BIT))
    attn_c = cols_core(attn_cols, attn_y, y, core)
    gain_grad, dz_all, attn_c, both_own, up_received, gate_received = tie(
        (gain_grad, dz_all, attn_c, both_own, up_received, gate_received)
    )
    up, up_send = pair_middle(both_own[:, share:], up_received, z2)
    up_received = flip(up_send, Z2_BIT)
    gain_rows = at(gain_grad.reshape(4, 4, -1).transpose(1, 0, 2), y * 2 + core)[:, None]
    gain_share = gain_rows.shape[-1]
    gain_rows = jnp.pad(gain_rows, ((0, 0), (0, EXTRA_ROWS - 1), (0, width - gain_share)))
    qkv_owners = QKV_COLS // share
    is_qkv = (qkv_owners // 4 * 4 + y * 2 + core < qkv_owners).astype(jnp.int32)
    attn_own, attn_send = plane_product(
        attn_cols,
        attn_y,
        attn_c,
        [n_all, dz_all],
        (*here, is_qkv, *pairs),
        (qkv_owners // 4, -(-qkv_owners // 4)),
        gain_rows,
    )
    attn_received = flip(attn_send, Z1_BIT)
    attn_own, attn_received, up_received = tie((attn_own, attn_received, up_received))
    attn, attn_send = pair_middle(attn_own, attn_received, z2)
    attn_received = flip(attn_send, Z2_BIT)
    down = down + down_received.astype(f32)
    gate = gate + gate_received.astype(f32)
    up = up + up_received.astype(f32)
    attn = attn + attn_received.astype(f32)
    return (
        du,
        attn[:share],
        jnp.stack([gate, up, down]),
        attn[share : share + 1, :gain_share],
    )


def local(edge_data, segment_ids, attn_weight, ffn_weight, gains):
    micro = segment_ids.shape[0]
    leading = lax.axis_index("section") == 0
    tables = block_tables(segment_ids)
    block, width = edge_data.shape[2], edge_data.shape[3]
    x = edge_data[0].reshape(micro * block, width)
    planes = lax.axis_size("dp") == 16
    me = lax.axis_index("dp")
    attn_own = attn_weight[0].T
    ffn_own = ffn_weight[0].swapaxes(1, 2)
    share = attn_own.shape[0]
    if planes:
        own = jnp.concatenate([attn_own[None], ffn_own], axis=0).reshape(-1, width)
        everything = lax.all_gather(own, "dp", axis=0, tiled=True).reshape(4, 4, 4, share, width)
        attn_t = everything[:, :, 0].reshape(-1, width)
        ffn_t = everything
    else:
        attn_t = lax.all_gather(attn_own, "dp", axis=0, tiled=True)
        ffn_t = lax.all_gather(ffn_own, "dp", axis=1, tiled=True)
    gain_row = gather_small(gains[0]).astype(f32)
    weights = (
        attn_t[:QKV_COLS],
        attn_t[QKV_COLS:],
        ffn_t,
        gain_row[:width],
        gain_row[width:],
    )
    first, _ = forward(x, weights, tables)
    received = lax.ppermute(first.astype(bf16), "section", [(0, 1)])
    u = jnp.where(leading, x, received)
    if planes:
        out, state, first_grad, early = middle_rounds(u, x, weights, tables, me)
        received = lax.ppermute(first_grad, "section", [(1, 0)])
        e = jnp.where(leading, received, x)
        du, attn_rows, ffn_rows, gain_shard = last_round(e, state, early, weights, tables, me)
    else:
        out, state = forward(u, weights, tables)
        first_grad, _, _ = backward(x, state, weights, tables)
        received = lax.ppermute(first_grad.astype(bf16), "section", [(1, 0)])
        e = jnp.where(leading, received, x)
        du, pieces, gain_grad = backward(e, state, weights, tables)
        attn_rows, ffn_rows = grads_generic(pieces)
        gain_shard = scatter_small(gain_grad)[None]
    edge_out = jnp.where(leading, du, out).astype(bf16).reshape(micro, block, width)
    return (
        edge_out[None],
        attn_rows.T[None],
        ffn_rows.swapaxes(1, 2)[None],
        gain_shard,
    )


def solution(mesh):
    in_specs = (
        P("section", None, "dp", None),
        P(None, "dp"),
        P("section", None, "dp"),
        P("section", None, None, "dp"),
        P("section", "dp"),
    )
    out_specs = (
        P("section", None, "dp", None),
        P("section", None, "dp"),
        P("section", None, None, "dp"),
        P("section", "dp"),
    )
    return jax.shard_map(local, mesh=mesh, in_specs=in_specs, out_specs=out_specs, check_vma=False)
```

```python
import jax
import jax.numpy as jnp
from jax import lax
from jax.experimental import pallas as pl
from jax.experimental.pallas import tpu as pltpu
from jax.sharding import PartitionSpec as P

QUERY_HEADS = 15
KEY_VALUE_HEADS = 5
HEAD_SIZE = 64
GROUP = QUERY_HEADS // KEY_VALUE_HEADS
Q_COLS = QUERY_HEADS * HEAD_SIZE
KV_COLS = KEY_VALUE_HEADS * HEAD_SIZE
QKV_COLS = Q_COLS + 2 * KV_COLS

epsilon = 1e-05
theta_base = 100000.0
Z2_BIT, Z1_BIT, Y_BIT, CORE_BIT = 8, 4, 2, 1
EXTRA_ROWS = 8
bf16 = jnp.bfloat16
f32 = jnp.float32


def dot_nn(a, b):
    return lax.dot_general(a, b, (((1,), (0,)), ((), ())), preferred_element_type=f32)


def dot_nt(a, b):
    return lax.dot_general(a, b, (((1,), (1,)), ((), ())), preferred_element_type=f32)


def rope(rows, cosine, sine):
    half = rows.shape[-1] // 2
    a, b = rows[..., :half], rows[..., half:]
    return jnp.concatenate([a * cosine - b * sine, b * cosine + a * sine], axis=-1)


def block_tables(segments):
    micro, block_len = segments.shape
    offsets = jnp.arange(block_len, dtype=jnp.int32)
    same = segments[:, :, None] == segments[:, None, :]
    start = jnp.min(jnp.where(same, offsets, block_len), axis=-1)
    positions = (offsets - start).astype(f32).reshape(-1)
    half = HEAD_SIZE // 2
    frequency = theta_base ** (-(2.0 * jnp.arange(half, dtype=f32)) / HEAD_SIZE)
    angles = positions[:, None] * frequency
    allowed = same & (offsets[:, None] >= offsets[None, :])
    eye = jnp.eye(micro, dtype=bool)
    full = allowed[:, :, None, :] & eye[:, None, :, None]
    total = micro * block_len
    return jnp.cos(angles), jnp.sin(angles), full.reshape(total, total)


def scores_of(q, k, allowed):
    s = jnp.einsum("tgrd,ugd->grtu", q, k, preferred_element_type=f32) * HEAD_SIZE**-0.5
    return jnp.where(allowed, s, -1000000000.0)


def forward_attention(u, weights, tables):
    qkv_w, out_w, ffn_w, gain_one, gain_two = weights
    cosine, sine, allowed = tables
    tokens = u.shape[0]
    u = u.astype(f32)
    r1 = lax.rsqrt(jnp.mean(u * u, axis=-1, keepdims=True) + epsilon)
    n = (u * r1 * gain_one).astype(bf16)
    proj = dot_nt(n, qkv_w)
    q = rope(
        proj[:, :Q_COLS].reshape(tokens, KEY_VALUE_HEADS, GROUP, HEAD_SIZE),
        cosine[:, None, None, :],
        sine[:, None, None, :],
    ).astype(bf16)
    k = rope(
        proj[:, Q_COLS : Q_COLS + KV_COLS].reshape(tokens, KEY_VALUE_HEADS, HEAD_SIZE),
        cosine[:, None, :],
        sine[:, None, :],
    ).astype(bf16)
    v = proj[:, Q_COLS + KV_COLS :].reshape(tokens, KEY_VALUE_HEADS, HEAD_SIZE).astype(bf16)
    masked = scores_of(q, k, allowed)
    peak = jnp.max(masked, axis=-1, keepdims=True)
    lse = peak + jnp.log(jnp.sum(jnp.exp(masked - peak), axis=-1, keepdims=True))
    prob = jnp.exp(masked - lse).astype(bf16)
    o = jnp.einsum("grtu,ugd->tgrd", prob, v, preferred_element_type=f32)
    o = o.reshape(tokens, Q_COLS).astype(bf16)
    h1 = u + dot_nn(o, out_w)
    r2 = lax.rsqrt(jnp.mean(h1 * h1, axis=-1, keepdims=True) + epsilon)
    m = (h1 * r2 * gain_two).astype(bf16)
    return u, r1, n, q, k, v, lse, o, h1, r2, m


def forward(u, weights, tables):
    state = forward_attention(u, weights, tables)
    gate, up, act, out = ffn_forward(state[10], state[8], weights[2])
    return out, (*state, gate, up, act)


def norm_back(grad, rows, r, gain):
    scaled = grad * gain
    part = r * scaled - rows * (r * r * r) * jnp.mean(scaled * rows, axis=-1, keepdims=True)
    return part, jnp.sum(grad * rows * r, axis=0)


def backward_ffn(eb, state, weights):
    gate, up = state[11], state[12]
    return ffn_backward(eb, gate, up, weights[2])


def backward_mid(e, dm, state, weights):
    out_w, gain_two = weights[1], weights[4]
    h1, r2 = state[8], state[9]
    part, gain_two_grad = norm_back(dm, h1, r2, gain_two)
    dh1 = e.astype(f32) + part
    dz = dh1.astype(bf16)
    return dh1, dz, dot_nt(dz, out_w).astype(bf16), gain_two_grad


def backward_attention(do, state, tables):
    cosine, sine, allowed = tables
    q, k, v, lse = state[3:7]
    tokens = do.shape[0]
    do = do.reshape(tokens, KEY_VALUE_HEADS, GROUP, HEAD_SIZE)
    prob = jnp.exp(scores_of(q, k, allowed) - lse)
    dv = jnp.einsum("grtu,tgrd->ugd", prob.astype(bf16), do, preferred_element_type=f32)
    dp = jnp.einsum("tgrd,ugd->grtu", do, v, preferred_element_type=f32)
    ds = (prob * (dp - jnp.sum(dp * prob, axis=-1, keepdims=True))).astype(bf16)
    dq = jnp.einsum("grtu,ugd->tgrd", ds, k, preferred_element_type=f32) * HEAD_SIZE**-0.5
    dk = jnp.einsum("grtu,tgrd->ugd", ds, q, preferred_element_type=f32) * HEAD_SIZE**-0.5
    dq = rope(dq, cosine[:, None, None, :], -sine[:, None, None, :])
    dk = rope(dk, cosine[:, None, :], -sine[:, None, :])
    return jnp.concatenate(
        [dq.reshape(tokens, Q_COLS), dk.reshape(tokens, KV_COLS), dv.reshape(tokens, KV_COLS)],
        axis=1,
    ).astype(bf16)


def backward_in(dproj, dh1, state, weights):
    qkv_w, gain_one = weights[0], weights[3]
    u, r1 = state[0], state[1]
    part, gain_one_grad = norm_back(dot_nn(dproj, qkv_w), u, r1, gain_one)
    return dh1 + part, gain_one_grad


def backward(e, state, weights, tables):
    dgate, dup, dm = backward_ffn(e.astype(bf16), state, weights)
    dh1, dz, do, gain_two_grad = backward_mid(e, dm, state, weights)
    dproj = backward_attention(do, state, tables)
    du, gain_one_grad = backward_in(dproj, dh1, state, weights)
    pieces = (state[2], dproj, state[7], dz, state[10], dgate, dup, e.astype(bf16), state[13])
    return du, pieces, jnp.concatenate([gain_one_grad, gain_two_grad])


def ffn_forward_kernel(m_ref, h1_ref, wg_ref, wu_ref, wd_ref, gate_ref, up_ref, act_ref, out_ref):
    flat = lambda ref: ref[...].reshape(-1, ref.shape[-1])
    m = m_ref[...]
    gate = dot_nt(m, flat(wg_ref))
    up = dot_nt(m, flat(wu_ref))
    act = (gate * jax.nn.sigmoid(gate) * up).astype(bf16)
    gate_ref[...] = gate
    up_ref[...] = up
    act_ref[...] = act
    add = dot_nn(act, flat(wd_ref))

    @pl.when(pl.program_id(0) == 0)
    def _():
        out_ref[...] = h1_ref[...] + add

    @pl.when(pl.program_id(0) > 0)
    def _():
        out_ref[...] += add


def ffn_backward_kernel(
    eb_ref, gate_ref, up_ref, wg_ref, wu_ref, wd_ref, both_ref, dm_ref
):
    flat = lambda ref: ref[...].reshape(-1, ref.shape[-1])
    da = dot_nt(eb_ref[...], flat(wd_ref))
    gate = gate_ref[...]
    sig = jax.nn.sigmoid(gate)
    dgate = (da * up_ref[...] * sig * (1.0 + gate * (1.0 - sig))).astype(bf16)
    dup = (da * gate * sig).astype(bf16)
    both_ref[0] = dgate
    both_ref[1] = dup
    add = dot_nn(dgate, flat(wg_ref)) + dot_nn(dup, flat(wu_ref))

    @pl.when(pl.program_id(0) == 0)
    def _():
        dm_ref[...] = add

    @pl.when(pl.program_id(0) > 0)
    def _():
        dm_ref[...] += add


def weight_spec(w, matrix):
    lines, _, _, share, width = w.shape
    return pl.BlockSpec((lines, None, None, share, width), lambda i: (0, i, matrix, 0, 0))


def ffn_call(kernel, w, wholes, blocks, out_blocks):
    lines, steps, _, share, width = w.shape
    tokens, cols = wholes[0].shape[0], lines * share
    whole = pl.BlockSpec((tokens, width), lambda i: (0, 0))
    block = pl.BlockSpec((None, tokens, cols), lambda i: (i, 0, 0))
    out_specs = [
        pl.BlockSpec((None, *shape), lambda i, n=len(shape): (i,) + (0,) * n) for shape, _ in out_blocks
    ]
    return pl.pallas_call(
        kernel,
        grid=(steps,),
        in_specs=[whole] * len(wholes)
        + [block] * len(blocks)
        + [weight_spec(w, matrix) for matrix in (1, 2, 3)],
        out_specs=out_specs + [whole],
        out_shape=[jax.ShapeDtypeStruct((steps, *shape), t) for shape, t in out_blocks]
        + [jax.ShapeDtypeStruct((tokens, width), f32)],
        compiler_params=pltpu.CompilerParams(
            dimension_semantics=("arbitrary",), vmem_limit_bytes=60 * 1024 * 1024
        ),
        cost_estimate=pl.CostEstimate(
            flops=6 * tokens * steps * cols * width,
            bytes_accessed=6 * steps * cols * width,
            transcendentals=tokens * steps * cols,
        ),
    )(*wholes, *blocks, w, w, w)


def ffn_forward(m, h1, w):
    if w.ndim == 5:
        shape = (m.shape[0], w.shape[0] * w.shape[3])
        return ffn_call(ffn_forward_kernel, w, (m, h1), (), [(shape, t) for t in (f32, f32, bf16)])
    gate, up = dot_nt(m, w[0]), dot_nt(m, w[1])
    act = (jax.nn.silu(gate) * up).astype(bf16)
    return gate, up, act, h1 + dot_nn(act, w[2])


def ffn_backward(eb, gate, up, w):
    if w.ndim == 5:
        shape = (2, eb.shape[0], w.shape[0] * w.shape[3])
        both, dm = ffn_call(ffn_backward_kernel, w, (eb,), (gate, up), [(shape, bf16)])
        return both, both, dm
    da = dot_nt(eb, w[2])
    sig = jax.nn.sigmoid(gate)
    dgate = (da * up * sig * (1.0 + gate * (1.0 - sig))).astype(bf16)
    dup = (da * gate * sig).astype(bf16)
    return dgate, dup, dot_nn(dgate, w[0]) + dot_nn(dup, w[1])


def flip(x, bit):
    size = lax.axis_size("dp")
    return lax.ppermute(x, "dp", [(i, i ^ bit) for i in range(size)])


def gather_small(row):
    size = lax.axis_size("dp")
    me = lax.axis_index("dp")
    bit = 1
    while bit < size:
        other = flip(row, bit)
        high = (me & bit) != 0
        row = jnp.concatenate([jnp.where(high, other, row), jnp.where(high, row, other)])
        bit *= 2
    return row


def scatter_small(row):
    size = lax.axis_size("dp")
    me = lax.axis_index("dp")
    bit = size // 2
    while bit >= 1:
        half = row.shape[0] // 2
        low, top = row[:half], row[half:]
        high = (me & bit) != 0
        row = jnp.where(high, top, low) + flip(jnp.where(high, low, top), bit)
        bit //= 2
    return row


def grads_generic(pieces):
    n, dproj, o, dz, m, dgate, dup, eb, act = pieces
    attn = jnp.concatenate([dot_nn(dproj.T, n), dot_nn(o.T, dz)], axis=0)
    both = [
        lax.psum_scatter(g, "dp", scatter_dimension=0, tiled=True)
        for g in (attn, dot_nn(dgate.T, m), dot_nn(dup.T, m), dot_nn(act.T, eb))
    ]
    return both[0], jnp.stack(both[1:])


def z_pairs(x, pairs):
    return lax.ppermute(x, "dp", [(4 * a + i, 4 * b + i) for a, b in pairs for i in range(4)])


def inner_swap(x):
    return z_pairs(x, [(1, 2), (2, 1)])


def at(x, i):
    return lax.dynamic_index_in_dim(x, i, 0, keepdims=False)


def rows_of_plane(x):
    x_y = flip(x, Y_BIT)
    return x, x_y, flip(x, CORE_BIT), flip(x_y, CORE_BIT)


def cols_y(x, y):
    x = x.reshape(2, 2, *x.shape[1:])
    return flip(at(x, 1 - y), Y_BIT)


def cols_core(x, x_y, y, core):
    other = 1 - core
    return flip(jnp.stack([at(x, 2 * y + other), at(x_y, other)]), CORE_BIT)


def plane_kernel(n_rows, split, out_kinds, picks_ref, *refs):
    cols_ref, y_ref, core_ref = refs[:3]
    rows = [
        jnp.concatenate([r[...] for r in refs[3 + 4 * i : 7 + 4 * i]], axis=0) for i in range(n_rows)
    ]
    rest = refs[3 + 4 * n_rows :]
    extra_ref = rest[0] if n_rows == 2 else None
    outs, total = rest[n_rows - 1 : -1], rest[-1]
    kinds = cols_ref.shape[1]
    height = total.shape[0] // kinds
    share = height // LINE

    def cols_of(j):
        return jnp.concatenate(
            [cols_ref[picks_ref[0], j], y_ref[picks_ref[1], j], core_ref[0, j], core_ref[1, j]], axis=0
        )

    def dot(c, r):
        return lax.dot_general(c, r, (((0,), (0,)), ((), ())), preferred_element_type=f32)

    if n_rows == 1:
        for j in range(kinds):
            total[j * height : (j + 1) * height] = dot(cols_of(j), rows[0])
    else:
        low, top = split
        cols = cols_of(0)
        total[...] = dot(cols, rows[1])
        first = dot(cols, rows[0])
        total[: low * share] = first[: low * share]
        if top > low:

            @pl.when(picks_ref[2] > 0)
            def _():
                total[low * share : top * share] = first[low * share : top * share]

    slot = 3
    for number, ref in enumerate(outs):
        for i in range(ref.shape[0]):
            pick = picks_ref[slot]
            slot += 1
            first = out_kinds[number][0]
            for j in out_kinds[number]:
                block = total[pl.ds(pl.multiple_of(j * height + pick * share, 8), share)]
                ref[i, (j - first) * share : (j - first + 1) * share] = block.astype(ref.dtype)
            if extra_ref is not None:
                ref[i, share:] = extra_ref[pick].astype(ref.dtype)


def plane_product(cols, x_y, x_core, rows, picks, split=None, extra=None):
    _, kinds, tokens, width_cols = cols.shape
    share, width = width_cols // LINE, rows[0][0].shape[1]
    out_kinds = [tuple(range(kinds)), *((j,) for j in range(kinds))]
    more = 0 if extra is None else extra.shape[1]
    operands = [cols, x_y, x_core, *[r for chunk in rows for r in chunk]]
    if extra is not None:
        operands.append(extra)
    whole = lambda v: pl.BlockSpec(v.shape, lambda i, picks, n=v.ndim: (0,) * n)
    shapes = [
        jax.ShapeDtypeStruct((2, len(k) * share + more, width), f32 if i == 0 else bf16)
        for i, k in enumerate(out_kinds)
    ]
    kernel = lambda *refs: plane_kernel(len(rows), split, out_kinds, *refs)
    return pl.pallas_call(
        kernel,
        grid_spec=pltpu.PrefetchScalarGridSpec(
            num_scalar_prefetch=1,
            grid=(1,),
            in_specs=[whole(v) for v in operands],
            out_specs=[whole(v) for v in shapes],
            scratch_shapes=[pltpu.VMEM((kinds * LINE * share, width), f32)],
        ),
        out_shape=shapes,
        compiler_params=pltpu.CompilerParams(
            dimension_semantics=("arbitrary",), vmem_limit_bytes=60 * 1024 * 1024
        ),
        cost_estimate=pl.CostEstimate(
            flops=8 * tokens * kinds * width_cols * width * len(rows),
            bytes_accessed=8 * tokens * (kinds * width_cols + width) + 4 * kinds * width_cols * width,
            transcendentals=0,
        ),
    )(jnp.stack([jnp.asarray(p, jnp.int32) for p in picks]), *operands)


LINE = 4


def pair_middle(own, received, z2):
    total = own + received.astype(f32)
    return at(total, z2), at(total, 1 - z2).astype(bf16)


tie = lax.optimization_barrier


def middle_rounds(u, x, weights, tables, me):
    y, core = (me >> 1) & 1, me & 1
    state = forward_attention(u, weights, tables)
    n, m = state[2], state[10]
    gate, up, act, out = ffn_forward(m, state[8], weights[2])
    m_y, n_y = flip(m, Y_BIT), flip(n, Y_BIT)
    gate, up, act, out, m_y, n_y = tie((gate, up, act, out, m_y, n_y))
    state = (*state, gate, up, act)
    act = act[:, None]
    act_y = cols_y(act, y)
    m_all = (m, m_y, flip(m, CORE_BIT), flip(m_y, CORE_BIT))
    n_all = (n, n_y, flip(n, CORE_BIT), flip(n_y, CORE_BIT))
    _, _, dm = backward_ffn(x, state, weights)
    dm, act_y, m_all, n_all = tie((dm, act_y, m_all, n_all))
    act_c = (act, act_y, cols_core(act, act_y, y, core))
    dh1, _, do, _ = backward_mid(x, dm, state, weights)
    dproj = backward_attention(do, state, tables)
    first_grad, _ = backward_in(dproj, dh1, state, weights)
    first_grad, act_c = tie((first_grad.astype(bf16), act_c))
    return out, state, first_grad, (m_all, n_all, act_c)


def last_round(e, state, early, weights, tables, me):
    o = state[7]
    z, y, core = me // 4, (me >> 1) & 1, me & 1
    z2, z1 = z >> 1, z & 1
    m_all, n_all, act_c = early
    tokens, width = o.shape[0], e.shape[1]
    share = act_c[0].shape[3] // LINE
    here = (2 * y + core, core)
    eb = e.astype(bf16)
    eb_y, eb_c = flip(eb, Y_BIT), flip(eb, CORE_BIT)
    both, _, dm = backward_ffn(eb, state, weights)
    both, dm, eb_y, eb_c = tie((both, dm, eb_y, eb_c))
    both_y = cols_y(both, y)
    eb_yc = flip(eb_y, CORE_BIT)
    dm, eb_yc = tie((dm, eb_yc))
    pairs = (z1, 2 + z1, 1 - z1, 3 - z1)
    down_own, down_send = plane_product(*act_c, [(eb, eb_y, eb_c, eb_yc)], (*here, 0, *pairs))
    dm, down_own, down_send = tie((dm, down_own, down_send))
    down_received = flip(down_send, Z1_BIT)
    dh1, dz, do, gain_two_grad = backward_mid(e, dm, state, weights)
    do, dz, both_y, down_own, down_received = tie((do, dz, both_y, down_own, down_received))
    both_c = cols_core(both, both_y, y, core)
    down, down_send = pair_middle(down_own, down_received, z2)
    down_received = flip(down_send, Z2_BIT)
    both_own, gate_send, up_send = plane_product(
        both, both_y, both_c, [m_all], (*here, 0, *pairs, *pairs[2:])
    )
    do, dz, both_own, gate_send, up_send = tie((do, dz, both_own, gate_send, up_send))
    gate_received, up_received = flip(gate_send, Z1_BIT), flip(up_send, Z1_BIT)
    dproj = backward_attention(do, state, tables)
    dproj, down_received = tie((dproj, down_received))
    attn_cols = jnp.concatenate([dproj, o], axis=1).reshape(tokens, 4, 4, share)
    attn_cols = attn_cols.transpose(2, 0, 1, 3).reshape(4, 1, tokens, 4 * share)
    attn_y = cols_y(attn_cols, y)
    dz_y, dz_c = flip(dz, Y_BIT), flip(dz, CORE_BIT)
    du, gain_one_grad = backward_in(dproj, dh1, state, weights)
    gain_grad = jnp.concatenate([gain_one_grad, gain_two_grad])
    gain_grad, attn_y, dz_y, dz_c, both_own, gate_received = tie(
        (gain_grad, attn_y, dz_y, dz_c, both_own, gate_received)
    )
    gate, gate_send = pair_middle(both_own[:, :share], gate_received, z2)
    gate_received = flip(gate_send, Z2_BIT)
    gain_grad = gain_grad + flip(gain_grad, CORE_BIT)
    gain_grad = gain_grad + flip(gain_grad, Y_BIT)
    dz_all = (dz, dz_y, dz_c, flip(dz_y, CORE_BIT))
    attn_c = cols_core(attn_cols, attn_y, y, core)
    gain_rows = at(gain_grad.reshape(4, 4, -1).transpose(1, 0, 2), y * 2 + core)[:, None]
    gain_share = gain_rows.shape[-1]
    gain_rows = jnp.pad(gain_rows, ((0, 0), (0, EXTRA_ROWS - 1), (0, width - gain_share)))
    qkv_owners = QKV_COLS // share
    is_qkv = (qkv_owners // 4 * 4 + y * 2 + core < qkv_owners).astype(jnp.int32)
    attn_own, attn_send = plane_product(
        attn_cols,
        attn_y,
        attn_c,
        [n_all, dz_all],
        (*here, is_qkv, *pairs),
        (qkv_owners // 4, -(-qkv_owners // 4)),
        gain_rows,
    )
    attn_own, attn_send, both_own, up_received, gate_received = tie(
        (attn_own, attn_send, both_own, up_received, gate_received)
    )
    up, up_send = pair_middle(both_own[:, share:], up_received, z2)
    up_received = flip(up_send, Z2_BIT)
    attn_received = flip(attn_send, Z1_BIT)
    attn_own, attn_received, up_received = tie((attn_own, attn_received, up_received))
    attn, attn_send = pair_middle(attn_own, attn_received, z2)
    attn_received = flip(attn_send, Z2_BIT)
    down = down + down_received.astype(f32)
    gate = gate + gate_received.astype(f32)
    up = up + up_received.astype(f32)
    attn = attn + attn_received.astype(f32)
    return (
        du,
        attn[:share],
        jnp.stack([gate, up, down]),
        attn[share : share + 1, :gain_share],
    )


def local(edge_data, segment_ids, attn_weight, ffn_weight, gains):
    micro = segment_ids.shape[0]
    leading = lax.axis_index("section") == 0
    tables = block_tables(segment_ids)
    block, width = edge_data.shape[2], edge_data.shape[3]
    x = edge_data[0].reshape(micro * block, width)
    planes = lax.axis_size("dp") == 16
    me = lax.axis_index("dp")
    attn_own = attn_weight[0].T
    ffn_own = ffn_weight[0].swapaxes(1, 2)
    share = attn_own.shape[0]
    if planes:
        own = jnp.concatenate([attn_own[None], ffn_own], axis=0).reshape(-1, width)
        everything = lax.all_gather(own, "dp", axis=0, tiled=True).reshape(4, 4, 4, share, width)
        attn_t = everything[:, :, 0].reshape(-1, width)
        ffn_t = everything
    else:
        attn_t = lax.all_gather(attn_own, "dp", axis=0, tiled=True)
        ffn_t = lax.all_gather(ffn_own, "dp", axis=1, tiled=True)
    gain_row = gather_small(gains[0]).astype(f32)
    weights = (
        attn_t[:QKV_COLS],
        attn_t[QKV_COLS:],
        ffn_t,
        gain_row[:width],
        gain_row[width:],
    )
    first, _ = forward(x, weights, tables)
    received = lax.ppermute(first.astype(bf16), "section", [(0, 1)])
    u = jnp.where(leading, x, received)
    if planes:
        out, state, first_grad, early = middle_rounds(u, x, weights, tables, me)
        received = lax.ppermute(first_grad, "section", [(1, 0)])
        e = jnp.where(leading, received, x)
        du, attn_rows, ffn_rows, gain_shard = last_round(e, state, early, weights, tables, me)
    else:
        out, state = forward(u, weights, tables)
        first_grad, _, _ = backward(x, state, weights, tables)
        received = lax.ppermute(first_grad.astype(bf16), "section", [(1, 0)])
        e = jnp.where(leading, received, x)
        du, pieces, gain_grad = backward(e, state, weights, tables)
        attn_rows, ffn_rows = grads_generic(pieces)
        gain_shard = scatter_small(gain_grad)[None]
    edge_out = jnp.where(leading, du, out).astype(bf16).reshape(micro, block, width)
    return (
        edge_out[None],
        attn_rows.T[None],
        ffn_rows.swapaxes(1, 2)[None],
        gain_shard,
    )


def solution(mesh):
    in_specs = (
        P("section", None, "dp", None),
        P(None, "dp"),
        P("section", None, "dp"),
        P("section", None, None, "dp"),
        P("section", "dp"),
    )
    out_specs = (
        P("section", None, "dp", None),
        P("section", None, "dp"),
        P("section", None, None, "dp"),
        P("section", "dp"),
    )
    return jax.shard_map(local, mesh=mesh, in_specs=in_specs, out_specs=out_specs, check_vma=False)
```

```python
import jax
import jax.numpy as jnp
from jax import lax
from jax.experimental import pallas as pl
from jax.experimental.pallas import tpu as pltpu
from jax.sharding import PartitionSpec as P

QUERY_HEADS = 15
KEY_VALUE_HEADS = 5
HEAD_SIZE = 64
GROUP = QUERY_HEADS // KEY_VALUE_HEADS
Q_COLS = QUERY_HEADS * HEAD_SIZE
KV_COLS = KEY_VALUE_HEADS * HEAD_SIZE
QKV_COLS = Q_COLS + 2 * KV_COLS

epsilon = 1e-05
theta_base = 100000.0
Z2_BIT, Z1_BIT, Y_BIT, CORE_BIT = 8, 4, 2, 1
EXTRA_ROWS = 8
bf16 = jnp.bfloat16
f32 = jnp.float32


def dot_nn(a, b):
    return lax.dot_general(a, b, (((1,), (0,)), ((), ())), preferred_element_type=f32)


def dot_nt(a, b):
    return lax.dot_general(a, b, (((1,), (1,)), ((), ())), preferred_element_type=f32)


def rope(rows, cosine, sine):
    half = rows.shape[-1] // 2
    a, b = rows[..., :half], rows[..., half:]
    return jnp.concatenate([a * cosine - b * sine, b * cosine + a * sine], axis=-1)


def block_tables(segments):
    micro, block_len = segments.shape
    offsets = jnp.arange(block_len, dtype=jnp.int32)
    same = segments[:, :, None] == segments[:, None, :]
    start = jnp.min(jnp.where(same, offsets, block_len), axis=-1)
    positions = (offsets - start).astype(f32).reshape(-1)
    half = HEAD_SIZE // 2
    frequency = theta_base ** (-(2.0 * jnp.arange(half, dtype=f32)) / HEAD_SIZE)
    angles = positions[:, None] * frequency
    allowed = same & (offsets[:, None] >= offsets[None, :])
    eye = jnp.eye(micro, dtype=bool)
    full = allowed[:, :, None, :] & eye[:, None, :, None]
    total = micro * block_len
    return jnp.cos(angles), jnp.sin(angles), full.reshape(total, total)


def scores_of(q, k, allowed):
    s = jnp.einsum("tgrd,ugd->grtu", q, k, preferred_element_type=f32) * HEAD_SIZE**-0.5
    return jnp.where(allowed, s, -1000000000.0)


def forward_attention(u, weights, tables):
    qkv_w, out_w, ffn_w, gain_one, gain_two = weights
    cosine, sine, allowed = tables
    tokens = u.shape[0]
    u = u.astype(f32)
    r1 = lax.rsqrt(jnp.mean(u * u, axis=-1, keepdims=True) + epsilon)
    n = (u * r1 * gain_one).astype(bf16)
    proj = dot_nt(n, qkv_w)
    q = rope(
        proj[:, :Q_COLS].reshape(tokens, KEY_VALUE_HEADS, GROUP, HEAD_SIZE),
        cosine[:, None, None, :],
        sine[:, None, None, :],
    ).astype(bf16)
    k = rope(
        proj[:, Q_COLS : Q_COLS + KV_COLS].reshape(tokens, KEY_VALUE_HEADS, HEAD_SIZE),
        cosine[:, None, :],
        sine[:, None, :],
    ).astype(bf16)
    v = proj[:, Q_COLS + KV_COLS :].reshape(tokens, KEY_VALUE_HEADS, HEAD_SIZE).astype(bf16)
    masked = scores_of(q, k, allowed)
    peak = jnp.max(masked, axis=-1, keepdims=True)
    lse = peak + jnp.log(jnp.sum(jnp.exp(masked - peak), axis=-1, keepdims=True))
    prob = jnp.exp(masked - lse).astype(bf16)
    o = jnp.einsum("grtu,ugd->tgrd", prob, v, preferred_element_type=f32)
    o = o.reshape(tokens, Q_COLS).astype(bf16)
    h1 = u + dot_nn(o, out_w)
    r2 = lax.rsqrt(jnp.mean(h1 * h1, axis=-1, keepdims=True) + epsilon)
    m = (h1 * r2 * gain_two).astype(bf16)
    return u, r1, n, q, k, v, lse, o, h1, r2, m


def forward(u, weights, tables):
    state = forward_attention(u, weights, tables)
    gate, up, act, out = ffn_forward(state[10], state[8], weights[2])
    return out, (*state, gate, up, act)


def norm_back(grad, rows, r, gain):
    scaled = grad * gain
    part = r * scaled - rows * (r * r * r) * jnp.mean(scaled * rows, axis=-1, keepdims=True)
    return part, jnp.sum(grad * rows * r, axis=0)


def backward_ffn(eb, state, weights):
    gate, up = state[11], state[12]
    return ffn_backward(eb, gate, up, weights[2])


def backward_mid(e, dm, state, weights):
    out_w, gain_two = weights[1], weights[4]
    h1, r2 = state[8], state[9]
    part, gain_two_grad = norm_back(dm, h1, r2, gain_two)
    dh1 = e.astype(f32) + part
    dz = dh1.astype(bf16)
    return dh1, dz, dot_nt(dz, out_w).astype(bf16), gain_two_grad


def backward_attention(do, state, tables):
    cosine, sine, allowed = tables
    q, k, v, lse = state[3:7]
    tokens = do.shape[0]
    do = do.reshape(tokens, KEY_VALUE_HEADS, GROUP, HEAD_SIZE)
    prob = jnp.exp(scores_of(q, k, allowed) - lse)
    dv = jnp.einsum("grtu,tgrd->ugd", prob.astype(bf16), do, preferred_element_type=f32)
    dp = jnp.einsum("tgrd,ugd->grtu", do, v, preferred_element_type=f32)
    ds = (prob * (dp - jnp.sum(dp * prob, axis=-1, keepdims=True))).astype(bf16)
    dq = jnp.einsum("grtu,ugd->tgrd", ds, k, preferred_element_type=f32) * HEAD_SIZE**-0.5
    dk = jnp.einsum("grtu,tgrd->ugd", ds, q, preferred_element_type=f32) * HEAD_SIZE**-0.5
    dq = rope(dq, cosine[:, None, None, :], -sine[:, None, None, :])
    dk = rope(dk, cosine[:, None, :], -sine[:, None, :])
    return jnp.concatenate(
        [dq.reshape(tokens, Q_COLS), dk.reshape(tokens, KV_COLS), dv.reshape(tokens, KV_COLS)],
        axis=1,
    ).astype(bf16)


def backward_in(dproj, dh1, state, weights):
    qkv_w, gain_one = weights[0], weights[3]
    u, r1 = state[0], state[1]
    part, gain_one_grad = norm_back(dot_nn(dproj, qkv_w), u, r1, gain_one)
    return dh1 + part, gain_one_grad


def backward(e, state, weights, tables):
    dgate, dup, dm = backward_ffn(e.astype(bf16), state, weights)
    dh1, dz, do, gain_two_grad = backward_mid(e, dm, state, weights)
    dproj = backward_attention(do, state, tables)
    du, gain_one_grad = backward_in(dproj, dh1, state, weights)
    pieces = (state[2], dproj, state[7], dz, state[10], dgate, dup, e.astype(bf16), state[13])
    return du, pieces, jnp.concatenate([gain_one_grad, gain_two_grad])


def ffn_forward_kernel(m_ref, h1_ref, wg_ref, wu_ref, wd_ref, gate_ref, up_ref, act_ref, out_ref):
    flat = lambda ref: ref[...].reshape(-1, ref.shape[-1])
    m = m_ref[...]
    gate = dot_nt(m, flat(wg_ref))
    up = dot_nt(m, flat(wu_ref))
    act = (gate * jax.nn.sigmoid(gate) * up).astype(bf16)
    gate_ref[...] = gate
    up_ref[...] = up
    act_ref[...] = act
    add = dot_nn(act, flat(wd_ref))

    @pl.when(pl.program_id(0) == 0)
    def _():
        out_ref[...] = h1_ref[...] + add

    @pl.when(pl.program_id(0) > 0)
    def _():
        out_ref[...] += add


def ffn_backward_kernel(
    eb_ref, gate_ref, up_ref, wg_ref, wu_ref, wd_ref, both_ref, dm_ref
):
    flat = lambda ref: ref[...].reshape(-1, ref.shape[-1])
    da = dot_nt(eb_ref[...], flat(wd_ref))
    gate = gate_ref[...]
    sig = jax.nn.sigmoid(gate)
    dgate = (da * up_ref[...] * sig * (1.0 + gate * (1.0 - sig))).astype(bf16)
    dup = (da * gate * sig).astype(bf16)
    both_ref[0] = dgate
    both_ref[1] = dup
    add = dot_nn(dgate, flat(wg_ref)) + dot_nn(dup, flat(wu_ref))

    @pl.when(pl.program_id(0) == 0)
    def _():
        dm_ref[...] = add

    @pl.when(pl.program_id(0) > 0)
    def _():
        dm_ref[...] += add


def weight_spec(w, matrix):
    lines, _, _, share, width = w.shape
    return pl.BlockSpec((lines, None, None, share, width), lambda i: (0, i, matrix, 0, 0))


def ffn_call(kernel, w, wholes, blocks, out_blocks):
    lines, steps, _, share, width = w.shape
    tokens, cols = wholes[0].shape[0], lines * share
    whole = pl.BlockSpec((tokens, width), lambda i: (0, 0))
    block = pl.BlockSpec((None, tokens, cols), lambda i: (i, 0, 0))
    out_specs = [
        pl.BlockSpec((None, *shape), lambda i, n=len(shape): (i,) + (0,) * n) for shape, _ in out_blocks
    ]
    return pl.pallas_call(
        kernel,
        grid=(steps,),
        in_specs=[whole] * len(wholes)
        + [block] * len(blocks)
        + [weight_spec(w, matrix) for matrix in (1, 2, 3)],
        out_specs=out_specs + [whole],
        out_shape=[jax.ShapeDtypeStruct((steps, *shape), t) for shape, t in out_blocks]
        + [jax.ShapeDtypeStruct((tokens, width), f32)],
        compiler_params=pltpu.CompilerParams(
            dimension_semantics=("arbitrary",), vmem_limit_bytes=40 * 1024 * 1024
        ),
        cost_estimate=pl.CostEstimate(
            flops=6 * tokens * steps * cols * width,
            bytes_accessed=6 * steps * cols * width,
            transcendentals=tokens * steps * cols,
        ),
    )(*wholes, *blocks, w, w, w)


def ffn_forward(m, h1, w):
    if w.ndim == 5:
        shape = (m.shape[0], w.shape[0] * w.shape[3])
        return ffn_call(ffn_forward_kernel, w, (m, h1), (), [(shape, t) for t in (f32, f32, bf16)])
    gate, up = dot_nt(m, w[0]), dot_nt(m, w[1])
    act = (jax.nn.silu(gate) * up).astype(bf16)
    return gate, up, act, h1 + dot_nn(act, w[2])


def ffn_backward(eb, gate, up, w):
    if w.ndim == 5:
        shape = (2, eb.shape[0], w.shape[0] * w.shape[3])
        both, dm = ffn_call(ffn_backward_kernel, w, (eb,), (gate, up), [(shape, bf16)])
        return both, both, dm
    da = dot_nt(eb, w[2])
    sig = jax.nn.sigmoid(gate)
    dgate = (da * up * sig * (1.0 + gate * (1.0 - sig))).astype(bf16)
    dup = (da * gate * sig).astype(bf16)
    return dgate, dup, dot_nn(dgate, w[0]) + dot_nn(dup, w[1])


def flip(x, bit):
    size = lax.axis_size("dp")
    return lax.ppermute(x, "dp", [(i, i ^ bit) for i in range(size)])


def gather_small(row):
    size = lax.axis_size("dp")
    me = lax.axis_index("dp")
    bit = 1
    while bit < size:
        other = flip(row, bit)
        high = (me & bit) != 0
        row = jnp.concatenate([jnp.where(high, other, row), jnp.where(high, row, other)])
        bit *= 2
    return row


def scatter_small(row):
    size = lax.axis_size("dp")
    me = lax.axis_index("dp")
    bit = size // 2
    while bit >= 1:
        half = row.shape[0] // 2
        low, top = row[:half], row[half:]
        high = (me & bit) != 0
        row = jnp.where(high, top, low) + flip(jnp.where(high, low, top), bit)
        bit //= 2
    return row


def grads_generic(pieces):
    n, dproj, o, dz, m, dgate, dup, eb, act = pieces
    attn = jnp.concatenate([dot_nn(dproj.T, n), dot_nn(o.T, dz)], axis=0)
    both = [
        lax.psum_scatter(g, "dp", scatter_dimension=0, tiled=True)
        for g in (attn, dot_nn(dgate.T, m), dot_nn(dup.T, m), dot_nn(act.T, eb))
    ]
    return both[0], jnp.stack(both[1:])


def z_pairs(x, pairs):
    return lax.ppermute(x, "dp", [(4 * a + i, 4 * b + i) for a, b in pairs for i in range(4)])


def inner_swap(x):
    return z_pairs(x, [(1, 2), (2, 1)])


def at(x, i):
    return lax.dynamic_index_in_dim(x, i, 0, keepdims=False)


def rows_of_plane(x):
    x_y = flip(x, Y_BIT)
    return x, x_y, flip(x, CORE_BIT), flip(x_y, CORE_BIT)


def cols_y(x, y):
    x = x.reshape(2, 2, *x.shape[1:])
    return flip(at(x, 1 - y), Y_BIT)


def cols_core(x, x_y, y, core):
    other = 1 - core
    return flip(jnp.stack([at(x, 2 * y + other), at(x_y, other)]), CORE_BIT)


def plane_kernel(n_rows, split, out_kinds, picks_ref, *refs):
    cols_ref, y_ref, core_ref = refs[:3]
    rows = [
        jnp.concatenate([r[...] for r in refs[3 + 4 * i : 7 + 4 * i]], axis=0) for i in range(n_rows)
    ]
    rest = refs[3 + 4 * n_rows :]
    extra_ref = rest[0] if n_rows == 2 else None
    outs, total = rest[n_rows - 1 : -1], rest[-1]
    kinds = cols_ref.shape[1]
    height = total.shape[0] // kinds
    share = height // LINE

    def cols_of(j):
        return jnp.concatenate(
            [cols_ref[picks_ref[0], j], y_ref[picks_ref[1], j], core_ref[0, j], core_ref[1, j]], axis=0
        )

    def dot(c, r):
        return lax.dot_general(c, r, (((0,), (0,)), ((), ())), preferred_element_type=f32)

    if n_rows == 1:
        for j in range(kinds):
            total[j * height : (j + 1) * height] = dot(cols_of(j), rows[0])
    else:
        low, top = split
        cols = cols_of(0)
        total[...] = dot(cols, rows[1])
        first = dot(cols, rows[0])
        total[: low * share] = first[: low * share]
        if top > low:

            @pl.when(picks_ref[2] > 0)
            def _():
                total[low * share : top * share] = first[low * share : top * share]

    slot = 3
    for number, ref in enumerate(outs):
        for i in range(ref.shape[0]):
            pick = picks_ref[slot]
            slot += 1
            first = out_kinds[number][0]
            for j in out_kinds[number]:
                block = total[pl.ds(pl.multiple_of(j * height + pick * share, 8), share)]
                ref[i, (j - first) * share : (j - first + 1) * share] = block.astype(ref.dtype)
            if extra_ref is not None:
                ref[i, share:] = extra_ref[pick].astype(ref.dtype)


def plane_product(cols, x_y, x_core, rows, picks, split=None, extra=None):
    _, kinds, tokens, width_cols = cols.shape
    share, width = width_cols // LINE, rows[0][0].shape[1]
    out_kinds = [tuple(range(kinds)), *((j,) for j in range(kinds))]
    more = 0 if extra is None else extra.shape[1]
    operands = [cols, x_y, x_core, *[r for chunk in rows for r in chunk]]
    if extra is not None:
        operands.append(extra)
    whole = lambda v: pl.BlockSpec(v.shape, lambda i, picks, n=v.ndim: (0,) * n)
    shapes = [
        jax.ShapeDtypeStruct((2, len(k) * share + more, width), f32 if i == 0 else bf16)
        for i, k in enumerate(out_kinds)
    ]
    kernel = lambda *refs: plane_kernel(len(rows), split, out_kinds, *refs)
    return pl.pallas_call(
        kernel,
        grid_spec=pltpu.PrefetchScalarGridSpec(
            num_scalar_prefetch=1,
            grid=(1,),
            in_specs=[whole(v) for v in operands],
            out_specs=[whole(v) for v in shapes],
            scratch_shapes=[pltpu.VMEM((kinds * LINE * share, width), f32)],
        ),
        out_shape=shapes,
        compiler_params=pltpu.CompilerParams(
            dimension_semantics=("arbitrary",), vmem_limit_bytes=32 * 1024 * 1024
        ),
        cost_estimate=pl.CostEstimate(
            flops=8 * tokens * kinds * width_cols * width * len(rows),
            bytes_accessed=8 * tokens * (kinds * width_cols + width) + 4 * kinds * width_cols * width,
            transcendentals=0,
        ),
    )(jnp.stack([jnp.asarray(p, jnp.int32) for p in picks]), *operands)


LINE = 4


def pair_middle(own, received, z2):
    total = own + received.astype(f32)
    return at(total, z2), at(total, 1 - z2).astype(bf16)


tie = lax.optimization_barrier


def middle_rounds(u, x, weights, tables, me):
    y, core = (me >> 1) & 1, me & 1
    state = forward_attention(u, weights, tables)
    n, m = state[2], state[10]
    gate, up, act, out = ffn_forward(m, state[8], weights[2])
    m_y, n_y = flip(m, Y_BIT), flip(n, Y_BIT)
    gate, up, act, out, m_y, n_y = tie((gate, up, act, out, m_y, n_y))
    state = (*state, gate, up, act)
    act = act[:, None]
    act_y = cols_y(act, y)
    m_all = (m, m_y, flip(m, CORE_BIT), flip(m_y, CORE_BIT))
    n_all = (n, n_y, flip(n, CORE_BIT), flip(n_y, CORE_BIT))
    _, _, dm = backward_ffn(x, state, weights)
    dm, act_y, m_all, n_all = tie((dm, act_y, m_all, n_all))
    act_c = (act, act_y, cols_core(act, act_y, y, core))
    dh1, _, do, _ = backward_mid(x, dm, state, weights)
    dproj = backward_attention(do, state, tables)
    first_grad, _ = backward_in(dproj, dh1, state, weights)
    first_grad, act_c = tie((first_grad.astype(bf16), act_c))
    return out, state, first_grad, (m_all, n_all, act_c)


def last_round(e, state, early, weights, tables, me):
    o = state[7]
    z, y, core = me // 4, (me >> 1) & 1, me & 1
    z2, z1 = z >> 1, z & 1
    m_all, n_all, act_c = early
    tokens, width = o.shape[0], e.shape[1]
    share = act_c[0].shape[3] // LINE
    here = (2 * y + core, core)
    eb = e.astype(bf16)
    eb_y, eb_c = flip(eb, Y_BIT), flip(eb, CORE_BIT)
    both, _, dm = backward_ffn(eb, state, weights)
    both, dm, eb_y, eb_c = tie((both, dm, eb_y, eb_c))
    both_y = cols_y(both, y)
    eb_yc = flip(eb_y, CORE_BIT)
    dm, eb_yc = tie((dm, eb_yc))
    pairs = (z1, 2 + z1, 1 - z1, 3 - z1)
    down_own, down_send = plane_product(*act_c, [(eb, eb_y, eb_c, eb_yc)], (*here, 0, *pairs))
    dm, down_own, down_send = tie((dm, down_own, down_send))
    down_received = flip(down_send, Z1_BIT)
    dh1, dz, do, gain_two_grad = backward_mid(e, dm, state, weights)
    do, dz, both_y, down_own, down_received = tie((do, dz, both_y, down_own, down_received))
    both_c = cols_core(both, both_y, y, core)
    down, down_send = pair_middle(down_own, down_received, z2)
    down_received = flip(down_send, Z2_BIT)
    both_own, gate_send, up_send = plane_product(
        both, both_y, both_c, [m_all], (*here, 0, *pairs, *pairs[2:])
    )
    do, dz, both_own, gate_send, up_send = tie((do, dz, both_own, gate_send, up_send))
    gate_received, up_received = flip(gate_send, Z1_BIT), flip(up_send, Z1_BIT)
    dproj = backward_attention(do, state, tables)
    dproj, down_received = tie((dproj, down_received))
    attn_cols = jnp.concatenate([dproj, o], axis=1).reshape(tokens, 4, 4, share)
    attn_cols = attn_cols.transpose(2, 0, 1, 3).reshape(4, 1, tokens, 4 * share)
    attn_y = cols_y(attn_cols, y)
    dz_y, dz_c = flip(dz, Y_BIT), flip(dz, CORE_BIT)
    du, gain_one_grad = backward_in(dproj, dh1, state, weights)
    gain_grad = jnp.concatenate([gain_one_grad, gain_two_grad])
    gain_grad, attn_y, dz_y, dz_c, both_own, gate_received = tie(
        (gain_grad, attn_y, dz_y, dz_c, both_own, gate_received)
    )
    gate, gate_send = pair_middle(both_own[:, :share], gate_received, z2)
    gate_received = flip(gate_send, Z2_BIT)
    gain_grad = gain_grad + flip(gain_grad, CORE_BIT)
    gain_grad = gain_grad + flip(gain_grad, Y_BIT)
    dz_all = (dz, dz_y, dz_c, flip(dz_y, CORE_BIT))
    attn_c = cols_core(attn_cols, attn_y, y, core)
    gain_rows = at(gain_grad.reshape(4, 4, -1).transpose(1, 0, 2), y * 2 + core)[:, None]
    gain_share = gain_rows.shape[-1]
    gain_rows = jnp.pad(gain_rows, ((0, 0), (0, EXTRA_ROWS - 1), (0, width - gain_share)))
    qkv_owners = QKV_COLS // share
    is_qkv = (qkv_owners // 4 * 4 + y * 2 + core < qkv_owners).astype(jnp.int32)
    attn_own, attn_send = plane_product(
        attn_cols,
        attn_y,
        attn_c,
        [n_all, dz_all],
        (*here, is_qkv, *pairs),
        (qkv_owners // 4, -(-qkv_owners // 4)),
        gain_rows,
    )
    attn_own, attn_send, both_own, up_received, gate_received = tie(
        (attn_own, attn_send, both_own, up_received, gate_received)
    )
    up, up_send = pair_middle(both_own[:, share:], up_received, z2)
    up_received = flip(up_send, Z2_BIT)
    attn_received = flip(attn_send, Z1_BIT)
    attn_own, attn_received, up_received = tie((attn_own, attn_received, up_received))
    attn, attn_send = pair_middle(attn_own, attn_received, z2)
    attn_received = flip(attn_send, Z2_BIT)
    down = down + down_received.astype(f32)
    gate = gate + gate_received.astype(f32)
    up = up + up_received.astype(f32)
    attn = attn + attn_received.astype(f32)
    return (
        du,
        attn[:share],
        jnp.stack([gate, up, down]),
        attn[share : share + 1, :gain_share],
    )


def local(edge_data, segment_ids, attn_weight, ffn_weight, gains):
    micro = segment_ids.shape[0]
    leading = lax.axis_index("section") == 0
    tables = block_tables(segment_ids)
    block, width = edge_data.shape[2], edge_data.shape[3]
    x = edge_data[0].reshape(micro * block, width)
    planes = lax.axis_size("dp") == 16
    me = lax.axis_index("dp")
    attn_own = attn_weight[0].T
    ffn_own = ffn_weight[0].swapaxes(1, 2)
    share = attn_own.shape[0]
    if planes:
        own = jnp.concatenate([attn_own[None], ffn_own], axis=0).reshape(-1, width)
        everything = lax.all_gather(own, "dp", axis=0, tiled=True).reshape(4, 4, 4, share, width)
        attn_t = everything[:, :, 0].reshape(-1, width)
        ffn_t = everything
    else:
        attn_t = lax.all_gather(attn_own, "dp", axis=0, tiled=True)
        ffn_t = lax.all_gather(ffn_own, "dp", axis=1, tiled=True)
    gain_row = gather_small(gains[0]).astype(f32)
    weights = (
        attn_t[:QKV_COLS],
        attn_t[QKV_COLS:],
        ffn_t,
        gain_row[:width],
        gain_row[width:],
    )
    first, _ = forward(x, weights, tables)
    received = lax.ppermute(first.astype(bf16), "section", [(0, 1)])
    u = jnp.where(leading, x, received)
    if planes:
        out, state, first_grad, early = middle_rounds(u, x, weights, tables, me)
        received = lax.ppermute(first_grad, "section", [(1, 0)])
        e = jnp.where(leading, received, x)
        du, attn_rows, ffn_rows, gain_shard = last_round(e, state, early, weights, tables, me)
    else:
        out, state = forward(u, weights, tables)
        first_grad, _, _ = backward(x, state, weights, tables)
        received = lax.ppermute(first_grad.astype(bf16), "section", [(1, 0)])
        e = jnp.where(leading, received, x)
        du, pieces, gain_grad = backward(e, state, weights, tables)
        attn_rows, ffn_rows = grads_generic(pieces)
        gain_shard = scatter_small(gain_grad)[None]
    edge_out = jnp.where(leading, du, out).astype(bf16).reshape(micro, block, width)
    return (
        edge_out[None],
        attn_rows.T[None],
        ffn_rows.swapaxes(1, 2)[None],
        gain_shard,
    )


def solution(mesh):
    in_specs = (
        P("section", None, "dp", None),
        P(None, "dp"),
        P("section", None, "dp"),
        P("section", None, None, "dp"),
        P("section", "dp"),
    )
    out_specs = (
        P("section", None, "dp", None),
        P("section", None, "dp"),
        P("section", None, None, "dp"),
        P("section", "dp"),
    )
    return jax.shard_map(local, mesh=mesh, in_specs=in_specs, out_specs=out_specs, check_vma=False)
```

```python
import jax
import jax.numpy as jnp
from jax import lax
from jax.experimental import pallas as pl
from jax.experimental.pallas import tpu as pltpu
from jax.sharding import PartitionSpec as P

QUERY_HEADS = 15
KEY_VALUE_HEADS = 5
HEAD_SIZE = 64
GROUP = QUERY_HEADS // KEY_VALUE_HEADS
Q_COLS = QUERY_HEADS * HEAD_SIZE
KV_COLS = KEY_VALUE_HEADS * HEAD_SIZE
QKV_COLS = Q_COLS + 2 * KV_COLS

epsilon = 1e-05
theta_base = 100000.0
Z2_BIT, Z1_BIT, Y_BIT, CORE_BIT = 8, 4, 2, 1
EXTRA_ROWS = 8
bf16 = jnp.bfloat16
f32 = jnp.float32


def dot_nn(a, b):
    return lax.dot_general(a, b, (((1,), (0,)), ((), ())), preferred_element_type=f32)


def dot_nt(a, b):
    return lax.dot_general(a, b, (((1,), (1,)), ((), ())), preferred_element_type=f32)


def rope(rows, cosine, sine):
    half = rows.shape[-1] // 2
    a, b = rows[..., :half], rows[..., half:]
    return jnp.concatenate([a * cosine - b * sine, b * cosine + a * sine], axis=-1)


def block_tables(segments):
    micro, block_len = segments.shape
    offsets = jnp.arange(block_len, dtype=jnp.int32)
    same = segments[:, :, None] == segments[:, None, :]
    start = jnp.min(jnp.where(same, offsets, block_len), axis=-1)
    positions = (offsets - start).astype(f32).reshape(-1)
    half = HEAD_SIZE // 2
    frequency = theta_base ** (-(2.0 * jnp.arange(half, dtype=f32)) / HEAD_SIZE)
    angles = positions[:, None] * frequency
    allowed = same & (offsets[:, None] >= offsets[None, :])
    eye = jnp.eye(micro, dtype=bool)
    full = allowed[:, :, None, :] & eye[:, None, :, None]
    total = micro * block_len
    return jnp.cos(angles), jnp.sin(angles), full.reshape(total, total)


def scores_of(q, k, allowed):
    s = jnp.einsum("tgrd,ugd->grtu", q, k, preferred_element_type=f32) * HEAD_SIZE**-0.5
    return jnp.where(allowed, s, -1000000000.0)


def forward_attention(u, weights, tables):
    qkv_w, out_w, ffn_w, gain_one, gain_two = weights
    cosine, sine, allowed = tables
    tokens = u.shape[0]
    u = u.astype(f32)
    r1 = lax.rsqrt(jnp.mean(u * u, axis=-1, keepdims=True) + epsilon)
    n = (u * r1 * gain_one).astype(bf16)
    proj = dot_nt(n, qkv_w)
    q = rope(
        proj[:, :Q_COLS].reshape(tokens, KEY_VALUE_HEADS, GROUP, HEAD_SIZE),
        cosine[:, None, None, :],
        sine[:, None, None, :],
    ).astype(bf16)
    k = rope(
        proj[:, Q_COLS : Q_COLS + KV_COLS].reshape(tokens, KEY_VALUE_HEADS, HEAD_SIZE),
        cosine[:, None, :],
        sine[:, None, :],
    ).astype(bf16)
    v = proj[:, Q_COLS + KV_COLS :].reshape(tokens, KEY_VALUE_HEADS, HEAD_SIZE).astype(bf16)
    masked = scores_of(q, k, allowed)
    peak = jnp.max(masked, axis=-1, keepdims=True)
    lse = peak + jnp.log(jnp.sum(jnp.exp(masked - peak), axis=-1, keepdims=True))
    prob = jnp.exp(masked - lse).astype(bf16)
    o = jnp.einsum("grtu,ugd->tgrd", prob, v, preferred_element_type=f32)
    o = o.reshape(tokens, Q_COLS).astype(bf16)
    h1 = u + dot_nn(o, out_w)
    r2 = lax.rsqrt(jnp.mean(h1 * h1, axis=-1, keepdims=True) + epsilon)
    m = (h1 * r2 * gain_two).astype(bf16)
    return u, r1, n, q, k, v, lse, o, h1, r2, m


def forward(u, weights, tables):
    state = forward_attention(u, weights, tables)
    gate, up, act, out = ffn_forward(state[10], state[8], weights[2])
    return out, (*state, gate, up, act)


def norm_back(grad, rows, r, gain):
    scaled = grad * gain
    part = r * scaled - rows * (r * r * r) * jnp.mean(scaled * rows, axis=-1, keepdims=True)
    return part, jnp.sum(grad * rows * r, axis=0)


def backward_ffn(eb, state, weights):
    gate, up = state[11], state[12]
    return ffn_backward(eb, gate, up, weights[2])


def backward_mid(e, dm, state, weights):
    out_w, gain_two = weights[1], weights[4]
    h1, r2 = state[8], state[9]
    part, gain_two_grad = norm_back(dm, h1, r2, gain_two)
    dh1 = e.astype(f32) + part
    dz = dh1.astype(bf16)
    return dh1, dz, dot_nt(dz, out_w).astype(bf16), gain_two_grad


def backward_attention(do, state, tables):
    cosine, sine, allowed = tables
    q, k, v, lse = state[3:7]
    tokens = do.shape[0]
    do = do.reshape(tokens, KEY_VALUE_HEADS, GROUP, HEAD_SIZE)
    prob = jnp.exp(scores_of(q, k, allowed) - lse)
    dv = jnp.einsum("grtu,tgrd->ugd", prob.astype(bf16), do, preferred_element_type=f32)
    dp = jnp.einsum("tgrd,ugd->grtu", do, v, preferred_element_type=f32)
    ds = (prob * (dp - jnp.sum(dp * prob, axis=-1, keepdims=True))).astype(bf16)
    dq = jnp.einsum("grtu,ugd->tgrd", ds, k, preferred_element_type=f32) * HEAD_SIZE**-0.5
    dk = jnp.einsum("grtu,tgrd->ugd", ds, q, preferred_element_type=f32) * HEAD_SIZE**-0.5
    dq = rope(dq, cosine[:, None, None, :], -sine[:, None, None, :])
    dk = rope(dk, cosine[:, None, :], -sine[:, None, :])
    return jnp.concatenate(
        [dq.reshape(tokens, Q_COLS), dk.reshape(tokens, KV_COLS), dv.reshape(tokens, KV_COLS)],
        axis=1,
    ).astype(bf16)


def backward_in(dproj, dh1, state, weights):
    qkv_w, gain_one = weights[0], weights[3]
    u, r1 = state[0], state[1]
    part, gain_one_grad = norm_back(dot_nn(dproj, qkv_w), u, r1, gain_one)
    return dh1 + part, gain_one_grad


def backward(e, state, weights, tables):
    dgate, dup, dm = backward_ffn(e.astype(bf16), state, weights)
    dh1, dz, do, gain_two_grad = backward_mid(e, dm, state, weights)
    dproj = backward_attention(do, state, tables)
    du, gain_one_grad = backward_in(dproj, dh1, state, weights)
    pieces = (state[2], dproj, state[7], dz, state[10], dgate, dup, e.astype(bf16), state[13])
    return du, pieces, jnp.concatenate([gain_one_grad, gain_two_grad])


def ffn_forward_kernel(m_ref, h1_ref, wg_ref, wu_ref, wd_ref, gate_ref, up_ref, act_ref, out_ref):
    flat = lambda ref: ref[...].reshape(-1, ref.shape[-1])
    m = m_ref[...]
    gate = dot_nt(m, flat(wg_ref))
    up = dot_nt(m, flat(wu_ref))
    act = (gate * jax.nn.sigmoid(gate) * up).astype(bf16)
    gate_ref[...] = gate
    up_ref[...] = up
    act_ref[...] = act
    add = dot_nn(act, flat(wd_ref))

    @pl.when(pl.program_id(0) == 0)
    def _():
        out_ref[...] = h1_ref[...] + add

    @pl.when(pl.program_id(0) > 0)
    def _():
        out_ref[...] += add


def ffn_backward_kernel(
    eb_ref, gate_ref, up_ref, wg_ref, wu_ref, wd_ref, both_ref, dm_ref
):
    flat = lambda ref: ref[...].reshape(-1, ref.shape[-1])
    da = dot_nt(eb_ref[...], flat(wd_ref))
    gate = gate_ref[...]
    sig = jax.nn.sigmoid(gate)
    dgate = (da * up_ref[...] * sig * (1.0 + gate * (1.0 - sig))).astype(bf16)
    dup = (da * gate * sig).astype(bf16)
    both_ref[0] = dgate
    both_ref[1] = dup
    add = dot_nn(dgate, flat(wg_ref)) + dot_nn(dup, flat(wu_ref))

    @pl.when(pl.program_id(0) == 0)
    def _():
        dm_ref[...] = add

    @pl.when(pl.program_id(0) > 0)
    def _():
        dm_ref[...] += add


def weight_spec(w, matrix):
    lines, _, _, share, width = w.shape
    return pl.BlockSpec((lines, None, None, share, width), lambda i: (0, i, matrix, 0, 0))


def ffn_call(kernel, w, wholes, blocks, out_blocks):
    lines, steps, _, share, width = w.shape
    tokens, cols = wholes[0].shape[0], lines * share
    whole = pl.BlockSpec((tokens, width), lambda i: (0, 0))
    block = pl.BlockSpec((None, tokens, cols), lambda i: (i, 0, 0))
    out_specs = [
        pl.BlockSpec((None, *shape), lambda i, n=len(shape): (i,) + (0,) * n) for shape, _ in out_blocks
    ]
    return pl.pallas_call(
        kernel,
        grid=(steps,),
        in_specs=[whole] * len(wholes)
        + [block] * len(blocks)
        + [weight_spec(w, matrix) for matrix in (1, 2, 3)],
        out_specs=out_specs + [whole],
        out_shape=[jax.ShapeDtypeStruct((steps, *shape), t) for shape, t in out_blocks]
        + [jax.ShapeDtypeStruct((tokens, width), f32)],
        compiler_params=pltpu.CompilerParams(
            dimension_semantics=("arbitrary",), vmem_limit_bytes=24 * 1024 * 1024
        ),
        cost_estimate=pl.CostEstimate(
            flops=6 * tokens * steps * cols * width,
            bytes_accessed=6 * steps * cols * width,
            transcendentals=tokens * steps * cols,
        ),
    )(*wholes, *blocks, w, w, w)


def ffn_forward(m, h1, w):
    if w.ndim == 5:
        shape = (m.shape[0], w.shape[0] * w.shape[3])
        return ffn_call(ffn_forward_kernel, w, (m, h1), (), [(shape, t) for t in (f32, f32, bf16)])
    gate, up = dot_nt(m, w[0]), dot_nt(m, w[1])
    act = (jax.nn.silu(gate) * up).astype(bf16)
    return gate, up, act, h1 + dot_nn(act, w[2])


def ffn_backward(eb, gate, up, w):
    if w.ndim == 5:
        shape = (2, eb.shape[0], w.shape[0] * w.shape[3])
        both, dm = ffn_call(ffn_backward_kernel, w, (eb,), (gate, up), [(shape, bf16)])
        return both, both, dm
    da = dot_nt(eb, w[2])
    sig = jax.nn.sigmoid(gate)
    dgate = (da * up * sig * (1.0 + gate * (1.0 - sig))).astype(bf16)
    dup = (da * gate * sig).astype(bf16)
    return dgate, dup, dot_nn(dgate, w[0]) + dot_nn(dup, w[1])


def flip(x, bit):
    size = lax.axis_size("dp")
    return lax.ppermute(x, "dp", [(i, i ^ bit) for i in range(size)])


def gather_small(row):
    size = lax.axis_size("dp")
    me = lax.axis_index("dp")
    bit = 1
    while bit < size:
        other = flip(row, bit)
        high = (me & bit) != 0
        row = jnp.concatenate([jnp.where(high, other, row), jnp.where(high, row, other)])
        bit *= 2
    return row


def scatter_small(row):
    size = lax.axis_size("dp")
    me = lax.axis_index("dp")
    bit = size // 2
    while bit >= 1:
        half = row.shape[0] // 2
        low, top = row[:half], row[half:]
        high = (me & bit) != 0
        row = jnp.where(high, top, low) + flip(jnp.where(high, low, top), bit)
        bit //= 2
    return row


def grads_generic(pieces):
    n, dproj, o, dz, m, dgate, dup, eb, act = pieces
    attn = jnp.concatenate([dot_nn(dproj.T, n), dot_nn(o.T, dz)], axis=0)
    both = [
        lax.psum_scatter(g, "dp", scatter_dimension=0, tiled=True)
        for g in (attn, dot_nn(dgate.T, m), dot_nn(dup.T, m), dot_nn(act.T, eb))
    ]
    return both[0], jnp.stack(both[1:])


def z_pairs(x, pairs):
    return lax.ppermute(x, "dp", [(4 * a + i, 4 * b + i) for a, b in pairs for i in range(4)])


def inner_swap(x):
    return z_pairs(x, [(1, 2), (2, 1)])


def at(x, i):
    return lax.dynamic_index_in_dim(x, i, 0, keepdims=False)


def rows_of_plane(x):
    x_y = flip(x, Y_BIT)
    return x, x_y, flip(x, CORE_BIT), flip(x_y, CORE_BIT)


def cols_y(x, y):
    x = x.reshape(2, 2, *x.shape[1:])
    return flip(at(x, 1 - y), Y_BIT)


def cols_core(x, x_y, y, core):
    other = 1 - core
    return flip(jnp.stack([at(x, 2 * y + other), at(x_y, other)]), CORE_BIT)


def plane_kernel(n_rows, split, out_kinds, picks_ref, *refs):
    cols_ref, y_ref, core_ref = refs[:3]
    rows = [
        jnp.concatenate([r[...] for r in refs[3 + 4 * i : 7 + 4 * i]], axis=0) for i in range(n_rows)
    ]
    rest = refs[3 + 4 * n_rows :]
    extra_ref = rest[0] if n_rows == 2 else None
    outs, total = rest[n_rows - 1 : -1], rest[-1]
    kinds = cols_ref.shape[1]
    height = total.shape[0] // kinds
    share = height // LINE

    def cols_of(j):
        return jnp.concatenate(
            [cols_ref[picks_ref[0], j], y_ref[picks_ref[1], j], core_ref[0, j], core_ref[1, j]], axis=0
        )

    def dot(c, r):
        return lax.dot_general(c, r, (((0,), (0,)), ((), ())), preferred_element_type=f32)

    if n_rows == 1:
        for j in range(kinds):
            total[j * height : (j + 1) * height] = dot(cols_of(j), rows[0])
    else:
        low, top = split
        cols = cols_of(0)
        total[...] = dot(cols, rows[1])
        first = dot(cols, rows[0])
        total[: low * share] = first[: low * share]
        if top > low:

            @pl.when(picks_ref[2] > 0)
            def _():
                total[low * share : top * share] = first[low * share : top * share]

    slot = 3
    for number, ref in enumerate(outs):
        for i in range(ref.shape[0]):
            pick = picks_ref[slot]
            slot += 1
            first = out_kinds[number][0]
            for j in out_kinds[number]:
                block = total[pl.ds(pl.multiple_of(j * height + pick * share, 8), share)]
                ref[i, (j - first) * share : (j - first + 1) * share] = block.astype(ref.dtype)
            if extra_ref is not None:
                ref[i, share:] = extra_ref[pick].astype(ref.dtype)


def plane_product(cols, x_y, x_core, rows, picks, split=None, extra=None):
    _, kinds, tokens, width_cols = cols.shape
    share, width = width_cols // LINE, rows[0][0].shape[1]
    out_kinds = [tuple(range(kinds)), *((j,) for j in range(kinds))]
    more = 0 if extra is None else extra.shape[1]
    operands = [cols, x_y, x_core, *[r for chunk in rows for r in chunk]]
    if extra is not None:
        operands.append(extra)
    whole = lambda v: pl.BlockSpec(v.shape, lambda i, picks, n=v.ndim: (0,) * n)
    shapes = [
        jax.ShapeDtypeStruct((2, len(k) * share + more, width), f32 if i == 0 else bf16)
        for i, k in enumerate(out_kinds)
    ]
    kernel = lambda *refs: plane_kernel(len(rows), split, out_kinds, *refs)
    return pl.pallas_call(
        kernel,
        grid_spec=pltpu.PrefetchScalarGridSpec(
            num_scalar_prefetch=1,
            grid=(1,),
            in_specs=[whole(v) for v in operands],
            out_specs=[whole(v) for v in shapes],
            scratch_shapes=[pltpu.VMEM((kinds * LINE * share, width), f32)],
        ),
        out_shape=shapes,
        compiler_params=pltpu.CompilerParams(
            dimension_semantics=("arbitrary",), vmem_limit_bytes=20 * 1024 * 1024
        ),
        cost_estimate=pl.CostEstimate(
            flops=8 * tokens * kinds * width_cols * width * len(rows),
            bytes_accessed=8 * tokens * (kinds * width_cols + width) + 4 * kinds * width_cols * width,
            transcendentals=0,
        ),
    )(jnp.stack([jnp.asarray(p, jnp.int32) for p in picks]), *operands)


LINE = 4


def pair_middle(own, received, z2):
    total = own + received.astype(f32)
    return at(total, z2), at(total, 1 - z2).astype(bf16)


tie = lax.optimization_barrier


def middle_rounds(u, x, weights, tables, me):
    y, core = (me >> 1) & 1, me & 1
    state = forward_attention(u, weights, tables)
    n, m = state[2], state[10]
    gate, up, act, out = ffn_forward(m, state[8], weights[2])
    m_y, n_y = flip(m, Y_BIT), flip(n, Y_BIT)
    gate, up, act, out, m_y, n_y = tie((gate, up, act, out, m_y, n_y))
    state = (*state, gate, up, act)
    act = act[:, None]
    act_y = cols_y(act, y)
    m_all = (m, m_y, flip(m, CORE_BIT), flip(m_y, CORE_BIT))
    n_all = (n, n_y, flip(n, CORE_BIT), flip(n_y, CORE_BIT))
    _, _, dm = backward_ffn(x, state, weights)
    dm, act_y, m_all, n_all = tie((dm, act_y, m_all, n_all))
    act_c = (act, act_y, cols_core(act, act_y, y, core))
    dh1, _, do, _ = backward_mid(x, dm, state, weights)
    dproj = backward_attention(do, state, tables)
    first_grad, _ = backward_in(dproj, dh1, state, weights)
    first_grad, act_c = tie((first_grad.astype(bf16), act_c))
    return out, state, first_grad, (m_all, n_all, act_c)


def last_round(e, state, early, weights, tables, me):
    o = state[7]
    z, y, core = me // 4, (me >> 1) & 1, me & 1
    z2, z1 = z >> 1, z & 1
    m_all, n_all, act_c = early
    tokens, width = o.shape[0], e.shape[1]
    share = act_c[0].shape[3] // LINE
    here = (2 * y + core, core)
    eb = e.astype(bf16)
    eb_y, eb_c = flip(eb, Y_BIT), flip(eb, CORE_BIT)
    both, _, dm = backward_ffn(eb, state, weights)
    both, dm, eb_y, eb_c = tie((both, dm, eb_y, eb_c))
    both_y = cols_y(both, y)
    eb_yc = flip(eb_y, CORE_BIT)
    dm, eb_yc = tie((dm, eb_yc))
    pairs = (z1, 2 + z1, 1 - z1, 3 - z1)
    down_own, down_send = plane_product(*act_c, [(eb, eb_y, eb_c, eb_yc)], (*here, 0, *pairs))
    dm, down_own, down_send = tie((dm, down_own, down_send))
    down_received = flip(down_send, Z1_BIT)
    dh1, dz, do, gain_two_grad = backward_mid(e, dm, state, weights)
    do, dz, both_y, down_own, down_received = tie((do, dz, both_y, down_own, down_received))
    both_c = cols_core(both, both_y, y, core)
    down, down_send = pair_middle(down_own, down_received, z2)
    down_received = flip(down_send, Z2_BIT)
    both_own, gate_send, up_send = plane_product(
        both, both_y, both_c, [m_all], (*here, 0, *pairs, *pairs[2:])
    )
    do, dz, both_own, gate_send, up_send = tie((do, dz, both_own, gate_send, up_send))
    gate_received, up_received = flip(gate_send, Z1_BIT), flip(up_send, Z1_BIT)
    dproj = backward_attention(do, state, tables)
    dproj, down_received = tie((dproj, down_received))
    attn_cols = jnp.concatenate([dproj, o], axis=1).reshape(tokens, 4, 4, share)
    attn_cols = attn_cols.transpose(2, 0, 1, 3).reshape(4, 1, tokens, 4 * share)
    attn_y = cols_y(attn_cols, y)
    dz_y, dz_c = flip(dz, Y_BIT), flip(dz, CORE_BIT)
    du, gain_one_grad = backward_in(dproj, dh1, state, weights)
    gain_grad = jnp.concatenate([gain_one_grad, gain_two_grad])
    gain_grad, attn_y, dz_y, dz_c, both_own, gate_received = tie(
        (gain_grad, attn_y, dz_y, dz_c, both_own, gate_received)
    )
    gate, gate_send = pair_middle(both_own[:, :share], gate_received, z2)
    gate_received = flip(gate_send, Z2_BIT)
    gain_grad = gain_grad + flip(gain_grad, CORE_BIT)
    gain_grad = gain_grad + flip(gain_grad, Y_BIT)
    dz_all = (dz, dz_y, dz_c, flip(dz_y, CORE_BIT))
    attn_c = cols_core(attn_cols, attn_y, y, core)
    gain_rows = at(gain_grad.reshape(4, 4, -1).transpose(1, 0, 2), y * 2 + core)[:, None]
    gain_share = gain_rows.shape[-1]
    gain_rows = jnp.pad(gain_rows, ((0, 0), (0, EXTRA_ROWS - 1), (0, width - gain_share)))
    qkv_owners = QKV_COLS // share
    is_qkv = (qkv_owners // 4 * 4 + y * 2 + core < qkv_owners).astype(jnp.int32)
    attn_own, attn_send = plane_product(
        attn_cols,
        attn_y,
        attn_c,
        [n_all, dz_all],
        (*here, is_qkv, *pairs),
        (qkv_owners // 4, -(-qkv_owners // 4)),
        gain_rows,
    )
    attn_own, attn_send, both_own, up_received, gate_received = tie(
        (attn_own, attn_send, both_own, up_received, gate_received)
    )
    up, up_send = pair_middle(both_own[:, share:], up_received, z2)
    up_received = flip(up_send, Z2_BIT)
    attn_received = flip(attn_send, Z1_BIT)
    attn_own, attn_received, up_received = tie((attn_own, attn_received, up_received))
    attn, attn_send = pair_middle(attn_own, attn_received, z2)
    attn_received = flip(attn_send, Z2_BIT)
    down = down + down_received.astype(f32)
    gate = gate + gate_received.astype(f32)
    up = up + up_received.astype(f32)
    attn = attn + attn_received.astype(f32)
    return (
        du,
        attn[:share],
        jnp.stack([gate, up, down]),
        attn[share : share + 1, :gain_share],
    )


def local(edge_data, segment_ids, attn_weight, ffn_weight, gains):
    micro = segment_ids.shape[0]
    leading = lax.axis_index("section") == 0
    tables = block_tables(segment_ids)
    block, width = edge_data.shape[2], edge_data.shape[3]
    x = edge_data[0].reshape(micro * block, width)
    planes = lax.axis_size("dp") == 16
    me = lax.axis_index("dp")
    attn_own = attn_weight[0].T
    ffn_own = ffn_weight[0].swapaxes(1, 2)
    share = attn_own.shape[0]
    if planes:
        own = jnp.concatenate([attn_own[None], ffn_own], axis=0).reshape(-1, width)
        everything = lax.all_gather(own, "dp", axis=0, tiled=True).reshape(4, 4, 4, share, width)
        attn_t = everything[:, :, 0].reshape(-1, width)
        ffn_t = everything
    else:
        attn_t = lax.all_gather(attn_own, "dp", axis=0, tiled=True)
        ffn_t = lax.all_gather(ffn_own, "dp", axis=1, tiled=True)
    gain_row = gather_small(gains[0]).astype(f32)
    weights = (
        attn_t[:QKV_COLS],
        attn_t[QKV_COLS:],
        ffn_t,
        gain_row[:width],
        gain_row[width:],
    )
    first, _ = forward(x, weights, tables)
    received = lax.ppermute(first.astype(bf16), "section", [(0, 1)])
    u = jnp.where(leading, x, received)
    if planes:
        out, state, first_grad, early = middle_rounds(u, x, weights, tables, me)
        received = lax.ppermute(first_grad, "section", [(1, 0)])
        e = jnp.where(leading, received, x)
        du, attn_rows, ffn_rows, gain_shard = last_round(e, state, early, weights, tables, me)
    else:
        out, state = forward(u, weights, tables)
        first_grad, _, _ = backward(x, state, weights, tables)
        received = lax.ppermute(first_grad.astype(bf16), "section", [(1, 0)])
        e = jnp.where(leading, received, x)
        du, pieces, gain_grad = backward(e, state, weights, tables)
        attn_rows, ffn_rows = grads_generic(pieces)
        gain_shard = scatter_small(gain_grad)[None]
    edge_out = jnp.where(leading, du, out).astype(bf16).reshape(micro, block, width)
    return (
        edge_out[None],
        attn_rows.T[None],
        ffn_rows.swapaxes(1, 2)[None],
        gain_shard,
    )


def solution(mesh):
    in_specs = (
        P("section", None, "dp", None),
        P(None, "dp"),
        P("section", None, "dp"),
        P("section", None, None, "dp"),
        P("section", "dp"),
    )
    out_specs = (
        P("section", None, "dp", None),
        P("section", None, "dp"),
        P("section", None, None, "dp"),
        P("section", "dp"),
    )
    return jax.shard_map(local, mesh=mesh, in_specs=in_specs, out_specs=out_specs, check_vma=False)
```
